32 devices in a mesh: dp: 4 (over z), row: 4 (over y, x), col: 2 (over core).
Axes of the slice: x: 2, y: 2, z: 4, core: 2. Of those that a mesh axis runs over, the one named last changes fastest.
Arguments:
- tokens: bfloat16 [8, 2048, 768], P(('dp', 'col'), 'row'), may hold values from -6 to 6
- cotangent: bfloat16 [8, 2048, 768], P(('dp', 'col'), 'row'), may hold values from -6 to 6
- timesteps: int32 [8], P(('dp', 'col')), may hold values from 0 to 999
- prefix_len: int32 [8], P(('dp', 'col')), may hold values from 204 to 1024, as said below
- time_table: bfloat16 [1000, 768], P('col'), may hold values from -3 to 3
- ln1_gain: float32 [768], replicated, may hold values from 0.25 to 1.75
- ln1_bias: float32 [768], replicated, may hold values from -3 to 3
- w_qkv: bfloat16 [768, 3, 768], P('col', None, 'row'), may hold values from -0.3125 to 0.3125
- w_out: bfloat16 [768, 768], P('col', 'row'), may hold values from -1.75 to 1.75
- out_bias: float32 [768], replicated, may hold values from -3 to 3
- ln2_gain: float32 [768], replicated, may hold values from 0.25 to 1.75
- ln2_bias: float32 [768], replicated, may hold values from -3 to 3
- w_up: bfloat16 [768, 3072], P('col', 'row'), may hold values from -0.21875 to 0.21875
- up_bias: float32 [3072], P('row'), may hold values from -3 to 3
- w_down: bfloat16 [768, 3072], P('col', 'row'), may hold values from -0.109375 to 0.109375
- down_bias: float32 [768], replicated, may hold values from -4 to 4
Outputs:
- layer_out: bfloat16 [8, 2048, 768], P(('dp', 'col'), 'row')
- tokens_grad: float32 [8, 2048, 768], P(('dp', 'col'), 'row')
- table_grad: float32 [1000, 768], P('col')
- ln1_gain_grad: float32 [768], replicated
- ln1_bias_grad: float32 [768], replicated
- qkv_grad: float32 [768, 3, 768], P('col', None, 'row')
- out_grad: float32 [768, 768], P('col', 'row')
- out_bias_grad: float32 [768], replicated
- ln2_gain_grad: float32 [768], replicated
- ln2_bias_grad: float32 [768], replicated
- up_grad: float32 [768, 3072], P('col', 'row')
- up_bias_grad: float32 [3072], P('row')
- down_grad: float32 [768, 3072], P('col', 'row')
- down_bias_grad: float32 [768], replicated
The draws below stay inside these ranges and needn't reach their ends.
Inputs may be any that keep to these rules, and one draw needn't show every extreme that they name: `prefix_len`: each sequence's prefix length lies between 204 and 1024, and some sequence takes each end.
All inputs are finite; a program needn't handle non-finite values.
Results may differ from the reference program's by a relative error of at most 0.02.
Values may be sent and summed in bfloat16 or wider, within the bound.
A program may use at most 128 MiB of HBM per device.

```python
import jax
import jax.numpy as jnp
from jax import lax

D = 768
HEADS = 12
HD = 64
FF = 3072
NT = 1000
LEN = 2048
SEQS = 8


def draw_prefix_len(key, part):
    low_end = LEN // 10
    high_end = LEN // 2
    key_values, key_high, key_low = jax.random.split(key, 3)
    values = jax.random.randint(key_values, (SEQS,), low_end, high_end + 1, dtype=jnp.int32)
    where_high = jax.random.randint(key_high, (), 0, SEQS, dtype=jnp.int32)
    where_low = (where_high + 1 + jax.random.randint(key_low, (), 0, SEQS - 1, dtype=jnp.int32)) % SEQS
    values = values.at[where_high].set(high_end)
    values = values.at[where_low].set(low_end)
    return values


def set_ends(entries, own_key, low, largest):
    dims = entries.shape
    spot = [jax.random.randint(jax.random.fold_in(own_key, axis), (), 0, dims[axis]) for axis in range(len(dims))]
    entries = entries.at[tuple(spot)].set(low)
    longest = dims.index(max(dims))
    spot[longest] = (spot[longest] + 1) % dims[longest]
    return entries.at[tuple(spot)].set(largest)


def level_of(stream_key, extent, pieces, least, high):
    factor_of = 1.0
    for position, shards_of in pieces:
        heights = jax.random.uniform(jax.random.fold_in(jax.random.fold_in(stream_key, 6), position), (shards_of,), jnp.float32, least / len(pieces), high / len(pieces))
        factor_of = factor_of * jnp.repeat(jnp.exp(heights), extent[position] // shards_of).reshape((-1,) + (1,) * (len(extent) - 1 - position))
    return factor_of


def gaussian(stream_key, shape, deviation, bound, shards=(), kind=jnp.bfloat16):
    factor_of = level_of(stream_key, shape, shards, -0.22, 0.18) if shards else 1.0
    values = jax.random.normal(stream_key, shape, jnp.float32) * deviation * factor_of
    return jnp.minimum(jnp.maximum(values, -bound), bound).astype(kind)


def setup_inputs(seed: int = 0) -> dict:
    key_of = jax.random.split(jax.random.key(seed), 17)
    return {
        "tokens": gaussian(key_of[0], (SEQS, LEN, D), 1.0, 6.0, ((0, 8), (1, 4))),
        "cotangent": gaussian(key_of[1], (SEQS, LEN, D), 1.0, 6.0, ((0, 8), (1, 4))),
        "timesteps": set_ends(jax.random.randint(key_of[2], (SEQS,), 0, NT), jax.random.fold_in(key_of[2], 1), 0, NT - 1).astype(jnp.int32),
        "prefix_len": draw_prefix_len(jax.random.fold_in(key_of[16], 71), 0),
        "time_table": gaussian(key_of[4], (NT, D), 0.5, 3.0, ((0, 2),)),
        "ln1_gain": jnp.clip(1.0 + 0.15 * jax.random.normal(key_of[5], (D,), jnp.float32), 0.25, 1.75),
        "ln1_bias": gaussian(key_of[6], (D,), 0.3, 3.0, (), jnp.float32),
        "w_qkv": gaussian(key_of[7], (D, 3, D), (D // 2) ** -0.5, 0.3125, ((0, 2), (2, 4))),
        "w_out": gaussian(key_of[8], (D, D), (max(D // 64, 1)) ** -0.5, 1.75, ((0, 2), (1, 4))),
        "out_bias": gaussian(key_of[9], (D,), 0.3, 3.0, (), jnp.float32),
        "ln2_gain": jnp.clip(1.0 + 0.15 * jax.random.normal(key_of[10], (D,), jnp.float32), 0.25, 1.75),
        "ln2_bias": gaussian(key_of[11], (D,), 0.3, 3.0, (), jnp.float32),
        "w_up": gaussian(key_of[12], (D, FF), D ** -0.5, 0.21875, ((0, 2), (1, 4))),
        "up_bias": gaussian(key_of[13], (FF,), 0.3, 3.0, ((0, 4),), jnp.float32),
        "w_down": gaussian(key_of[14], (D, FF), FF ** -0.5, 0.109375, ((0, 2), (1, 4))),
        "down_bias": gaussian(key_of[15], (D,), 1.0, 4.0, (), jnp.float32),
    }


@jax.custom_vjp
def low(v):
    return lax.optimization_barrier(v.astype(jnp.bfloat16)).astype(jnp.float32)

@jax.custom_vjp
def low_back(v):
    return v

def low_keep(v):
    return (low(v), None)

def low_pass(kept, grad):
    return (grad,)

def back_keep(v):
    return (v, None)

def back_low(kept, grad):
    return (low(grad),)
low.defvjp(low_keep, low_pass)
low_back.defvjp(back_keep, back_low)
norm_eps = 1e-05
masked_score = -1e+30

def layer_norm(hidden, gain_vec, bias_vec):
    average = lax.optimization_barrier(jnp.mean(hidden, axis=-1, keepdims=True))
    variance = lax.optimization_barrier(jnp.mean(hidden * hidden, axis=-1, keepdims=True)) - average * average
    return (hidden - average) * lax.rsqrt(variance + norm_eps) * gain_vec + bias_vec

def reference(tokens, cotangent, timesteps, prefix_len, time_table, ln1_gain, ln1_bias, w_qkv, w_out, out_bias, ln2_gain, ln2_bias, w_up, up_bias, w_down, down_bias):
    highest = lax.Precision.HIGHEST
    key_pos = jnp.arange(LEN, dtype=jnp.int32)
    score_scale = HD ** (-0.5)

    def forward(tokens_f, table_f, gain_one, bias_one, qkv_f, out_f, out_bias_f, gain_two, bias_two, up_f, up_bias_f, down_f, down_bias_f):
        embeds = table_f[timesteps]

        def one_sequence(carry_zero, seq_item):
            seq_tokens, seq_embed, prefix = seq_item
            embedded = seq_tokens + seq_embed[None, :]
            normed1 = low(layer_norm(embedded, gain_one, bias_one))
            project = low(low_back(jnp.einsum('td,dkh->tkh', normed1, qkv_f, precision=highest)))
            heads_view = project.reshape(LEN, 3, HEADS, HD)
            raw_scores = jnp.einsum('qhd,khd->hqk', heads_view[:, 0], heads_view[:, 1], precision=highest) * score_scale
            scores = low_back(raw_scores)
            allowed = (key_pos[None, :] <= key_pos[:, None]) | (key_pos[None, :] < prefix)
            scores = jnp.where(allowed[None], scores, masked_score)
            row_max = lax.optimization_barrier(jnp.max(scores, axis=2, keepdims=True))
            exponent = jnp.exp(scores - row_max)
            soft_probs = exponent / lax.optimization_barrier(jnp.sum(exponent, axis=2, keepdims=True))
            attended = jnp.einsum('hqk,khd->qhd', low(soft_probs), heads_view[:, 2], precision=highest).reshape(LEN, D)
            attended = low(low_back(attended))
            hidden = embedded + low_back(jnp.einsum('th,dh->td', attended, out_f, precision=highest)) + out_bias_f
            normed2 = low(layer_norm(hidden, gain_two, bias_two))
            inner = low_back(jnp.einsum('td,df->tf', normed2, up_f, precision=highest)) + up_bias_f
            active = low(jax.nn.gelu(inner, approximate=False))
            result = hidden + jnp.einsum('tf,df->td', active, down_f, precision=highest) + down_bias_f
            return (carry_zero, result)
        unused, results = lax.scan(jax.checkpoint(one_sequence), jnp.zeros((), jnp.float32), (tokens_f, embeds, prefix_len))
        return results
    floats = tuple((item.astype(jnp.float32) for item in (tokens, time_table, ln1_gain, ln1_bias, w_qkv, w_out, out_bias, ln2_gain, ln2_bias, w_up, up_bias, w_down, down_bias)))
    result, backward = jax.vjp(forward, *floats)
    grads = backward(cotangent.astype(jnp.float32))
    return (result.astype(jnp.bfloat16), grads[0], grads[1], grads[2], grads[3], grads[4], grads[5], grads[6], grads[7], grads[8], grads[9], grads[10], grads[11], grads[12])
```

```python
import jax
import jax.numpy as jnp
from jax import lax
from jax.sharding import PartitionSpec as P

HD = 64


norm_eps = 1e-05
masked_score = -1e30


def gelu_exact(values):
    return jax.nn.gelu(values, approximate=False)


def gather_rows(values):
    return lax.all_gather(values, "row", axis=1, tiled=True)


def scatter_rows(values):
    return lax.psum_scatter(
        values.astype(jnp.bfloat16), "row", scatter_dimension=1, tiled=True
    ).astype(jnp.float32)


def gather_grads(values):
    return lax.all_gather(values, "row", axis=1, tiled=True)


def scatter_grads(values):
    return lax.psum_scatter(
        values.astype(jnp.bfloat16), "row", scatter_dimension=1, tiled=True
    ).astype(jnp.float32)


def norm_forward(hidden, gain_vec, bias_vec):
    width = hidden.shape[-1]
    average = jnp.sum(hidden, axis=-1, keepdims=True) / width
    variance = jnp.sum(hidden * hidden, axis=-1, keepdims=True) / width - average * average
    inverse = lax.rsqrt(variance + norm_eps)
    centred = (hidden - average) * inverse
    return (centred * gain_vec + bias_vec, centred, inverse)


def norm_backward(grad_out, centred, inverse, gain_vec):
    width = grad_out.shape[-1]
    scaled = grad_out * gain_vec
    first_mean = jnp.sum(scaled, axis=-1, keepdims=True) / width
    second_mean = jnp.sum(scaled * centred, axis=-1, keepdims=True) / width
    grad_in = inverse * (scaled - first_mean - centred * second_mean)
    return (grad_in, jnp.sum(grad_out * centred, axis=(0, 1)), jnp.sum(grad_out, axis=(0, 1)))


def attend_forward(queries, key_rows, values, prefix):
    length = queries.shape[0]
    block_rows = min(512, length)
    score_scale = queries.shape[2] ** (-0.5)
    key_pos = jnp.arange(length, dtype=jnp.int32)

    def one_block(block_index):
        row_start = block_index * block_rows
        query_blk = lax.dynamic_slice_in_dim(queries, row_start, block_rows, 0)
        scores = (
            jnp.einsum("qhd,khd->hqk", query_blk, key_rows, preferred_element_type=jnp.float32)
            * score_scale
        )
        query_pos = row_start + jnp.arange(block_rows, dtype=jnp.int32)
        allowed = (key_pos[None, :] <= query_pos[:, None]) | (key_pos[None, :] < prefix)
        scores = jnp.where(allowed[None], scores, masked_score)
        row_max = jnp.max(scores, axis=2, keepdims=True)
        exponent = jnp.exp(scores - row_max)
        row_total = jnp.sum(exponent, axis=2, keepdims=True)
        soft_low = (exponent / row_total).astype(jnp.bfloat16)
        mixed_blk = jnp.einsum("hqk,khd->qhd", soft_low, values, preferred_element_type=jnp.float32)
        return (mixed_blk, (row_max + jnp.log(row_total))[:, :, 0])

    mixed, logsums = lax.map(one_block, jnp.arange(length // block_rows, dtype=jnp.int32))
    return (mixed.reshape(queries.shape), logsums)


def attend_backward(queries, key_rows, values, mixed, logsums, grad_mixed, prefix):
    length = queries.shape[0]
    block_rows = min(512, length)
    score_scale = queries.shape[2] ** (-0.5)
    key_pos = jnp.arange(length, dtype=jnp.int32)
    delta = jnp.sum(grad_mixed.astype(jnp.float32) * mixed, axis=2)

    def one_block(grads_carry, block_index):
        grad_keys, grad_values = grads_carry
        row_start = block_index * block_rows
        query_blk = lax.dynamic_slice_in_dim(queries, row_start, block_rows, 0)
        grad_blk = lax.dynamic_slice_in_dim(grad_mixed, row_start, block_rows, 0)
        delta_blk = lax.dynamic_slice_in_dim(delta, row_start, block_rows, 0)
        scores = (
            jnp.einsum("qhd,khd->hqk", query_blk, key_rows, preferred_element_type=jnp.float32)
            * score_scale
        )
        query_pos = row_start + jnp.arange(block_rows, dtype=jnp.int32)
        allowed = (key_pos[None, :] <= query_pos[:, None]) | (key_pos[None, :] < prefix)
        scores = jnp.where(allowed[None], scores, masked_score)
        weights_soft = jnp.exp(scores - logsums[block_index][:, :, None])
        grad_soft = jnp.einsum("qhd,khd->hqk", grad_blk, values, preferred_element_type=jnp.float32)
        grad_scores = (weights_soft * (grad_soft - delta_blk.T[:, :, None])).astype(jnp.bfloat16)
        grad_query = (
            jnp.einsum("hqk,khd->qhd", grad_scores, key_rows, preferred_element_type=jnp.float32)
            * score_scale
        )
        grad_keys = (
            grad_keys
            + jnp.einsum("hqk,qhd->khd", grad_scores, query_blk, preferred_element_type=jnp.float32)
            * score_scale
        )
        grad_values = grad_values + jnp.einsum(
            "hqk,qhd->khd",
            weights_soft.astype(jnp.bfloat16),
            grad_blk,
            preferred_element_type=jnp.float32,
        )
        return ((grad_keys, grad_values), grad_query)

    zero_grads = jnp.zeros(key_rows.shape, jnp.float32)
    final_grads, grad_queries = lax.scan(
        one_block, (zero_grads, zero_grads), jnp.arange(length // block_rows, dtype=jnp.int32)
    )
    return jnp.stack([grad_queries.reshape(key_rows.shape), final_grads[0], final_grads[1]], axis=1)


def body(
    tokens,
    cotangent,
    timesteps,
    prefix_len,
    time_table,
    ln1_gain,
    ln1_bias,
    w_qkv,
    w_out,
    out_bias,
    ln2_gain,
    ln2_bias,
    w_up,
    up_bias,
    w_down,
    down_bias,
):
    highest = lax.Precision.HIGHEST
    qkv_full, out_full, up_full, down_full, table_full = (
        lax.all_gather(w_qkv, "col", axis=0, tiled=True),
        lax.all_gather(w_out, "col", axis=0, tiled=True),
        lax.all_gather(w_up, "col", axis=0, tiled=True),
        lax.all_gather(w_down, "col", axis=0, tiled=True),
        lax.all_gather(time_table, "col", axis=0, tiled=True),
    )
    seq_count = tokens.shape[0]
    width_heads = qkv_full.shape[2]
    heads_local = width_heads // HD
    picked = (
        timesteps[:, None] == jnp.arange(table_full.shape[0], dtype=jnp.int32)[None, :]
    ).astype(jnp.float32)
    embed_rows = jnp.dot(picked, table_full.astype(jnp.float32), precision=highest)

    def sequence_forward(seq_item):
        parts_seq, prefix = seq_item
        return attend_forward(parts_seq[:, 0], parts_seq[:, 1], parts_seq[:, 2], prefix)

    def forward_pass(tokens_in):
        hidden0 = tokens_in.astype(jnp.float32) + embed_rows[:, None, :]
        normed1, centred1, inverse1 = norm_forward(hidden0, ln1_gain, ln1_bias)
        full_one = gather_rows(normed1.astype(jnp.bfloat16))
        length = full_one.shape[1]
        project = jnp.einsum(
            "std,dkh->stkh", full_one, qkv_full, preferred_element_type=jnp.float32
        ).astype(jnp.bfloat16)
        parts = project.reshape(seq_count, length, 3, heads_local, HD)
        mixed, logsums = lax.map(sequence_forward, (parts, prefix_len))
        weighted = mixed.reshape(seq_count, length, width_heads).astype(jnp.bfloat16)
        branch = scatter_rows(
            jnp.einsum("sth,dh->std", weighted, out_full, preferred_element_type=jnp.float32)
        )
        hidden1 = hidden0 + (branch + out_bias)
        normed2, centred2, inverse2 = norm_forward(hidden1, ln2_gain, ln2_bias)
        full_two = gather_rows(normed2.astype(jnp.bfloat16))
        inner = (
            jnp.einsum("std,df->stf", full_two, up_full, preferred_element_type=jnp.float32)
            + up_bias
        )
        active = gelu_exact(inner).astype(jnp.bfloat16)
        result = hidden1 + (
            scatter_rows(
                jnp.einsum("stf,df->std", active, down_full, preferred_element_type=jnp.float32)
            )
            + down_bias
        )
        saved = (
            full_one,
            centred1,
            inverse1,
            parts,
            mixed,
            logsums,
            weighted,
            centred2,
            inverse2,
            full_two,
            inner,
            active,
        )
        return (result, saved)

    result, saved = forward_pass(tokens)
    (
        full_one,
        centred1,
        inverse1,
        parts,
        mixed,
        logsums,
        weighted,
        centred2,
        inverse2,
        full_two,
        inner,
        active,
    ) = saved
    length = full_one.shape[1]
    grad_full = gather_grads(cotangent)
    down_grad_full = jnp.einsum(
        "std,stf->df", grad_full, active, preferred_element_type=jnp.float32
    )
    grad_active = jnp.einsum(
        "std,df->stf", grad_full, down_full, preferred_element_type=jnp.float32
    )
    unused_out, gelu_back = jax.vjp(gelu_exact, inner)
    grad_inner = gelu_back(grad_active)[0]
    inner_low = grad_inner.astype(jnp.bfloat16)
    up_grad_full = jnp.einsum(
        "std,stf->df", full_two, inner_low, preferred_element_type=jnp.float32
    )
    grad_normed2 = scatter_grads(
        jnp.einsum("stf,df->std", inner_low, up_full, preferred_element_type=jnp.float32)
    )
    grad_norm_two, ln2_gain_part, ln2_bias_part = norm_backward(
        grad_normed2, centred2, inverse2, ln2_gain
    )
    grad_hidden1 = cotangent.astype(jnp.float32) + grad_norm_two
    grad_branch_full = gather_grads(grad_hidden1.astype(jnp.bfloat16))
    out_grad_full = jnp.einsum(
        "std,sth->dh", grad_branch_full, weighted, preferred_element_type=jnp.float32
    )
    grad_weighted = jnp.einsum(
        "std,dh->sth", grad_branch_full, out_full, preferred_element_type=jnp.float32
    ).astype(jnp.bfloat16)

    def sequence_backward(seq_item):
        parts_seq, mixed_seq, logsum_seq, grad_seq, prefix = seq_item
        return attend_backward(
            parts_seq[:, 0],
            parts_seq[:, 1],
            parts_seq[:, 2],
            mixed_seq,
            logsum_seq,
            grad_seq,
            prefix,
        )

    grad_parts = lax.map(
        sequence_backward,
        (
            parts,
            mixed,
            logsums,
            grad_weighted.reshape(seq_count, length, heads_local, HD),
            prefix_len,
        ),
    )
    grad_project = grad_parts.reshape(seq_count, length, 3, width_heads).astype(jnp.bfloat16)
    qkv_grad_full = jnp.einsum(
        "std,stkh->dkh", full_one, grad_project, preferred_element_type=jnp.float32
    )
    grad_normed1 = scatter_grads(
        jnp.einsum("stkh,dkh->std", grad_project, qkv_full, preferred_element_type=jnp.float32)
    )
    grad_norm_one, ln1_gain_part, ln1_bias_part = norm_backward(
        grad_normed1, centred1, inverse1, ln1_gain
    )
    grad_hidden0 = grad_hidden1 + grad_norm_one
    seq_sums = jnp.sum(grad_hidden0, axis=1)
    table_grad_full = jnp.einsum("sn,sd->nd", picked, seq_sums, precision=highest)
    vectors = lax.psum(
        (
            ln1_gain_part,
            ln1_bias_part,
            jnp.sum(grad_hidden1, axis=(0, 1)),
            ln2_gain_part,
            ln2_bias_part,
            jnp.sum(cotangent.astype(jnp.float32), axis=(0, 1)),
        ),
        ("dp", "row", "col"),
    )
    up_bias_grad = lax.psum(jnp.sum(grad_inner, axis=(0, 1)), ("dp", "col"))
    weights_full = (qkv_grad_full, out_grad_full, up_grad_full, down_grad_full)
    blocks = (
        lax.psum_scatter(
            weights_full[0].astype(jnp.bfloat16), "col", scatter_dimension=0, tiled=True
        ).astype(jnp.float32),
        lax.psum_scatter(
            weights_full[1].astype(jnp.bfloat16), "col", scatter_dimension=0, tiled=True
        ).astype(jnp.float32),
        lax.psum_scatter(
            weights_full[2].astype(jnp.bfloat16), "col", scatter_dimension=0, tiled=True
        ).astype(jnp.float32),
        lax.psum_scatter(
            weights_full[3].astype(jnp.bfloat16), "col", scatter_dimension=0, tiled=True
        ).astype(jnp.float32),
        lax.psum_scatter(
            table_grad_full.astype(jnp.bfloat16), "col", scatter_dimension=0, tiled=True
        ).astype(jnp.float32),
    )
    weight_blocks = (blocks[0], blocks[1], blocks[2], blocks[3])
    weight_blocks = (
        lax.psum(blocks[0].astype(jnp.bfloat16), "dp").astype(jnp.float32),
        lax.psum(blocks[1].astype(jnp.bfloat16), "dp").astype(jnp.float32),
        lax.psum(blocks[2].astype(jnp.bfloat16), "dp").astype(jnp.float32),
        lax.psum(blocks[3].astype(jnp.bfloat16), "dp").astype(jnp.float32),
    )
    table_block = lax.psum(blocks[4].astype(jnp.bfloat16), ("dp", "row")).astype(jnp.float32)
    return (
        result.astype(jnp.bfloat16),
        grad_hidden0,
        table_block,
        vectors[0],
        vectors[1],
        weight_blocks[0],
        weight_blocks[1],
        vectors[2],
        vectors[3],
        vectors[4],
        weight_blocks[2],
        up_bias_grad,
        weight_blocks[3],
        vectors[5],
    )


def solution(mesh):
    placed = (
        P(("dp", "col"), "row", None),
        P(("dp", "col"), "row", None),
        P(("dp", "col")),
        P(("dp", "col")),
        P("col", None),
        P(),
        P(),
        P("col", None, "row"),
        P("col", "row"),
        P(),
        P(),
        P(),
        P("col", "row"),
        P("row"),
        P("col", "row"),
        P(),
    )
    return jax.shard_map(
        body,
        mesh=mesh,
        in_specs=placed,
        out_specs=(
            P(("dp", "col"), "row", None),
            P(("dp", "col"), "row", None),
            P("col", None),
            P(),
            P(),
            P("col", None, "row"),
            P("col", "row"),
            P(),
            P(),
            P(),
            P("col", "row"),
            P("row"),
            P("col", "row"),
            P(),
        ),
        check_vma=False,
    )
```

```python
import functools

import jax
import jax.numpy as jnp
from jax import lax
from jax.experimental import pallas as pl
from jax.experimental.pallas import tpu as pltpu
from jax.sharding import PartitionSpec as P

HD = 64
LANES = 128
norm_eps = 1e-05
masked_score = -1e30
f32, bf16 = jnp.float32, jnp.bfloat16
MESH = pl.DeviceIdType.MESH
NN = (((1,), (0,)), ((), ()))
NT = (((1,), (1,)), ((), ()))
TN = (((0,), (0,)), ((), ()))
VM = pl.BlockSpec(memory_space=pltpu.VMEM)
SM = pl.BlockSpec(memory_space=pltpu.SMEM)
AN = pl.BlockSpec(memory_space=pl.ANY)


def mm(a, b, dims):
    return lax.dot_general(a, b, dims, preferred_element_type=f32)


def remote(src, dst, send, recv, **where):
    return pltpu.make_async_remote_copy(
        src_ref=src, dst_ref=dst, send_sem=send, recv_sem=recv, device_id=where, device_id_type=MESH
    )


def shifted(name, step, count):
    return lax.rem(lax.axis_index(name) + (step + count), count)


def greet(sizes):
    barrier = pltpu.get_barrier_semaphore()
    total = 0
    for name, count in sizes.items():
        for step in range(1, count):
            pl.semaphore_signal(
                barrier, inc=1, device_id={name: shifted(name, step, count)}, device_id_type=MESH
            )
            total += 1
    pl.semaphore_wait(barrier, total)


def other_half(z):
    return z + 1 - 2 * lax.rem(z, 2)


def normalize(hidden, width):
    average = jnp.sum(hidden, axis=-1, keepdims=True) / width
    variance = jnp.sum(hidden * hidden, axis=-1, keepdims=True) / width - average * average
    inverse = lax.rsqrt(variance + norm_eps)
    return (hidden - average) * inverse, inverse


def split_parts(value, lane, count):
    out = jnp.zeros(lane.shape, f32)
    for place in range(count):
        high = value.astype(bf16).astype(f32)
        out = jnp.where(lane == place, high, out)
        value = value - high
    return out.astype(bf16)


def forward_kernel(
    R, C, Z,
    stamp, prefix_ref, x, table, gain, bias, w, wud, wo, ub,
    q, k, v, one, wq, emb, att, mine, wud_all, wo_all, ub_all,
    tab, tabf, o,
    tab_s, tab_r, w_s, w_r, n_s, n_r, a_s, a_r, g_s, g_r, gz_s, gz_r, gc_s, gc_r, wo_s, wo_r, woc_s, woc_r, ub_s, ub_r, loc,
):
    r, c, z = lax.axis_index("row"), lax.axis_index("col"), lax.axis_index("dp")
    T, D = x.shape
    DC = w.shape[0]
    H = w.shape[1] // 3
    heads = H // HD
    L = R * T
    NTB = table.shape[0]
    half = T // 2
    cols = pl.ds(pl.multiple_of(c * DC, DC), DC)
    pair = Z % 2 == 0
    parity = lax.rem(z, 2)

    barrier = pltpu.get_barrier_semaphore()
    total = 0
    for name, count in (("row", R), ("col", C)):
        for step in range(1, count):
            pl.semaphore_signal(barrier, inc=1, device_id={name: shifted(name, step, count)}, device_id_type=MESH)
            total += 1
    if pair:
        pl.semaphore_signal(barrier, inc=1, device_id={"dp": other_half(z)}, device_id_type=MESH)
        total += 1
    pl.semaphore_wait(barrier, total)

    def tab_copy(s):
        return remote(table, tab.at[c], tab_s.at[s - 1], tab_r.at[s - 1], col=shifted("col", s, C))

    def w_copy(s):
        return remote(w, wq.at[cols], w_s.at[s - 1], w_r.at[s - 1], col=shifted("col", s, C))

    def n_copy(s, part):
        piece = one.at[r, pl.ds(part * half, half)]
        return remote(piece, piece, n_s.at[part, s - 1], n_r.at[part, s - 1], row=lax.rem(r + s, R))

    for s in range(1, C):
        tab_copy(s).start()
    for s in range(1, C):
        w_copy(s).start()
    wq[cols, :] = w[...]

    when = stamp[0]

    def pick(block):
        place = when - block * NTB
        inside = (place >= 0) & (place < NTB)
        row = tabf[pl.ds(jnp.clip(place, 0, NTB - 1), 1), :]
        return jnp.where(inside, row, jnp.zeros_like(row))

    tabf[...] = table[...].astype(f32)
    chosen = pick(c)
    for s in range(1, C):
        tab_copy(s).wait_recv()
        block = lax.rem(c - s + C, C)
        tabf[...] = tab[block].astype(f32)
        chosen = chosen + pick(block)
    emb[...] = jnp.broadcast_to(chosen, emb.shape)

    rows_ln = 128
    for part in range(2):

        def norm_step(t, carry, part=part):
            rows = pl.ds(pl.multiple_of(part * half + t * rows_ln, rows_ln), rows_ln)
            hidden = x[rows, :].astype(f32) + chosen
            centred, inverse = normalize(hidden, D)
            one[r, rows, :] = (centred * gain[...] + bias[...]).astype(bf16)
            return carry

        lax.fori_loop(0, half // rows_ln, norm_step, 0)
        for s in range(1, R):
            n_copy(s, part).start()

    which = parity if pair else 0

    def g_copy(s):
        to = lax.rem(r + s, R)
        if pair:
            return remote(wud.at[parity], wud_all.at[parity, r, cols], g_s.at[s - 1], g_r.at[s - 1], row=to)
        return remote(wud, wud_all.at[:, r, cols], g_s.at[s - 1], g_r.at[s - 1], row=to)

    def z_copy(s):
        piece = wud_all.at[parity, lax.rem(r - s + R, R), cols]
        return remote(piece, piece, gz_s.at[s - 1], gz_r.at[s - 1], dp=other_half(z))

    def gc_copy(s, kind, t):
        to = shifted("col", t, C)
        block = lax.rem(r - s + R, R)
        if s == 0:
            return remote(wud, wud_all.at[:, r, cols], gc_s.at[0, 0, t - 1], gc_r.at[0, 0, t - 1], col=to)
        if not pair:
            piece = wud_all.at[:, block, cols]
        else:
            piece = wud_all.at[parity if kind == 0 else 1 - parity, block, cols]
        return remote(piece, piece, gc_s.at[s, kind, t - 1], gc_r.at[s, kind, t - 1], col=to)

    def wo_copy(s):
        return remote(wo, wo_all.at[r, cols], wo_s.at[s - 1], wo_r.at[s - 1], row=lax.rem(r + s, R))

    def woc_copy(s, t):
        to = shifted("col", t, C)
        if s == 0:
            return remote(wo, wo_all.at[r, cols], woc_s.at[0, t - 1], woc_r.at[0, t - 1], col=to)
        piece = wo_all.at[lax.rem(r - s + R, R), cols]
        return remote(piece, piece, woc_s.at[s, t - 1], woc_r.at[s, t - 1], col=to)

    def ub_copy(s):
        return remote(ub, ub_all.at[r], ub_s.at[s - 1], ub_r.at[s - 1], row=lax.rem(r + s, R))

    own_ud = pltpu.make_async_copy(wud, wud_all.at[:, r, cols], loc.at[0])
    own_wo = pltpu.make_async_copy(wo, wo_all.at[r, cols], loc.at[1])
    own_ud.start()
    own_wo.start()
    ub_all[r] = ub[...]
    for s in range(1, R):
        ub_copy(s).start()
        g_copy(s).start()
    for s in range(1, R):
        wo_copy(s).start()
    for t in range(1, C):
        gc_copy(0, 0, t).start()
        woc_copy(0, t).start()

    for s in range(1, C):
        w_copy(s).wait_recv()
    lane = lax.broadcasted_iota(jnp.int32, (T, HD), 1)
    k_tail = jnp.where(lane < 3, 1.0, 0.0).astype(bf16)
    v_tail = jnp.where(lane < 2, 1.0, 0.0).astype(bf16)
    q_tail = jnp.zeros((T, HD), bf16)

    def project(s, carry):
        @pl.when(s > 0)
        def _():
            for part in range(2):
                piece = one.at[r, pl.ds(part * half, half)]
                remote(piece, piece, n_s.at[part, s - 1], n_r.at[part, s - 1], row=lax.rem(r + s, R)).wait_recv()

        block = lax.rem(r - s + R, R)
        y = mm(one[block], wq[...], NN).astype(bf16)
        rows = pl.ds(pl.multiple_of(block * T, T), T)
        scale = HD ** (-0.5)
        for h in range(heads):
            q[h, rows, :] = jnp.concatenate([y[:, h * HD : (h + 1) * HD] * scale, q_tail], axis=1)
            k[h, rows, :] = jnp.concatenate([y[:, H + h * HD : H + (h + 1) * HD], k_tail], axis=1)
            v[h, rows, :] = jnp.concatenate([y[:, 2 * H + h * HD : 2 * H + (h + 1) * HD], v_tail], axis=1)
        return carry

    lax.fori_loop(0, R, project, 0)

    def spread(s):
        g_copy(s).wait_recv()
        if pair:
            z_copy(s).start()
        for t in range(1, C):
            gc_copy(s, 0, t).start()
        wo_copy(s).wait_recv()
        for t in range(1, C):
            woc_copy(s, t).start()

    def spread_pair(s):
        if pair:
            z_copy(s).wait_recv()
            for t in range(1, C):
                gc_copy(s, 1, t).start()

    prefix = prefix_ref[0]
    longest = L // 2
    SB = min(256, T)
    nsub = T // SB
    lane_sb = lax.broadcasted_iota(jnp.int32, (SB, HD), 1)

    def a_copy(i, s):
        return remote(mine.at[i], att.at[r], a_s.at[s - 1], a_r.at[s - 1], row=i)

    for i in range(R):
        early = (i + 1) * T <= longest
        nk = longest if early else (i + 1) * T
        nm = nk if early else T

        def attend(t, carry, i=i, nk=nk, nm=nm):
            h = t // nsub
            sub = pl.multiple_of(lax.rem(t, nsub) * SB, SB)
            row = i * T + sub
            rows = pl.ds(pl.multiple_of(row, SB), SB)
            scores = mm(q[h, rows, :], k[h, :nk, :], NT)
            limit = jnp.maximum(row + 1 + lax.broadcasted_iota(jnp.int32, (SB, 1), 0), prefix)
            place = (nk - nm) + lax.broadcasted_iota(jnp.int32, (SB, nm), 1)
            last = jnp.where(place < limit, scores[:, nk - nm :], masked_score)
            top = jnp.max(last, axis=1, keepdims=True)
            if nk > nm:
                top = jnp.maximum(top, jnp.max(scores[:, : nk - nm], axis=1, keepdims=True))
            mixed = mm(jnp.exp(last - top).astype(bf16), v[h, nk - nm : nk, :], NN)
            if nk > nm:
                mixed += mm(jnp.exp(scores[:, : nk - nm] - top).astype(bf16), v[h, : nk - nm, :], NN)
            weight = mixed[:, HD : HD + 1]
            o[h, pl.ds(sub, SB), :] = mixed / weight
            q[h, rows, HD:] = split_parts(-(top + jnp.log(weight)), lane_sb, 3)
            return carry

        lax.fori_loop(0, heads * nsub, attend, 0)
        mine[i] = jnp.concatenate([o[h][:, :HD] for h in range(heads)], axis=1).astype(bf16)

        @pl.when(r != i)
        def _(i=i):
            a_copy(i, lax.rem(i - r + R, R)).start()

        if 1 <= i < R:
            spread(i)
    att[r] = mine[r]
    for s in range(1, R):
        spread_pair(s)

    for s in range(1, R):
        remote(mine.at[lax.rem(r + s, R)], att.at[r], a_s.at[s - 1], a_r.at[s - 1], row=lax.rem(r + s, R)).wait()
    own_ud.wait()
    own_wo.wait()
    for s in range(1, C):
        tab_copy(s).wait_send()
        w_copy(s).wait_send()
    for s in range(1, R):
        for part in range(2):
            n_copy(s, part).wait_send()
        g_copy(s).wait_send()
        wo_copy(s).wait_send()
        ub_copy(s).wait()
        if pair:
            z_copy(s).wait_send()
    for t in range(1, C):
        for s in range(R):
            gc_copy(s, 0, t).wait()
            if pair and s > 0:
                gc_copy(s, 1, t).wait()
            woc_copy(s, t).wait()


def run_forward(R, C, Z, stamp, prefix, x, table, gain, bias, w, wud, wo, ub):
    T, D = x.shape
    H = w.shape[1] // 3
    F = wud.shape[2]
    heads = H // HD
    L = R * T
    sds = jax.ShapeDtypeStruct
    dma = pltpu.SemaphoreType.DMA
    c1 = max(C - 1, 1)
    sem2 = lambda *shape: [dma(shape), dma(shape)]
    return pl.pallas_call(
        functools.partial(forward_kernel, R, C, Z),
        out_shape=(
            sds((heads, L, LANES), bf16), sds((heads, L, LANES), bf16), sds((heads, L, LANES), bf16),
            sds((R, T, D), bf16), sds((D, 3 * H), bf16), sds((8, D), f32),
            sds((R, T, H), bf16), sds((R, T, H), bf16),
            sds((2, R, D, F), bf16), sds((R, D, H), bf16), sds((R, 1, F), f32),
        ),
        in_specs=[SM, SM] + [VM] * 8,
        out_specs=(VM,) * 8 + (AN, AN, VM),
        scratch_shapes=[
            pltpu.VMEM((C,) + table.shape, bf16), pltpu.VMEM(table.shape, f32), pltpu.VMEM((heads, T, LANES), f32),
        ]
        + sem2(c1) + sem2(c1) + sem2(2, R - 1) + sem2(R - 1) + sem2(R - 1) + sem2(R - 1)
        + sem2(R, 2, c1) + sem2(R - 1) + sem2(R, c1) + sem2(R - 1) + [dma((2,))],
        compiler_params=pltpu.CompilerParams(collective_id=0, has_side_effects=True, vmem_limit_bytes=60 * 2**20),
        name="forward_attention",
    )(stamp, prefix, x, table, gain, bias, w, wud, wo, ub)


def middle_kernel(
    R, C,
    x, cot, emb, att, wud_all, wo_all, ub_all, out_bias, gain, bias, down_bias,
    out, ghid, gatt, gs, gos, vecs, ubg,
    wbuf, hid, acc, gn, n2, n2t, cott, gbuf, crecv, obuf, orecv, gsend,
    wsem, c_s, c_r, o_s, o_r, a_s, a_r,
):
    r, c = lax.axis_index("row"), lax.axis_index("col")
    T, D = x.shape
    F = wud_all.shape[3]
    DC = gs.shape[2]
    TF = 384 if F % 384 == 0 else F
    tiles = F // TF
    cols = pl.ds(pl.multiple_of(c * DC, DC), DC)

    def fetch(s):
        return pltpu.make_async_copy(wud_all.at[:, lax.rem(r + s, R)], wbuf.at[lax.rem(s, 2)], wsem.at[lax.rem(s, 2)])

    fetch(0).start()
    fetch(1).start()
    greet({"row": R, "col": C})

    def c_copy(s, t):
        to = shifted("col", t, C)
        rows = pl.ds(pl.multiple_of(to * DC, DC), DC)
        return remote(gbuf.at[s, :, rows], crecv.at[s, t - 1], c_s.at[s, t - 1], c_r.at[s, t - 1], col=to)

    def o_copy(t):
        to = shifted("col", t, C)
        rows = pl.ds(pl.multiple_of(to * DC, DC), DC)
        return remote(obuf.at[:, rows], orecv.at[t - 1], o_s.at[t - 1], o_r.at[t - 1], col=to)

    TR = min(256, T)
    vsum = jnp.zeros((1, D), f32)
    for part in range(T // TR):
        rows = slice(part * TR, (part + 1) * TR)
        branch = mm(att[0, rows, :], wo_all[0], NT)
        for b in range(1, R):
            branch += mm(att[b, rows, :], wo_all[b], NT)
        hidden = x[rows, :].astype(f32) + emb[0:1, :] + branch + out_bias[...]
        hid[rows, :] = hidden
        centred, inverse = normalize(hidden, D)
        n2[rows, :] = (centred * gain[...] + bias[...]).astype(bf16)
        acc[rows, :] = jnp.zeros((TR, D), f32)
        gn[rows, :] = jnp.zeros((TR, D), f32)
        vsum = vsum + jnp.sum(cot[rows, :].astype(f32), axis=0, keepdims=True)
    n2t[...] = n2[...].T
    cott[...] = cot[...].T
    vecs[5:6, :] = vsum

    def block_step(s, carry):
        slot = lax.rem(s, 2)
        b = lax.rem(r + s, R)
        fetch(s).wait()

        def tile_step(t, inner_carry):
            fcols = pl.ds(pl.multiple_of(t * TF, TF), TF)
            wu = wbuf[slot, 0, :, fcols]
            wd = wbuf[slot, 1, :, fcols]
            inner = mm(n2[...], wu, NN) + ub_all[b, :, fcols]
            cdf = 0.5 * (1.0 + lax.erf(inner * 0.7071067811865476))
            slope = cdf + inner * (jnp.exp(-0.5 * inner * inner) * 0.3989422804014327)
            active = (inner * cdf).astype(bf16)
            acc[...] += mm(active, wd, NT)
            ginner = mm(cot[...], wd, NN) * slope
            glow = ginner.astype(bf16)
            gn[...] += mm(glow, wu, NT)
            gbuf[s, 1, :, fcols] = mm(cott[...], active, NN).astype(bf16)
            gbuf[s, 0, :, fcols] = mm(n2t[...], glow, NN).astype(bf16)
            ubg[b, :, fcols] = jnp.sum(ginner, axis=0, keepdims=True)
            return inner_carry

        lax.fori_loop(0, tiles, tile_step, 0)

        @pl.when(s + 2 < R)
        def _():
            fetch(s + 2).start()

        for t in range(1, C):
            c_copy(s, t).start()

        @pl.when(s > 0)
        def _():
            join(s - 1)

        return carry

    def join(s):
        b = lax.rem(r + s, R)
        for kind in range(2):
            total = gbuf[s, kind, cols, :].astype(f32)
            if kind == 0:
                for t in range(1, C):
                    c_copy(s, t).wait_recv()
            for t in range(1, C):
                total = total + crecv[s, t - 1, kind].astype(f32)
            gs[b, kind] = total.astype(bf16)

    lax.fori_loop(0, R, block_step, 0)

    gain_sum = jnp.zeros((1, D), f32)
    bias_sum = jnp.zeros((1, D), f32)
    hid_sum = jnp.zeros((1, D), f32)
    for part in range(T // TR):
        rows = slice(part * TR, (part + 1) * TR)
        hidden = hid[rows, :]
        out[rows, :] = (hidden + acc[rows, :] + down_bias[...]).astype(bf16)
        centred, inverse = normalize(hidden, D)
        g = gn[rows, :]
        scaled = g * gain[...]
        first = jnp.sum(scaled, axis=-1, keepdims=True) / D
        second = jnp.sum(scaled * centred, axis=-1, keepdims=True) / D
        gh = cot[rows, :].astype(f32) + inverse * (scaled - first - centred * second)
        ghid[rows, :] = gh
        n2[rows, :] = gh.astype(bf16)
        gain_sum = gain_sum + jnp.sum(g * centred, axis=0, keepdims=True)
        bias_sum = bias_sum + jnp.sum(g, axis=0, keepdims=True)
        hid_sum = hid_sum + jnp.sum(gh, axis=0, keepdims=True)
    vecs[0:2, :] = jnp.zeros((2, D), f32)
    vecs[2:3, :] = hid_sum
    vecs[3:4, :] = gain_sum
    vecs[4:5, :] = bias_sum
    vecs[6:8, :] = jnp.zeros((2, D), f32)

    def a_copy(s):
        b = lax.rem(r + s, R)
        return remote(gsend.at[b], gatt.at[r], a_s.at[s - 1], a_r.at[s - 1], row=b)

    def back_step(s, carry):
        b = lax.rem(r + s, R)
        gsend[b] = mm(n2[...], wo_all[b], NN).astype(bf16)

        @pl.when(s < R)
        def _():
            a_copy(s).start()

        return carry

    lax.fori_loop(1, R + 1, back_step, 0)
    gatt[r] = gsend[r]
    n2t[...] = n2[...].T

    def out_step(b, carry):
        obuf[b] = mm(n2t[...], att[b], NN).astype(bf16)
        return carry

    lax.fori_loop(0, R, out_step, 0)
    for t in range(1, C):
        o_copy(t).start()
    join(R - 1)
    for t in range(1, C):
        o_copy(t).wait_recv()
    for b in range(R):
        total = obuf[b, cols, :].astype(f32)
        for t in range(1, C):
            total = total + orecv[t - 1, b].astype(f32)
        gos[b] = total.astype(bf16)
    for s in range(1, R):
        a_copy(s).wait()
    for t in range(1, C):
        o_copy(t).wait_send()
        for s in range(R):
            c_copy(s, t).wait_send()


def run_middle(R, C, DC, x, cot, emb, att, wud_all, wo_all, ub_all, out_bias, gain, bias, down_bias):
    T, D = x.shape
    F = wud_all.shape[3]
    H = wo_all.shape[2]
    sds = jax.ShapeDtypeStruct
    dma = pltpu.SemaphoreType.DMA
    c1 = max(C - 1, 1)
    vm = pltpu.VMEM
    sem2 = lambda *shape: [dma(shape), dma(shape)]
    return pl.pallas_call(
        functools.partial(middle_kernel, R, C),
        out_shape=(
            sds((T, D), bf16), sds((T, D), f32), sds((R, T, H), bf16),
            sds((R, 2, DC, F), bf16), sds((R, DC, H), bf16), sds((8, D), f32), sds((R, 1, F), f32),
        ),
        in_specs=[VM] * 4 + [AN] + [VM] * 6,
        out_specs=(VM,) * 7,
        scratch_shapes=[
            vm((2, 2, D, F), bf16), vm((T, D), f32), vm((T, D), f32), vm((T, D), f32), vm((T, D), bf16),
            vm((D, T), bf16), vm((D, T), bf16), vm((R, 2, D, F), bf16), vm((R, c1, 2, DC, F), bf16),
            vm((R, D, H), bf16), vm((c1, R, DC, H), bf16), vm((R, T, H), bf16),
            dma((2,)),
        ]
        + sem2(R, c1) + sem2(c1) + sem2(R - 1),
        compiler_params=pltpu.CompilerParams(collective_id=1, has_side_effects=True, vmem_limit_bytes=62 * 2**20),
        name="feed_forward",
    )(x, cot, emb, att, wud_all, wo_all, ub_all, out_bias, gain, bias, down_bias)


def backward_kernel(
    R, C, Z,
    stamp, prefix_ref, q, k, v, mine, gatt, one, wq, gs, gos, ubg, vecs, x, emb, gain, ghid,
    tgrad, ffn_out, wo_out, qkv_out, small, table_out,
    d, dq, dk, dv, gp, part, prec, qg, qgb, qrecv, grow, orow, urow, blk, oblk, qblk, zr, zro, zrq,
    vbuf, vrow, vcol, vz,
    g_s, g_r, o_s, o_r, u_s, u_r, p_s, p_r, q_s, q_r, z_s, z_r, y_s, y_r, v_s, v_r, w_s, w_r, t_s, t_r,
):
    r, c, z = lax.axis_index("row"), lax.axis_index("col"), lax.axis_index("dp")
    _, T, H = gatt.shape
    D = x.shape[1]
    heads = H // HD
    L = R * T
    DC = gs.shape[2]
    DZ = blk.shape[1] // Z if zr.shape[2] != blk.shape[1] else blk.shape[1]
    split = DZ != blk.shape[1]
    NTB = table_out.shape[0]
    cols = pl.ds(pl.multiple_of(c * DC, DC), DC)
    greet({"row": R, "col": C, "dp": Z})

    def g_copy(s):
        b = lax.rem(r + s, R)
        return remote(gs.at[b], grow.at[s - 1], g_s.at[s - 1], g_r.at[s - 1], row=b)

    def o_copy(s):
        b = lax.rem(r + s, R)
        return remote(gos.at[b], orow.at[s - 1], o_s.at[s - 1], o_r.at[s - 1], row=b)

    def u_copy(s):
        b = lax.rem(r + s, R)
        return remote(ubg.at[b], urow.at[s - 1], u_s.at[s - 1], u_r.at[s - 1], row=b)

    for s in range(1, R):
        u_copy(s).start()
        g_copy(s).start()
    for s in range(1, R):
        o_copy(s).start()

    lane = lax.broadcasted_iota(jnp.int32, (T, HD), 1)

    def spread_step(b, carry):
        rows = pl.ds(pl.multiple_of(b * T, T), T)
        ga = gatt[b]
        both = ga.astype(f32) * mine[b].astype(f32)
        for h in range(heads):
            piece = slice(h * HD, (h + 1) * HD)
            delta = jnp.sum(both[:, piece], axis=1, keepdims=True)
            d[h, rows, :] = jnp.concatenate([ga[:, piece], split_parts(-delta, lane, 2)], axis=1)
        return carry

    lax.fori_loop(0, R, spread_step, 0)

    dq[...] = jnp.zeros_like(dq)
    dk[...] = jnp.zeros_like(dk)
    dv[...] = jnp.zeros_like(dv)
    prefix = prefix_ref[0]

    def pair(h, i, j, masked):
        qs = pl.ds(pl.multiple_of(i * T, T), T)
        ks = pl.ds(pl.multiple_of(j * T, T), T)
        qb, kb, vb, db = q[h, qs, :], k[h, ks, :], v[h, ks, :], d[h, qs, :]
        scores = mm(kb, qb, NT)
        if masked:
            limit = jnp.maximum(i * T + 1 + lax.broadcasted_iota(jnp.int32, (1, T), 1), prefix)
            place = j * T + lax.broadcasted_iota(jnp.int32, (T, T), 0)
            scores = jnp.where(place < limit, scores, masked_score)
        probs = jnp.exp(scores)
        gscores = (probs * mm(vb, db, NT)).astype(bf16)
        dv[h, ks, :] += mm(probs.astype(bf16), db, NN)
        dk[h, ks, :] += mm(gscores, qb, NN)
        dq[h, qs, :] += mm(gscores, kb, TN)

    def p_copy(b, s):
        return remote(part.at[b], prec.at[s - 1], p_s.at[s - 1], p_r.at[s - 1], row=b)

    def finish(b):
        rows = pl.ds(b * T, T)
        scale = HD ** (-0.5)
        stack = jnp.concatenate(
            [dq[h, rows, :][:, :HD] * scale for h in range(heads)]
            + [dk[h, rows, :][:, :HD] for h in range(heads)]
            + [dv[h, rows, :][:, :HD] for h in range(heads)],
            axis=1,
        ).astype(bf16)
        gp[b] = stack
        part[b] = mm(stack, wq[...], NT).astype(bf16)

        @pl.when(r != b)
        def _():
            p_copy(b, lax.rem(b - r + R, R)).start()

    early = R // 2
    for i in range(R - 1, early - 1, -1):

        def plain(t, carry, i=i):
            pair(t // i, i, lax.rem(t, i), False)
            return carry

        def diagonal(h, carry, i=i):
            pair(h, i, i, True)
            return carry

        lax.fori_loop(0, heads * i, plain, 0)
        lax.fori_loop(0, heads, diagonal, 0)
        finish(i)

    def square(t, carry):
        rest = lax.rem(t, early * early)
        pair(t // (early * early), rest // early, lax.rem(rest, early), True)
        return carry

    lax.fori_loop(0, heads * early * early, square, 0)
    for b in range(early - 1, -1, -1):
        finish(b)

    qg[...] = jnp.zeros_like(qg)

    def qkv_step(b, carry):
        qg[...] += mm(one[b], gp[b], TN)
        return carry

    lax.fori_loop(0, R, qkv_step, 0)
    qgb[...] = qg[...].astype(bf16)

    def q_copy(t):
        to = shifted("col", t, C)
        rows = pl.ds(pl.multiple_of(to * DC, DC), DC)
        return remote(qgb.at[rows], qrecv.at[t - 1], q_s.at[t - 1], q_r.at[t - 1], col=to)

    for t in range(1, C):
        q_copy(t).start()

    def z_copy(kind, s):
        to = lax.rem(z + s, Z)
        rows = pl.ds(pl.multiple_of(to * DZ, DZ), DZ) if split else slice(None)
        source, target = ((blk, zr), (oblk, zro), (qblk, zrq))[kind]
        if kind == 0:
            return remote(source.at[:, rows], target.at[s - 1], z_s.at[kind, s - 1], z_r.at[kind, s - 1], dp=to)
        return remote(source.at[rows], target.at[s - 1], z_s.at[kind, s - 1], z_r.at[kind, s - 1], dp=to)

    def y_copy(kind, s):
        to = lax.rem(z + s, Z)
        rows = pl.ds(pl.multiple_of(z * DZ, DZ), DZ)
        ref = (ffn_out, wo_out, qkv_out)[kind]
        piece = ref.at[:, rows] if kind == 0 else ref.at[rows]
        return remote(piece, piece, y_s.at[kind, s - 1], y_r.at[kind, s - 1], dp=to)

    def reduce_data(kind):
        for s in range(1, Z):
            z_copy(kind, s).wait_recv()
        rows = pl.ds(pl.multiple_of(z * DZ, DZ), DZ) if split else slice(None)
        source, target = ((blk, zr), (oblk, zro), (qblk, zrq))[kind]
        ref = (ffn_out, wo_out, qkv_out)[kind]
        for array in range(2 if kind == 0 else 1):
            where = (array, rows) if kind == 0 else (rows,)
            total = source[where].astype(f32)
            for s in range(1, Z):
                got = target[s - 1, array] if kind == 0 else target[s - 1]
                total = total + got.astype(f32)
            ref[where] = total.astype(bf16)
        if split:
            for s in range(1, Z):
                y_copy(kind, s).start()

    for s in range(1, R):
        g_copy(s).wait_recv()
    for array in range(2):
        total = gs[r, array].astype(f32)
        for s in range(1, R):
            total = total + grow[s - 1, array].astype(f32)
        blk[array] = total.astype(bf16)
    for s in range(1, Z):
        z_copy(0, s).start()
    for s in range(1, R):
        o_copy(s).wait_recv()
    total = gos[r].astype(f32)
    for s in range(1, R):
        total = total + orow[s - 1].astype(f32)
    oblk[...] = total.astype(bf16)
    for s in range(1, Z):
        z_copy(1, s).start()
    for t in range(1, C):
        q_copy(t).wait_recv()
    total = qgb[cols, :].astype(f32)
    for t in range(1, C):
        total = total + qrecv[t - 1].astype(f32)
    qblk[...] = total.astype(bf16)
    for s in range(1, Z):
        z_copy(2, s).start()
    reduce_data(0)

    for s in range(1, R):
        remote(part.at[0], prec.at[s - 1], p_s.at[s - 1], p_r.at[s - 1], row=lax.rem(r + s, R)).wait_recv()
        u_copy(s).wait_recv()
    TR = min(256, T)
    gain_sum = jnp.zeros((1, D), f32)
    bias_sum = jnp.zeros((1, D), f32)
    all_sum = jnp.zeros((1, D), f32)
    for piece in range(T // TR):
        rows = slice(piece * TR, (piece + 1) * TR)
        g = part[r, rows, :].astype(f32)
        for s in range(1, R):
            g = g + prec[s - 1, rows, :].astype(f32)
        centred, inverse = normalize(x[rows, :].astype(f32) + emb[0:1, :], D)
        scaled = g * gain[...]
        first = jnp.sum(scaled, axis=-1, keepdims=True) / D
        second = jnp.sum(scaled * centred, axis=-1, keepdims=True) / D
        total = ghid[rows, :] + inverse * (scaled - first - centred * second)
        tgrad[rows, :] = total
        gain_sum = gain_sum + jnp.sum(g * centred, axis=0, keepdims=True)
        bias_sum = bias_sum + jnp.sum(g, axis=0, keepdims=True)
        all_sum = all_sum + jnp.sum(total, axis=0, keepdims=True)

    vbuf[...] = vecs[...]
    vbuf[0:1, :] = gain_sum
    vbuf[1:2, :] = bias_sum
    vbuf[6:7, :] = all_sum

    def v_copy(s):
        return remote(vbuf, vrow.at[s - 1], v_s.at[s - 1], v_r.at[s - 1], row=lax.rem(r + s, R))

    for s in range(1, R):
        v_copy(s).start()
    reduce_data(1)
    reduce_data(2)
    up_bias = ubg[r]
    for s in range(1, R):
        up_bias = up_bias + urow[s - 1]
    for s in range(1, R):
        v_copy(s).wait_recv()
    total = vbuf[...]
    for s in range(1, R):
        total = total + vrow[s - 1]
    vcol[c, 0:8, :] = total
    vcol[c, 7:8, :] = up_bias
    vcol[c, 8:16, :] = jnp.full((8, D), stamp[0].astype(f32))

    def w_copy(t):
        return remote(vcol.at[c], vcol.at[c], w_s.at[t - 1], w_r.at[t - 1], col=shifted("col", t, C))

    for t in range(1, C):
        w_copy(t).start()
    for t in range(1, C):
        w_copy(t).wait_recv()

    def t_copy(s):
        return remote(vcol, vz.at[s - 1], t_s.at[s - 1], t_r.at[s - 1], dp=lax.rem(z + s, Z))

    for s in range(1, Z):
        t_copy(s).start()
    for s in range(1, Z):
        t_copy(s).wait_recv()
    total = jnp.zeros((8, D), f32)
    number = (lax.broadcasted_iota(jnp.int32, (NTB, D), 0) + c * NTB).astype(f32)
    table = jnp.zeros((NTB, D), f32)
    for s in range(Z):
        for t in range(C):
            entry = vcol[t] if s == 0 else vz[s - 1, t]
            total = total + entry[0:8]
            table = table + jnp.where(number == entry[8:9], entry[6:7], 0.0)
    small[...] = total
    table_out[...] = table

    for s in range(1, R):
        g_copy(s).wait_send()
        o_copy(s).wait_send()
        u_copy(s).wait_send()
        v_copy(s).wait_send()
        remote(part.at[0], prec.at[s - 1], p_s.at[s - 1], p_r.at[s - 1], row=lax.rem(r + s, R)).wait_send()
    for t in range(1, C):
        q_copy(t).wait_send()
        w_copy(t).wait_send()
    for s in range(1, Z):
        t_copy(s).wait_send()
        for kind in range(3):
            z_copy(kind, s).wait_send()
            if split:
                y_copy(kind, s).wait()


def run_backward(R, C, Z, NTB, stamp, prefix, q, k, v, mine, gatt, one, wq, gs, gos, ubg, vecs, x, emb, gain, ghid):
    T, D = x.shape
    H = gatt.shape[2]
    heads = H // HD
    L = R * T
    DC, F = gs.shape[2], gs.shape[3]
    DZ = DC // Z if DC % (16 * Z) == 0 else DC
    sds = jax.ShapeDtypeStruct
    dma = pltpu.SemaphoreType.DMA
    c1 = max(C - 1, 1)
    vm = pltpu.VMEM
    sem2 = lambda *shape: [dma(shape), dma(shape)]
    return pl.pallas_call(
        functools.partial(backward_kernel, R, C, Z),
        out_shape=(
            sds((T, D), f32), sds((2, DC, F), bf16), sds((DC, H), bf16), sds((DC, 3 * H), bf16),
            sds((8, D), f32), sds((NTB, D), f32),
        ),
        in_specs=[SM, SM] + [VM] * 15,
        out_specs=(VM,) * 6,
        scratch_shapes=[
            vm((heads, L, LANES), bf16), vm((heads, L, LANES), f32), vm((heads, L, LANES), f32), vm((heads, L, LANES), f32),
            vm((R, T, 3 * H), bf16), vm((R, T, D), bf16), vm((R - 1, T, D), bf16), vm((D, 3 * H), f32), vm((D, 3 * H), bf16),
            vm((c1, DC, 3 * H), bf16), vm((R - 1, 2, DC, F), bf16), vm((R - 1, DC, H), bf16), vm((R - 1, 1, F), f32),
            vm((2, DC, F), bf16), vm((DC, H), bf16), vm((DC, 3 * H), bf16),
            vm((Z - 1, 2, DZ, F), bf16), vm((Z - 1, DZ, H), bf16), vm((Z - 1, DZ, 3 * H), bf16),
            vm((8, D), f32), vm((R - 1, 8, D), f32), vm((C, 16, D), f32), vm((Z - 1, C, 16, D), f32),
        ]
        + sem2(R - 1) * 4 + sem2(c1) + sem2(3, Z - 1) + sem2(3, Z - 1) + sem2(R - 1) + sem2(c1) + sem2(Z - 1),
        compiler_params=pltpu.CompilerParams(collective_id=2, has_side_effects=True, vmem_limit_bytes=63 * 2**20),
        name="backward_attention",
    )(stamp, prefix, q, k, v, mine, gatt, one, wq, gs, gos, ubg, vecs, x, emb, gain, ghid)


def body(R, C, Z, *args):
    (tokens, cotangent, timesteps, prefix_len, time_table, ln1_gain, ln1_bias, w_qkv, w_out, out_bias,
     ln2_gain, ln2_bias, w_up, up_bias, w_down, down_bias) = args
    DC, _, H = w_qkv.shape
    D = tokens.shape[2]
    x, cot = tokens[0], cotangent[0]
    row = lambda vector: vector[None, :]
    q, k, v, one, wq, emb, att, mine, wud_all, wo_all, ub_all = run_forward(
        R, C, Z, timesteps, prefix_len, x, time_table, row(ln1_gain), row(ln1_bias),
        w_qkv.reshape(DC, 3 * H), jnp.stack([w_up, w_down]), w_out, row(up_bias),
    )
    out, ghid, gatt, gs, gos, vecs, ubg = run_middle(
        R, C, DC, x, cot, emb, att, wud_all, wo_all, ub_all,
        row(out_bias), row(ln2_gain), row(ln2_bias), row(down_bias),
    )
    tgrad, ffn, wo, qkv, small, table = run_backward(
        R, C, Z, time_table.shape[0], timesteps, prefix_len, q, k, v, mine, gatt, one, wq, gs, gos, ubg, vecs,
        x, emb, row(ln1_gain), ghid,
    )
    return (
        out[None], tgrad[None], table, small[0], small[1], qkv.astype(f32).reshape(DC, 3, H), wo.astype(f32),
        small[2], small[3], small[4], ffn[0].astype(f32), small[7], ffn[1].astype(f32), small[5],
    )


def solution(mesh):
    R, C, Z = mesh.shape["row"], mesh.shape["col"], mesh.shape["dp"]
    batch = P(("dp", "col"), "row", None)
    block = P("col", "row")
    return jax.shard_map(
        functools.partial(body, R, C, Z),
        mesh=mesh,
        in_specs=(
            batch, batch, P(("dp", "col")), P(("dp", "col")), P("col", None), P(), P(), P("col", None, "row"), block,
            P(), P(), P(), block, P("row"), block, P(),
        ),
        out_specs=(
            batch, batch, P("col", None), P(), P(), P("col", None, "row"), block, P(), P(), P(), block, P("row"),
            block, P(),
        ),
        check_vma=False,
    )
```

```python
import functools
from types import SimpleNamespace

import jax
import jax.numpy as jnp
from jax import lax
from jax.experimental import pallas as pl
from jax.experimental.pallas import tpu as pltpu
from jax.sharding import PartitionSpec as P

HD = 64
LANES = 128
norm_eps = 1e-05
masked_score = -1e30
f32, bf16 = jnp.float32, jnp.bfloat16
MESH = pl.DeviceIdType.MESH
NN = (((1,), (0,)), ((), ()))
NT = (((1,), (1,)), ((), ()))
TN = (((0,), (0,)), ((), ()))
VM = pl.BlockSpec(memory_space=pltpu.VMEM)
SM = pl.BlockSpec(memory_space=pltpu.SMEM)
AN = pl.BlockSpec(memory_space=pl.ANY)
R = 4


def mm(a, b, dims):
    return lax.dot_general(a, b, dims, preferred_element_type=f32)


def remote(src, dst, sems, index, **where):
    return pltpu.make_async_remote_copy(
        src_ref=src, dst_ref=dst, send_sem=sems[0].at[index], recv_sem=sems[1].at[index],
        device_id=where, device_id_type=MESH,
    )


def flip(a, b):
    a0, b0, a1, b1 = lax.rem(a, 2), lax.rem(b, 2), a // 2, b // 2
    return a0 + b0 - 2 * a0 * b0 + 2 * (a1 + b1 - 2 * a1 * b1)


def greet(sizes):
    barrier = pltpu.get_barrier_semaphore()
    total = 0
    for name, count in sizes.items():
        for step in range(1, count):
            to = lax.rem(lax.axis_index(name) + step, count)
            pl.semaphore_signal(barrier, inc=1, device_id={name: to}, device_id_type=MESH)
            total += 1
    pl.semaphore_wait(barrier, total)


def normalize(hidden, width):
    average = jnp.sum(hidden, axis=-1, keepdims=True) / width
    variance = jnp.sum(hidden * hidden, axis=-1, keepdims=True) / width - average * average
    inverse = lax.rsqrt(variance + norm_eps)
    return (hidden - average) * inverse, inverse


def norm_back(grad, centred, inverse, gain, width):
    scaled = grad * gain
    first = jnp.sum(scaled, axis=-1, keepdims=True) / width
    second = jnp.sum(scaled * centred, axis=-1, keepdims=True) / width
    return inverse * (scaled - first - centred * second)


def split_parts(value, lane, count):
    out = jnp.zeros(lane.shape, f32)
    for place in range(count):
        high = value.astype(bf16).astype(f32)
        out = jnp.where(lane == place, high, out)
        value = value - high
    return out.astype(bf16)


def layer_kernel(names, C, Z, *refs):
    n = SimpleNamespace(**dict(zip([name for name in names if not name.startswith("sem_")], refs)))
    plain = sum(1 for name in names if not name.startswith("sem_"))
    sem = {}
    place = plain
    for name in names:
        if name.startswith("sem_"):
            sem[name[4:]] = (refs[place], refs[place + 1])
            place += 2
    local = refs[place]
    r, c, z = lax.axis_index("row"), lax.axis_index("col"), lax.axis_index("dp")
    T, D = n.x.shape
    DC, F = n.w_up.shape
    H = n.w_out.shape[1]
    heads = H // HD
    L = R * T
    half = T // 2
    NTB = n.table.shape[0]
    parity = lax.rem(z, 2)
    zpair = z + 1 - 2 * parity
    nx, ny = flip(r, 1), flip(r, 2)
    cols = pl.ds(pl.multiple_of(c * DC, DC), DC)
    vec = lambda row: n.vectors[row : row + 1, :]
    others = range(1, R)
    peers = range(1, C)
    groups = range(1, Z)

    def col_at(t):
        return lax.rem(c + t, C)

    def rows_of(device):
        return pl.ds(pl.multiple_of(device * DC, DC), DC)

    greet({"row": R, "col": C, "dp": Z})

    def stamp_copy(t):
        return remote(n.stamp_own, n.stamp_got.at[t - 1], sem["stamp"], t - 1, col=col_at(t))

    def pick_copy(t):
        return remote(n.picked.at[t - 1], n.picked_got.at[t - 1], sem["pick"], t - 1, col=lax.rem(c - t + C, C))

    def w_copy(t):
        return remote(n.w_qkv, n.wq.at[cols], sem["w"], t - 1, col=col_at(t))

    n.stamp_own[...] = jnp.full(n.stamp_own.shape, n.stamp[0].astype(f32))
    for t in peers:
        stamp_copy(t).start()
    for t in peers:
        w_copy(t).start()
    n.wq[cols, :] = n.w_qkv[...]

    def row_of(stamps):
        number = (lax.broadcasted_iota(jnp.int32, (NTB, D), 0) + c * NTB).astype(f32)
        return jnp.sum(jnp.where(number == stamps, n.table[...].astype(f32), 0.0), axis=0, keepdims=True)

    for t in peers:
        stamp_copy(t).wait_recv()
        n.picked[t - 1] = jnp.broadcast_to(row_of(n.stamp_got[t - 1][0:1, 0:1]), (8, D))
        pick_copy(t).start()
    embed = row_of(n.stamp_own[0:1, 0:1])
    for t in peers:
        pick_copy(t).wait_recv()
        embed = embed + n.picked_got[t - 1][0:1]
    n.emb[...] = jnp.broadcast_to(embed, n.emb.shape)

    def n_copy(link, part):
        piece = n.one.at[r, pl.ds(part * half, half)]
        return remote(piece, piece, sem["n"], 2 * link + part, row=(nx, ny)[link])

    def relay_copy(link):
        piece = n.one.at[(ny, nx)[link], pl.ds(link * half, half)]
        return remote(piece, piece, sem["relay"], link, row=(nx, ny)[link])

    rows_ln = 128
    for part in range(2):

        def norm_step(t, carry, part=part):
            rows = pl.ds(pl.multiple_of(part * half + t * rows_ln, rows_ln), rows_ln)
            centred, inverse = normalize(n.x[rows, :].astype(f32) + n.emb[0:1, :], D)
            n.one[r, rows, :] = (centred * vec(0) + vec(1)).astype(bf16)
            return carry

        lax.fori_loop(0, half // rows_ln, norm_step, 0)
        n_copy(1 - part, part).start()
    n_copy(0, 0).start()
    n_copy(1, 1).start()

    for t in peers:
        w_copy(t).wait_recv()
    lane = lax.broadcasted_iota(jnp.int32, (T, HD), 1)
    q_tail = jnp.zeros((T, HD), bf16)
    k_tail = jnp.where(lane < 3, 1.0, 0.0).astype(bf16)
    v_tail = jnp.where(lane < 2, 1.0, 0.0).astype(bf16)
    scale = HD ** (-0.5)

    def project(s, carry):
        @pl.when(s == 1)
        def _():
            n_copy(1, 0).wait_recv()
            relay_copy(0).start()
            n_copy(0, 1).wait_recv()
            relay_copy(1).start()
            n_copy(0, 0).wait_recv()

        @pl.when(s == 2)
        def _():
            n_copy(1, 1).wait_recv()

        @pl.when(s == 3)
        def _():
            relay_copy(0).wait_recv()
            relay_copy(1).wait_recv()
            weights_start()

        block = flip(r, s)
        y = mm(n.one[block], n.wq[...], NN).astype(bf16)
        rows = pl.ds(pl.multiple_of(block * T, T), T)
        for h in range(heads):
            n.q[h, rows, :] = jnp.concatenate([y[:, h * HD : (h + 1) * HD] * scale, q_tail], axis=1)
            n.k[h, rows, :] = jnp.concatenate([y[:, H + h * HD : H + (h + 1) * HD], k_tail], axis=1)
            n.v[h, rows, :] = jnp.concatenate([y[:, 2 * H + h * HD : 2 * H + (h + 1) * HD], v_tail], axis=1)
        return carry

    def up_down(kind, link, s, go):
        if s == 0:
            for t in peers:
                source = (n.w_up, n.w_down)[kind]
                go(remote(source, n.wud.at[kind, r, cols], sem["gc"], kind * (C - 1) + t - 1, col=col_at(t)))
            return
        source = (n.w_up, n.w_down)[kind]
        go(remote(source, n.wud.at[kind, r, cols], sem["g"], s - 1, row=flip(r, s)))

    def g_start(s):
        for kind in range(2):

            @pl.when(parity == kind)
            def _(kind=kind):
                up_down(kind, 0, s, lambda copy: copy.start())

    def g_copy(s):
        piece = n.wud.at[parity, flip(r, s), cols]
        return remote(n.w_up, piece, sem["g"], s - 1, row=flip(r, s))

    def z_copy(s):
        piece = n.wud.at[parity, flip(r, s), cols]
        return remote(piece, piece, sem["gz"], s - 1, dp=zpair)

    def gc_copy(s, kind, t):
        piece = n.wud.at[parity if kind == 0 else 1 - parity, flip(r, s), cols]
        return remote(piece, piece, sem["gc"], (2 * s + kind) * (C - 1) + t - 1, col=col_at(t))

    def gc_own(kind, t):
        source = (n.w_up, n.w_down)[kind]
        return remote(source, n.wud.at[kind, r, cols], sem["gc"], kind * (C - 1) + t - 1, col=col_at(t))

    def wo_copy(s):
        piece = n.wo.at[r, cols]
        return remote(n.w_out, piece, sem["wo"], s - 1, row=flip(r, s))

    def woc_copy(s, t):
        piece = n.wo.at[flip(r, s), cols]
        source = n.w_out if s == 0 else piece
        return remote(source, piece, sem["woc"], s * (C - 1) + t - 1, col=col_at(t))

    def ub_copy(s):
        return remote(n.ub.at[r], n.ub.at[r], sem["ub"], s - 1, row=flip(r, s))

    own_up = pltpu.make_async_copy(n.w_up, n.wud.at[0, r, cols], local.at[0])
    own_down = pltpu.make_async_copy(n.w_down, n.wud.at[1, r, cols], local.at[1])
    n.ub[r] = jnp.broadcast_to(n.vectors[6:7, 0:F], (8, F))
    n.wo[r, cols, :] = n.w_out[...]

    def weights_start():
        for s in others:
            wo_copy(s).start()
            ub_copy(s).start()
        g_start(1)
        g_start(2)

    for t in peers:
        woc_copy(0, t).start()
        for kind in range(2):
            gc_own(kind, t).start()
    own_up.start()
    own_down.start()

    lax.fori_loop(0, R, project, 0)

    prefix = n.prefix[0]
    longest = L // 2
    SB = min(256, T)
    nsub = T // SB
    lane_sb = lax.broadcasted_iota(jnp.int32, (SB, HD), 1)

    def a_copy(s):
        i = flip(r, s)
        return remote(n.mine.at[i], n.att.at[r], sem["a"], s - 1, row=i)

    def attend_block(step, carry):
        s = lax.rem(step + 1, R)
        i = flip(r, s)
        for static in range(R):
            early = (static + 1) * T <= longest
            nk = longest if early else (static + 1) * T
            nm = nk if early else T

            def attend(t, inner, nk=nk, nm=nm):
                h = t // nsub
                sub = pl.multiple_of(lax.rem(t, nsub) * SB, SB)
                row = i * T + sub
                rows = pl.ds(pl.multiple_of(row, SB), SB)
                scores = mm(n.q[h, rows, :], n.k[h, :nk, :], NT)
                limit = jnp.maximum(row + 1 + lax.broadcasted_iota(jnp.int32, (SB, 1), 0), prefix)
                key = (nk - nm) + lax.broadcasted_iota(jnp.int32, (SB, nm), 1)
                last = jnp.where(key < limit, scores[:, nk - nm :], masked_score)
                top = jnp.max(last, axis=1, keepdims=True)
                if nk > nm:
                    top = jnp.maximum(top, jnp.max(scores[:, : nk - nm], axis=1, keepdims=True))
                mixed = mm(jnp.exp(last - top).astype(bf16), n.v[h, nk - nm : nk, :], NN)
                if nk > nm:
                    mixed += mm(jnp.exp(scores[:, : nk - nm] - top).astype(bf16), n.v[h, : nk - nm, :], NN)
                weight = mixed[:, HD : HD + 1]
                n.mixed[h, pl.ds(sub, SB), :] = mixed / weight
                n.q[h, rows, HD:] = split_parts(-(top + jnp.log(weight)), lane_sb, 3)
                return inner

            @pl.when(i == static)
            def _(attend=attend):
                lax.fori_loop(0, heads * nsub, attend, 0)

        n.mine[i] = jnp.concatenate([n.mixed[h][:, :HD] for h in range(heads)], axis=1).astype(bf16)

        for at in range(R - 1):

            @pl.when(step == at)
            def _(at=at):
                a_copy(at + 1).start()
                if at == 0:
                    for s in others:
                        wo_copy(s).wait_recv()
                        for t in peers:
                            woc_copy(s, t).start()
                if at == 1:
                    for s in (1, 2):
                        g_copy(s).wait_recv()
                        z_copy(s).start()
                        for t in peers:
                            gc_copy(s, 0, t).start()
                    g_start(3)

        return carry

    def attend_all(mixed_ref):
        n.mixed = mixed_ref
        lax.fori_loop(0, R, attend_block, 0)

    pl.run_scoped(attend_all, pltpu.VMEM((heads, T, LANES), f32))
    n.att[r] = n.mine[r]

    TR = min(256, T)
    TF = 384 if F % 384 == 0 else F
    tiles = F // TF
    ticks = R * tiles

    def a2_copy(s):
        b = flip(r, s)
        return remote(n.gsend.at[b], n.gatt.at[r], sem["a2"], s - 1, row=b)

    def row_copy(s, kind):
        return remote(n.crecv.at[s, 0, kind], n.grow.at[s - 1, kind], sem["row"], 2 * (s - 1) + kind, row=flip(r, s))

    def wrow_copy(s):
        b = flip(r, s)
        return remote(n.orecv.at[0, b], n.orow.at[s - 1], sem["wrow"], s - 1, row=b)

    def u_copy(s):
        return remote(n.ubg.at[flip(r, s)], n.urow.at[s - 1], sem["u"], s - 1, row=flip(r, s))

    def middle(wbuf, acc, gn, n2, n2t, cott, gbuf, obuf):
        def fetch(tick):
            fcols = pl.ds(pl.multiple_of(lax.rem(tick, tiles) * TF, TF), TF)
            slot = lax.rem(tick, 2)
            return pltpu.make_async_copy(
                n.wud.at[:, flip(r, tick // tiles), :, fcols], wbuf.at[slot], local.at[2 + slot]
            )

        def c_copy(s, t):
            to = col_at(t)
            return remote(
                gbuf.at[lax.rem(s, 2), :, rows_of(to)], n.crecv.at[s, t - 1], sem["c"], s * (C - 1) + t - 1, col=to
            )

        def o_copy(t):
            to = col_at(t)
            return remote(obuf.at[:, rows_of(to)], n.orecv.at[t - 1], sem["o"], t - 1, col=to)

        def join(s):
            for t in peers:
                c_copy(s, t).wait_recv()
            for kind in range(2):
                total = gbuf[lax.rem(s, 2), kind, cols, :].astype(f32)
                for t in peers:
                    total = total + n.crecv[s, t - 1, kind].astype(f32)
                n.crecv[s, 0, kind] = total.astype(bf16)

        def send_row(s):
            u_copy(s).start()
            for kind in range(2):
                row_copy(s, kind).start()

        own_up.wait()
        own_down.wait()
        for t in peers:
            for kind in range(2):
                gc_own(kind, t).wait()
        fetch(0).start()
        cott[...] = n.cot[...].T
        for s in others:
            for t in peers:
                woc_copy(s, t).wait_recv()
        for t in peers:
            woc_copy(0, t).wait_recv()
        for s in others:
            ub_copy(s).wait_recv()
            a_copy(s).wait_recv()
        vsum = jnp.zeros((1, D), f32)
        for part in range(T // TR):
            rows = slice(part * TR, (part + 1) * TR)
            branch = mm(n.att[0, rows, :], n.wo[0], NT)
            for b in range(1, R):
                branch += mm(n.att[b, rows, :], n.wo[b], NT)
            hidden = n.x[rows, :].astype(f32) + n.emb[0:1, :] + branch + vec(2)
            n.tgrad[rows, :] = hidden
            centred, inverse = normalize(hidden, D)
            n2[rows, :] = (centred * vec(3) + vec(4)).astype(bf16)
            acc[rows, :] = jnp.zeros((TR, D), f32)
            gn[rows, :] = jnp.zeros((TR, D), f32)
            vsum = vsum + jnp.sum(n.cot[rows, :].astype(f32), axis=0, keepdims=True)
        n2t[...] = n2[...].T
        n.vbuf[5:6, :] = vsum

        def tick_step(tick, carry):
            s, t = tick // tiles, lax.rem(tick, tiles)
            b = flip(r, s)
            slot, wslot = lax.rem(s, 2), lax.rem(tick, 2)
            fetch(tick).wait()

            @pl.when((t == 0) & (s + 1 < R))
            def _():
                @pl.when(s == 0)
                def _():
                    g_copy(3).wait_recv()
                    z_copy(3).start()
                    for p in peers:
                        gc_copy(3, 0, p).start()

                z_copy(s + 1).wait_recv()
                for p in peers:
                    gc_copy(s + 1, 1, p).start()

            @pl.when((t == 0) & (s >= 2))
            def _():
                for p in peers:
                    c_copy(s - 2, p).wait_send()

            @pl.when((t == tiles - 1) & (s + 1 < R))
            def _():
                for p in peers:
                    gc_copy(s + 1, 0, p).wait_recv()
                    gc_copy(s + 1, 1, p).wait_recv()

            @pl.when(tick + 1 < ticks)
            def _():
                fetch(tick + 1).start()

            fcols = pl.ds(pl.multiple_of(t * TF, TF), TF)
            wu = wbuf[wslot, 0]
            wd = wbuf[wslot, 1]
            inner = mm(n2[...], wu, NN) + n.ub[b, 0:1, fcols]
            cdf = 0.5 * (1.0 + lax.erf(inner * 0.7071067811865476))
            slope = cdf + inner * (jnp.exp(-0.5 * inner * inner) * 0.3989422804014327)
            active = (inner * cdf).astype(bf16)
            acc[...] += mm(active, wd, NT)
            ginner = mm(n.cot[...], wd, NN) * slope
            glow = ginner.astype(bf16)
            gn[...] += mm(glow, wu, NT)
            gbuf[slot, 1, :, fcols] = mm(cott[...], active, NN).astype(bf16)
            gbuf[slot, 0, :, fcols] = mm(n2t[...], glow, NN).astype(bf16)
            n.ubg[b, :, fcols] = jnp.sum(ginner, axis=0, keepdims=True)

            @pl.when(t == tiles - 1)
            def _():
                for p in peers:
                    c_copy(s, p).start()

            @pl.when((t == 0) & (s > 0))
            def _():
                join(s - 1)

                @pl.when(s > 1)
                def _():
                    send_row(s - 1)

            return carry

        lax.fori_loop(0, ticks, tick_step, 0)

        gain_sum = jnp.zeros((1, D), f32)
        bias_sum = jnp.zeros((1, D), f32)
        hid_sum = jnp.zeros((1, D), f32)
        for part in range(T // TR):
            rows = slice(part * TR, (part + 1) * TR)
            hidden = n.tgrad[rows, :]
            n.out[rows, :] = (hidden + acc[rows, :] + vec(5)).astype(bf16)
            centred, inverse = normalize(hidden, D)
            g = gn[rows, :]
            gh = n.cot[rows, :].astype(f32) + norm_back(g, centred, inverse, vec(3), D)
            n.tgrad[rows, :] = gh
            n2[rows, :] = gh.astype(bf16)
            gain_sum = gain_sum + jnp.sum(g * centred, axis=0, keepdims=True)
            bias_sum = bias_sum + jnp.sum(g, axis=0, keepdims=True)
            hid_sum = hid_sum + jnp.sum(gh, axis=0, keepdims=True)
        n.vbuf[2:3, :] = hid_sum
        n.vbuf[3:4, :] = gain_sum
        n.vbuf[4:5, :] = bias_sum

        def back_step(at, carry):
            s = R - 1 - at
            b = flip(r, s)
            n.gsend[b] = mm(n2[...], n.wo[b], NN).astype(bf16)

            @pl.when(s > 0)
            def _():
                a2_copy(s).start()

            return carry

        lax.fori_loop(0, R, back_step, 0)
        n.gatt[r] = n.gsend[r]
        n2t[...] = n2[...].T
        join(R - 1)
        send_row(R - 1)

        def out_step(b, carry):
            obuf[b] = mm(n2t[...], n.att[b], NN).astype(bf16)
            return carry

        lax.fori_loop(0, R, out_step, 0)
        for t in peers:
            o_copy(t).start()
        for t in peers:
            o_copy(t).wait_recv()
        for b in range(R):
            total = obuf[b, cols, :].astype(f32)
            for t in peers:
                total = total + n.orecv[t - 1, b].astype(f32)
            n.orecv[0, b] = total.astype(bf16)
        for s in others:
            wrow_copy(s).start()
        for t in peers:
            o_copy(t).wait_send()
            for s in range(R - 2, R):
                c_copy(s, t).wait_send()

    dt = bf16
    pl.run_scoped(
        middle,
        pltpu.VMEM((2, 2, D, TF), dt), pltpu.VMEM((T, D), f32), pltpu.VMEM((T, D), f32), pltpu.VMEM((T, D), dt),
        pltpu.VMEM((D, T), dt), pltpu.VMEM((D, T), dt), pltpu.VMEM((2, 2, D, F), dt), pltpu.VMEM((R, D, H), dt),
    )

    DZ = n.zr.shape[2]
    split = DZ != DC
    sources = (n.crecv.at[0, 0, 0], n.crecv.at[0, 0, 1], n.oblk, n.qblk)
    landing = (n.zr.at[0], n.zr.at[1], n.zro, n.zrq)
    finals = (n.up_out, n.down_out, n.wo_out, n.qkv_out)

    def part_of(device):
        return pl.ds(pl.multiple_of(device * DZ, DZ), DZ) if split else slice(None)

    def zz_copy(kind, s):
        to = lax.rem(z + s, Z)
        return remote(sources[kind].at[part_of(to)], landing[kind].at[s - 1], sem["z"], kind * (Z - 1) + s - 1, dp=to)

    def y_copy(kind, s):
        piece = finals[kind].at[part_of(z)]
        return remote(piece, piece, sem["y"], kind * (Z - 1) + s - 1, dp=lax.rem(z + s, Z))

    def row_sum(kind):
        for s in others:
            row_copy(s, kind).wait_recv()
        total = n.crecv[0, 0, kind].astype(f32)
        for s in others:
            total = total + n.grow[s - 1, kind].astype(f32)
        n.crecv[0, 0, kind] = total.astype(bf16)
        for s in groups:
            zz_copy(kind, s).start()

    def wrow_sum():
        for s in others:
            wrow_copy(s).wait_recv()
        total = n.orecv[0, r].astype(f32)
        for s in others:
            total = total + n.orow[s - 1].astype(f32)
        n.oblk[...] = total.astype(bf16)
        for s in groups:
            zz_copy(2, s).start()

    def data_sum(kind):
        for s in groups:
            zz_copy(kind, s).wait_recv()
        total = sources[kind][part_of(z), :].astype(f32)
        for s in groups:
            total = total + landing[kind][s - 1].astype(f32)
        finals[kind][part_of(z), :] = total.astype(bf16)
        if split:
            for s in groups:
                y_copy(kind, s).start()

    def p_copy(link, part, b):
        piece = pl.ds(part * half, half)
        return remote(n.part.at[b, piece], n.prec.at[link, piece], sem["p"], 2 * link + part, row=(nx, ny)[link])

    def pr_copy(link, b):
        return remote(n.part.at[b, pl.ds(link * half, half)], n.prel.at[link], sem["pr"], link, row=(nx, ny)[link])

    def back(d, dq, dk, dv, gp, qg):
        def spread(b):
            rows = pl.ds(b * T, T)

            @pl.when(r != b)
            def _():
                s = flip(r, b)
                remote(n.gsend.at[b], n.gatt.at[b], sem["a2"], s - 1, row=b).wait_recv()

            ga = n.gatt[b]
            both = ga.astype(f32) * n.mine[b].astype(f32)
            for h in range(heads):
                piece = slice(h * HD, (h + 1) * HD)
                delta = jnp.sum(both[:, piece], axis=1, keepdims=True)
                d[h, rows, :] = jnp.concatenate([ga[:, piece], split_parts(-delta, lane, 2)], axis=1)

        def pair(h, i, j, masked):
            qs = pl.ds(pl.multiple_of(i * T, T), T)
            ks = pl.ds(pl.multiple_of(j * T, T), T)
            qb, kb, vb, db = n.q[h, qs, :], n.k[h, ks, :], n.v[h, ks, :], d[h, qs, :]
            scores = mm(kb, qb, NT)
            if masked:
                limit = jnp.maximum(i * T + 1 + lax.broadcasted_iota(jnp.int32, (1, T), 1), prefix)
                key = j * T + lax.broadcasted_iota(jnp.int32, (T, T), 0)
                scores = jnp.where(key < limit, scores, masked_score)
            probs = jnp.exp(scores)
            gscores = (probs * mm(vb, db, NT)).astype(bf16)
            dv[h, ks, :] += mm(probs.astype(bf16), db, NN)
            dk[h, ks, :] += mm(gscores, qb, NN)
            dq[h, qs, :] += mm(gscores, kb, TN)

        def finish(b):
            rows = pl.ds(b * T, T)
            stack = jnp.concatenate(
                [dq[h, rows, :][:, :HD] * scale for h in range(heads)]
                + [dk[h, rows, :][:, :HD] for h in range(heads)]
                + [dv[h, rows, :][:, :HD] for h in range(heads)],
                axis=1,
            ).astype(bf16)
            gp[b] = stack
            n.part[b] = mm(stack, n.wq[...], NT).astype(bf16)
            s = flip(r, b)

            @pl.when(s == 3)
            def _():
                pr_copy(0, b).start()
                pr_copy(1, b).start()

            for link in range(2):

                @pl.when(s == link + 1)
                def _(link=link):
                    p_copy(link, link, b).start()

        def combine(b):
            s = flip(r, b)
            for link in range(2):

                @pl.when(s == link + 1)
                def _(link=link):
                    came = 1 - link
                    pr_copy(came, b).wait_recv()
                    piece = pl.ds(came * half, half)
                    total = n.part[b, piece, :].astype(f32) + n.prel[came].astype(f32)
                    n.part[b, piece, :] = total.astype(bf16)
                    p_copy(link, came, b).start()

        dq[...] = jnp.zeros_like(dq)
        dk[...] = jnp.zeros_like(dk)
        dv[...] = jnp.zeros_like(dv)
        early = R // 2
        for i in range(R - 1, early - 1, -1):
            spread(i)

            def plain_pair(t, carry, i=i):
                pair(t // i, i, lax.rem(t, i), False)
                return carry

            def diagonal(h, carry, i=i):
                pair(h, i, i, True)
                return carry

            lax.fori_loop(0, heads * i, plain_pair, 0)
            lax.fori_loop(0, heads, diagonal, 0)
            finish(i)
            if i + 1 < R:
                combine(i + 1)
        for i in range(early - 1, -1, -1):
            spread(i)
        row_sum(0)

        def square(t, carry):
            rest = lax.rem(t, early * early)
            pair(t // (early * early), rest // early, lax.rem(rest, early), True)
            return carry

        lax.fori_loop(0, heads * early * early, square, 0)
        for b in range(early - 1, -1, -1):
            finish(b)
        combine(early)
        row_sum(1)
        wrow_sum()

        qg[...] = jnp.zeros_like(qg)

        def qkv_step(b, carry):
            qg[...] += mm(n.one[b], gp[b], TN)
            return carry

        lax.fori_loop(0, R, qkv_step, 0)
        n.qgb[...] = qg[...].astype(bf16)

        def q_copy(t):
            to = col_at(t)
            return remote(n.qgb.at[rows_of(to)], n.qrecv.at[t - 1], sem["q"], t - 1, col=to)

        for t in peers:
            q_copy(t).start()
        for b in range(early - 1, -1, -1):
            combine(b)
        data_sum(0)
        for t in peers:
            q_copy(t).wait()
        total = n.qgb[cols, :].astype(f32)
        for t in peers:
            total = total + n.qrecv[t - 1].astype(f32)
        n.qblk[...] = total.astype(bf16)
        for s in groups:
            zz_copy(3, s).start()

    pl.run_scoped(
        back,
        pltpu.VMEM((heads, L, LANES), bf16), pltpu.VMEM((heads, L, LANES), f32), pltpu.VMEM((heads, L, LANES), f32),
        pltpu.VMEM((heads, L, LANES), f32), pltpu.VMEM((R, T, 3 * H), bf16), pltpu.VMEM((D, 3 * H), f32),
    )
    data_sum(1)
    data_sum(2)

    for link in range(2):
        for part in range(2):
            p_copy(link, part, 0).wait_recv()
    gain_sum = jnp.zeros((1, D), f32)
    bias_sum = jnp.zeros((1, D), f32)
    all_sum = jnp.zeros((1, D), f32)
    for piece in range(T // TR):
        rows = slice(piece * TR, (piece + 1) * TR)
        g = n.part[r, rows, :].astype(f32) + n.prec[0, rows, :].astype(f32) + n.prec[1, rows, :].astype(f32)
        centred, inverse = normalize(n.x[rows, :].astype(f32) + n.emb[0:1, :], D)
        total = n.tgrad[rows, :] + norm_back(g, centred, inverse, vec(0), D)
        n.tgrad[rows, :] = total
        gain_sum = gain_sum + jnp.sum(g * centred, axis=0, keepdims=True)
        bias_sum = bias_sum + jnp.sum(g, axis=0, keepdims=True)
        all_sum = all_sum + jnp.sum(total, axis=0, keepdims=True)

    n.vbuf[0:1, :] = gain_sum
    n.vbuf[1:2, :] = bias_sum
    n.vbuf[6:7, :] = all_sum
    n.vbuf[7:8, :] = jnp.zeros((1, D), f32)

    def v_copy(s):
        return remote(n.vbuf, n.vrow.at[s - 1], sem["v"], s - 1, row=flip(r, s))

    def vc_copy(t):
        return remote(n.vcol.at[c], n.vcol.at[c], sem["vc"], t - 1, col=col_at(t))

    def vz_copy(s):
        return remote(n.vcol, n.vz.at[s - 1], sem["vz"], s - 1, dp=lax.rem(z + s, Z))

    for s in others:
        v_copy(s).start()
    up_bias = n.ubg[r]
    for s in others:
        u_copy(s).wait_recv()
        up_bias = up_bias + n.urow[s - 1]
    for s in others:
        v_copy(s).wait_recv()
    total = n.vbuf[...]
    for s in others:
        total = total + n.vrow[s - 1]
    n.vcol[c, 0:8, :] = total
    n.vcol[c, 7:8, :] = up_bias
    n.vcol[c, 8:16, :] = jnp.full((8, D), n.stamp[0].astype(f32))
    for t in peers:
        vc_copy(t).start()
    for t in peers:
        vc_copy(t).wait_recv()
    for s in groups:
        vz_copy(s).start()
    data_sum(3)
    for s in groups:
        vz_copy(s).wait_recv()
    total = jnp.zeros((8, D), f32)
    number = (lax.broadcasted_iota(jnp.int32, (NTB, D), 0) + c * NTB).astype(f32)
    table = jnp.zeros((NTB, D), f32)
    for s in range(Z):
        for t in range(C):
            entry = n.vcol[t] if s == 0 else n.vz[s - 1, t]
            total = total + entry[0:8]
            table = table + jnp.where(number == entry[8:9], entry[6:7], 0.0)
    n.small[...] = total
    n.table_out[...] = table

    for t in peers:
        stamp_copy(t).wait_send()
        pick_copy(t).wait_send()
        w_copy(t).wait_send()
        vc_copy(t).wait_send()
        for s in range(R):
            woc_copy(s, t).wait_send()
            if s > 0:
                gc_copy(s, 0, t).wait_send()
                gc_copy(s, 1, t).wait_send()
    for link in range(2):
        relay_copy(link).wait_send()
        pr_copy(link, 0).wait_send()
        for part in range(2):
            n_copy(link, part).wait_send()
            p_copy(link, part, 0).wait_send()
    for s in others:
        for copy in (a_copy, g_copy, z_copy, wo_copy, ub_copy, a2_copy, wrow_copy, u_copy, v_copy):
            copy(s).wait_send()
        for kind in range(2):
            row_copy(s, kind).wait_send()
    for s in groups:
        vz_copy(s).wait_send()
        for kind in range(4):
            zz_copy(kind, s).wait_send()
            if split:
                y_copy(kind, s).wait()


def run_layer(C, Z, stamp, prefix, x, cot, table, vectors, w_qkv, w_out, w_up, w_down):
    T, D = x.shape
    DC, F = w_up.shape
    H = w_out.shape[1]
    heads = H // HD
    L = R * T
    NTB = table.shape[0]
    DZ = DC // Z if DC % (16 * Z) == 0 else DC
    vm = pltpu.VMEM
    ins = dict(stamp=SM, prefix=SM, x=VM, cot=VM, table=VM, vectors=VM, w_qkv=VM, w_out=VM, w_up=AN, w_down=AN)
    outs = dict(
        out=((T, D), bf16), tgrad=((T, D), f32), up_out=((DC, F), bf16), down_out=((DC, F), bf16),
        wo_out=((DC, H), bf16), qkv_out=((DC, 3 * H), bf16), small=((8, D), f32), table_out=((NTB, D), f32),
        wud=((2, R, D, F), bf16),
    )
    scratch = dict(
        stamp_own=vm((8, LANES), f32), stamp_got=vm((C - 1, 8, LANES), f32), picked=vm((C - 1, 8, D), f32),
        picked_got=vm((C - 1, 8, D), f32), emb=vm((8, D), f32), wq=vm((D, 3 * H), bf16), one=vm((R, T, D), bf16),
        q=vm((heads, L, LANES), bf16), k=vm((heads, L, LANES), bf16), v=vm((heads, L, LANES), bf16),
        mine=vm((R, T, H), bf16), att=vm((R, T, H), bf16), wo=vm((R, D, H), bf16),
        ub=vm((R, 8, F), f32), vbuf=vm((8, D), f32), ubg=vm((R, 1, F), f32),
        crecv=vm((R, C - 1, 2, DC, F), bf16), orecv=vm((C - 1, R, DC, H), bf16), gsend=vm((R, T, H), bf16),
        gatt=vm((R, T, H), bf16), grow=vm((R - 1, 2, DC, F), bf16), orow=vm((R - 1, DC, H), bf16),
        urow=vm((R - 1, 1, F), f32), part=vm((R, T, D), bf16), prec=vm((2, T, D), bf16), prel=vm((2, T // 2, D), bf16),
        qgb=vm((D, 3 * H), bf16), qrecv=vm((C - 1, DC, 3 * H), bf16), oblk=vm((DC, H), bf16), qblk=vm((DC, 3 * H), bf16),
        zr=vm((2, Z - 1, DZ, F), bf16), zro=vm((Z - 1, DZ, H), bf16), zrq=vm((Z - 1, DZ, 3 * H), bf16),
        vrow=vm((R - 1, 8, D), f32), vcol=vm((C, 16, D), f32), vz=vm((Z - 1, C, 16, D), f32),
    )
    sems = dict(
        stamp=C - 1, pick=C - 1, w=C - 1, n=4, relay=2, g=R - 1, gz=R - 1, gc=2 * R * (C - 1), wo=R - 1,
        woc=R * (C - 1), ub=R - 1, a=R - 1, a2=R - 1, row=2 * (R - 1), wrow=R - 1, u=R - 1, c=R * (C - 1), o=C - 1,
        z=4 * (Z - 1), y=4 * (Z - 1), p=4, pr=2, q=C - 1, v=R - 1, vc=C - 1, vz=Z - 1,
    )
    names = list(ins) + list(outs) + list(scratch) + ["sem_" + name for name in sems]
    dma = pltpu.SemaphoreType.DMA
    semaphores = []
    for count in sems.values():
        semaphores += [dma((count,)), dma((count,))]
    results = pl.pallas_call(
        functools.partial(layer_kernel, names, C, Z),
        out_shape=tuple(jax.ShapeDtypeStruct(*spec) for spec in outs.values()),
        in_specs=list(ins.values()),
        out_specs=(VM,) * (len(outs) - 1) + (AN,),
        scratch_shapes=list(scratch.values()) + semaphores + [dma((4,))],
        compiler_params=pltpu.CompilerParams(collective_id=0, has_side_effects=True, vmem_limit_bytes=67043328),
        name="layer",
    )(stamp, prefix, x, cot, table, vectors, w_qkv, w_out, w_up, w_down)
    return dict(zip(outs, results))


def body(C, Z, *args):
    (tokens, cotangent, timesteps, prefix_len, time_table, ln1_gain, ln1_bias, w_qkv, w_out, out_bias,
     ln2_gain, ln2_bias, w_up, up_bias, w_down, down_bias) = args
    DC, _, H = w_qkv.shape
    vectors = jnp.stack([ln1_gain, ln1_bias, out_bias, ln2_gain, ln2_bias, down_bias, up_bias, up_bias])
    o = run_layer(
        C, Z, timesteps, prefix_len, tokens[0], cotangent[0], time_table, vectors, w_qkv.reshape(DC, 3 * H), w_out,
        w_up, w_down,
    )
    small = o["small"]
    return (
        o["out"][None], o["tgrad"][None], o["table_out"], small[0], small[1],
        o["qkv_out"].astype(f32).reshape(DC, 3, H), o["wo_out"].astype(f32), small[2], small[3], small[4],
        o["up_out"].astype(f32), small[7], o["down_out"].astype(f32), small[5],
    )


def solution(mesh):
    C, Z = mesh.shape["col"], mesh.shape["dp"]
    batch = P(("dp", "col"), "row", None)
    block = P("col", "row")
    return jax.shard_map(
        functools.partial(body, C, Z),
        mesh=mesh,
        in_specs=(
            batch, batch, P(("dp", "col")), P(("dp", "col")), P("col", None), P(), P(), P("col", None, "row"), block,
            P(), P(), P(), block, P("row"), block, P(),
        ),
        out_specs=(
            batch, batch, P("col", None), P(), P(), P("col", None, "row"), block, P(), P(), P(), block, P("row"),
            block, P(),
        ),
        check_vma=False,
    )
```

```python
import functools
from types import SimpleNamespace

import jax
import jax.numpy as jnp
from jax import lax
from jax.experimental import pallas as pl
from jax.experimental.pallas import tpu as pltpu
from jax.sharding import PartitionSpec as P

HD = 64
LANES = 128
norm_eps = 1e-05
masked_score = -1e30
f32, bf16 = jnp.float32, jnp.bfloat16
MESH = pl.DeviceIdType.MESH
NN = (((1,), (0,)), ((), ()))
NT = (((1,), (1,)), ((), ()))
TN = (((0,), (0,)), ((), ()))
VM = pl.BlockSpec(memory_space=pltpu.VMEM)
SM = pl.BlockSpec(memory_space=pltpu.SMEM)
AN = pl.BlockSpec(memory_space=pl.ANY)
R = 4


def mm(a, b, dims):
    return lax.dot_general(a, b, dims, preferred_element_type=f32)


def remote(src, dst, sems, index, **where):
    return pltpu.make_async_remote_copy(
        src_ref=src, dst_ref=dst, send_sem=sems[0].at[index], recv_sem=sems[1].at[index],
        device_id=where, device_id_type=MESH,
    )


def flip(a, b):
    a0, b0, a1, b1 = lax.rem(a, 2), lax.rem(b, 2), a // 2, b // 2
    return a0 + b0 - 2 * a0 * b0 + 2 * (a1 + b1 - 2 * a1 * b1)


def greet(sizes):
    barrier = pltpu.get_barrier_semaphore()
    total = 0
    for name, count in sizes.items():
        for step in range(1, count):
            to = lax.rem(lax.axis_index(name) + step, count)
            pl.semaphore_signal(barrier, inc=1, device_id={name: to}, device_id_type=MESH)
            total += 1
    for s in range(1, sizes["dp"]):
        for t in range(1, sizes["col"]):
            to = {"dp": lax.rem(lax.axis_index("dp") + s, sizes["dp"]), "col": lax.rem(lax.axis_index("col") + t, sizes["col"])}
            pl.semaphore_signal(barrier, inc=1, device_id=to, device_id_type=MESH)
            total += 1
    pl.semaphore_wait(barrier, total)


def normalize(hidden, width):
    average = jnp.sum(hidden, axis=-1, keepdims=True) / width
    variance = jnp.sum(hidden * hidden, axis=-1, keepdims=True) / width - average * average
    inverse = lax.rsqrt(variance + norm_eps)
    return (hidden - average) * inverse, inverse


def norm_back(grad, centred, inverse, gain, width):
    scaled = grad * gain
    first = jnp.sum(scaled, axis=-1, keepdims=True) / width
    second = jnp.sum(scaled * centred, axis=-1, keepdims=True) / width
    return inverse * (scaled - first - centred * second)


def split_parts(value, lane, count):
    out = jnp.zeros(lane.shape, f32)
    for place in range(count):
        high = value.astype(bf16).astype(f32)
        out = jnp.where(lane == place, high, out)
        value = value - high
    return out.astype(bf16)


def layer_kernel(names, C, Z, *refs):
    n = SimpleNamespace(**dict(zip([name for name in names if not name.startswith("sem_")], refs)))
    plain = sum(1 for name in names if not name.startswith("sem_"))
    sem = {}
    place = plain
    for name in names:
        if name.startswith("sem_"):
            sem[name[4:]] = (refs[place], refs[place + 1])
            place += 2
    local = refs[place]
    r, c, z = lax.axis_index("row"), lax.axis_index("col"), lax.axis_index("dp")
    T, D = n.x.shape
    DC, F = n.w_up.shape
    H = n.w_out.shape[0]
    heads = H // HD
    L = R * T
    half = T // 2
    NTB = n.table.shape[0]
    parity = lax.rem(z, 2)
    zpair = z + 1 - 2 * parity
    nx, ny = flip(r, 1), flip(r, 2)
    cols = pl.ds(pl.multiple_of(c * DC, DC), DC)
    vec = lambda row: n.vectors[row : row + 1, :]
    given = (n.ln1_gain, n.ln1_bias, n.out_bias, n.ln2_gain, n.ln2_bias, n.down_bias, n.up_bias)
    for row, ref in enumerate(given):
        n.vectors[row : row + 1, :] = ref[...].reshape(1, D)
    others = range(1, R)
    peers = range(1, C)
    groups = range(1, Z)

    def col_at(t):
        return lax.rem(c + t, C)

    def lanes(value, device):
        return value[:, device * DC : (device + 1) * DC]

    def rows_of(device):
        return pl.ds(pl.multiple_of(device * DC, DC), DC)

    greet({"row": R, "col": C, "dp": Z})

    def wo_copy(s):
        piece = n.wo.at[r, c]
        return remote(n.w_out, piece, sem["wo"], s - 1, row=flip(r, s))

    def woc_copy(s, t):
        piece = n.wo.at[flip(r, s), c]
        source = n.w_out if s == 0 else piece
        return remote(source, piece, sem["woc"], s * (C - 1) + t - 1, col=col_at(t))

    def ub_copy(s):
        return remote(n.ub.at[r], n.ub.at[r], sem["ub"], s - 1, row=flip(r, s))

    n.ub[r] = jnp.broadcast_to(vec(6), (8, F))
    n.wo[r, c] = n.w_out[...]
    for s in others:
        wo_copy(s).start()
        ub_copy(s).start()
    for t in peers:
        woc_copy(0, t).start()

    def stamp_copy(t):
        return remote(n.stamp_own, n.stamp_got.at[t - 1], sem["stamp"], t - 1, col=col_at(t))

    def pick_copy(t):
        return remote(n.picked.at[t - 1], n.picked_got.at[t - 1], sem["pick"], t - 1, col=lax.rem(c - t + C, C))

    def w_copy(t):
        return remote(n.w_qkv, n.wq.at[c], sem["w"], t - 1, col=col_at(t))

    n.stamp_own[...] = jnp.full(n.stamp_own.shape, n.stamp[0].astype(f32))
    for t in peers:
        stamp_copy(t).start()
    for t in peers:
        w_copy(t).start()
    n.wq[c] = n.w_qkv[...]

    def row_of(stamps):
        number = (lax.broadcasted_iota(jnp.int32, (NTB, D), 0) + c * NTB).astype(f32)
        return jnp.sum(jnp.where(number == stamps, n.table[...].astype(f32), 0.0), axis=0, keepdims=True)

    for t in peers:
        stamp_copy(t).wait_recv()
        n.picked[t - 1] = jnp.broadcast_to(row_of(n.stamp_got[t - 1][0:1, 0:1]), (8, D))
        pick_copy(t).start()
    embed = row_of(n.stamp_own[0:1, 0:1])
    for t in peers:
        pick_copy(t).wait_recv()
        embed = embed + n.picked_got[t - 1][0:1]
    n.emb[...] = jnp.broadcast_to(embed, n.emb.shape)

    def n_copy(link, part):
        piece = n.one.at[r, pl.ds(part * half, half)]
        return remote(piece, piece, sem["n"], 2 * link + part, row=(nx, ny)[link])

    def relay_copy(link):
        piece = n.one.at[(ny, nx)[link], pl.ds(link * half, half)]
        return remote(piece, piece, sem["relay"], link, row=(nx, ny)[link])

    rows_ln = 128
    for part in range(2):

        def norm_step(t, carry, part=part):
            rows = pl.ds(pl.multiple_of(part * half + t * rows_ln, rows_ln), rows_ln)
            centred, inverse = normalize(n.x[rows, :].astype(f32) + n.emb[0:1, :], D)
            n.one[r, rows, :] = (centred * vec(0) + vec(1)).astype(bf16)
            return carry

        lax.fori_loop(0, half // rows_ln, norm_step, 0)
        n_copy(1 - part, part).start()
    n_copy(0, 0).start()
    n_copy(1, 1).start()

    for t in peers:
        w_copy(t).wait_recv()
    lane = lax.broadcasted_iota(jnp.int32, (T, HD), 1)
    q_tail = jnp.zeros((T, HD), bf16)
    k_tail = jnp.where(lane < 3, 1.0, 0.0).astype(bf16)
    v_tail = jnp.where(lane < 2, 1.0, 0.0).astype(bf16)
    scale = HD ** (-0.5)

    def project(s, carry):
        @pl.when(s == 1)
        def _():
            n_copy(1, 0).wait_recv()
            relay_copy(0).start()
            n_copy(0, 1).wait_recv()
            relay_copy(1).start()
            n_copy(0, 0).wait_recv()

        @pl.when(s == 2)
        def _():
            n_copy(1, 1).wait_recv()

        @pl.when(s == 3)
        def _():
            relay_copy(0).wait_recv()
            relay_copy(1).wait_recv()
            weights_start()

        block = flip(r, s)
        normed = n.one[block]
        y = mm(lanes(normed, 0), n.wq[0], NT)
        for device in range(1, C):
            y += mm(lanes(normed, device), n.wq[device], NT)
        y = y.astype(bf16)
        rows = pl.ds(pl.multiple_of(block * T, T), T)
        for h in range(heads):
            n.q[h, rows, :] = jnp.concatenate([y[:, h * HD : (h + 1) * HD] * scale, q_tail], axis=1)
            n.k[h, rows, :] = jnp.concatenate([y[:, H + h * HD : H + (h + 1) * HD], k_tail], axis=1)
            n.v[h, rows, :] = jnp.concatenate([y[:, 2 * H + h * HD : 2 * H + (h + 1) * HD], v_tail], axis=1)
        return carry

    ups = (n.w_up, n.w_down)

    def half_copy(s, kind):
        return remote(ups[kind], n.wud.at[kind, r, cols], sem["g"], s - 1, row=flip(r, s))

    def z_copy(s):
        piece = n.wud.at[parity, flip(r, s), cols]
        return remote(piece, piece, sem["gz"], s - 1, dp=zpair)

    def gc_copy(s, kind, t):
        piece = n.wud.at[kind, flip(r, s), cols]
        source = ups[kind] if s == 0 else piece
        return remote(source, piece, sem["gc"], (2 * s + kind) * (C - 1) + t - 1, col=col_at(t))

    def gc_half(s, second, t):
        piece = n.wud.at[1 - parity if second else parity, flip(r, s), cols]
        return remote(piece, piece, sem["gc"], (2 * s + second) * (C - 1) + t - 1, col=col_at(t))

    def half_start(s):
        for kind in range(2):

            @pl.when(parity == kind)
            def _(kind=kind):
                half_copy(s, kind).start()

    def half_on(s):
        half_copy(s, 0).wait_recv()
        z_copy(s).start()
        for t in peers:
            gc_half(s, 0, t).start()

    def weights_start():
        half_start(3)

    for t in peers:
        for kind in range(2):
            gc_copy(0, kind, t).start()

    lax.fori_loop(0, R, project, 0)

    prefix = n.prefix[0]
    longest = L // 2
    SB = min(256, T)
    nsub = T // SB
    lane_sb = lax.broadcasted_iota(jnp.int32, (SB, HD), 1)

    def a_copy(s):
        i = flip(r, s)
        return remote(n.mine.at[i], n.att.at[r], sem["a"], s - 1, row=i)

    def attend_block(step, carry):
        s = lax.rem(step + 1, R)
        i = flip(r, s)
        for static in range(R):
            early = (static + 1) * T <= longest
            nk = longest if early else (static + 1) * T
            nm = nk if early else T

            def attend(t, inner, nk=nk, nm=nm):
                h = t // nsub
                sub = pl.multiple_of(lax.rem(t, nsub) * SB, SB)
                row = i * T + sub
                rows = pl.ds(pl.multiple_of(row, SB), SB)
                scores = mm(n.q[h, rows, :], n.k[h, :nk, :], NT)
                limit = jnp.maximum(row + 1 + lax.broadcasted_iota(jnp.int32, (SB, 1), 0), prefix)
                key = (nk - nm) + lax.broadcasted_iota(jnp.int32, (SB, nm), 1)
                last = jnp.where(key < limit, scores[:, nk - nm :], masked_score)
                top = jnp.max(last, axis=1, keepdims=True)
                if nk > nm:
                    top = jnp.maximum(top, jnp.max(scores[:, : nk - nm], axis=1, keepdims=True))
                mixed = mm(jnp.exp(last - top).astype(bf16), n.v[h, nk - nm : nk, :], NN)
                if nk > nm:
                    mixed += mm(jnp.exp(scores[:, : nk - nm] - top).astype(bf16), n.v[h, : nk - nm, :], NN)
                weight = mixed[:, HD : HD + 1]
                n.mixed[h, pl.ds(sub, SB), :] = mixed / weight
                n.q[h, rows, HD:] = split_parts(-(top + jnp.log(weight)), lane_sb, 3)
                return inner

            @pl.when(i == static)
            def _(attend=attend):
                lax.fori_loop(0, heads * nsub, attend, 0)

        n.mine[i] = jnp.concatenate([n.mixed[h][:, :HD] for h in range(heads)], axis=1).astype(bf16)

        for at in range(R - 1):

            @pl.when(step == at)
            def _(at=at):
                a_copy(at + 1).start()
                if at == 0:
                    for s in others:
                        wo_copy(s).wait_recv()
                        for t in peers:
                            woc_copy(s, t).start()
                    half_start(1)
                    half_start(2)
                if at == 2:
                    half_on(3)

        return carry

    def attend_all(mixed_ref):
        n.mixed = mixed_ref
        lax.fori_loop(0, R, attend_block, 0)

    pl.run_scoped(attend_all, pltpu.VMEM((heads, T, LANES), f32))
    n.att[r] = n.mine[r]
    half_on(1)

    TR = min(256, T)
    TF = 384 if F % 384 == 0 else F
    tiles = F // TF
    ticks = R * tiles

    def turn(k):
        return lax.rem(156 // ((1 + 3 * lax.rem(k, 2)) * (1 + 15 * (k // 2))), R)

    def a2_copy(s):
        b = flip(r, s)
        return remote(n.gsend.at[b], n.gatt.at[r], sem["a2"], s - 1, row=b)

    z_first = n.grow.shape[1] == 1
    row_kinds = (0,) if z_first else (0, 1)

    def row_copy(s, kind):
        return remote(n.crecv.at[s, 0, kind], n.grow.at[s - 1, kind], sem["row"], 2 * (s - 1) + kind, row=flip(r, s))

    def b_part(device):
        height = n.bsum.shape[1]
        return pl.ds(pl.multiple_of(device * height, height), height)

    def b_copy(s, g):
        to = lax.rem(z + g, Z)
        return remote(n.crecv.at[s, 0, 1, b_part(to)], n.bz.at[s, g - 1], sem["b"], s * (Z - 1) + g - 1, dp=to)

    def br_copy(s):
        return remote(n.bsum.at[s], n.brow.at[s - 1], sem["br"], s - 1, row=flip(r, s))

    def b_sum(s):
        if not z_first:
            return
        for g in groups:
            b_copy(s, g).wait_recv()
        total = n.crecv[s, 0, 1, b_part(z), :].astype(f32)
        for g in groups:
            total = total + n.bz[s, g - 1].astype(f32)
        n.bsum[s] = total.astype(bf16)
        if s > 0:
            br_copy(s).start()

    def wrow_copy(s):
        b = flip(r, s)
        return remote(n.orecv.at[0, b], n.orow.at[s - 1], sem["wrow"], s - 1, row=b)

    def u_copy(s):
        return remote(n.ubg.at[flip(r, s)], n.urow.at[s - 1], sem["u"], s - 1, row=flip(r, s))

    def middle(wbuf, acc, gn, n2, n2t, cott, gbuf, obuf):
        def fetch(tick):
            fcols = pl.ds(pl.multiple_of(lax.rem(tick, tiles) * TF, TF), TF)
            slot = lax.rem(tick, 2)
            return pltpu.make_async_copy(
                n.wud.at[:, flip(r, turn(tick // tiles)), :, fcols], wbuf.at[slot], local.at[slot]
            )

        def fetch_start(tick):
            own = turn(tick // tiles) == 0

            @pl.when(jnp.logical_not(own))
            def _():
                fetch(tick).start()

            @pl.when(own)
            def _():
                fcols = pl.ds(pl.multiple_of(lax.rem(tick, tiles) * TF, TF), TF)
                slot = lax.rem(tick, 2)
                for kind in range(2):
                    source = (n.w_up, n.w_down)[kind].at[:, fcols]
                    pltpu.make_async_copy(source, wbuf.at[slot, kind, cols], local.at[slot]).start()
                    for p in peers:
                        rows = rows_of(col_at(p))
                        pltpu.make_async_copy(
                            n.wud.at[kind, r, rows, fcols], wbuf.at[slot, kind, rows], local.at[slot]
                        ).start()

        def c_copy(k, t):
            to = col_at(t)
            return remote(
                gbuf.at[lax.rem(k, 2), :, rows_of(to)], n.crecv.at[turn(k), t - 1], sem["c"], k * (C - 1) + t - 1,
                col=to,
            )

        def o_copy(t):
            to = col_at(t)
            return remote(obuf.at[:, to], n.orecv.at[t - 1], sem["o"], t - 1, col=to)

        def join(k):
            s = turn(k)
            for t in peers:
                c_copy(k, t).wait_recv()
            for kind in range(2):
                total = gbuf[lax.rem(k, 2), kind, cols, :].astype(f32)
                for t in peers:
                    total = total + n.crecv[s, t - 1, kind].astype(f32)
                n.crecv[s, 0, kind] = total.astype(bf16)

            if z_first:
                for g in groups:
                    b_copy(s, g).start()

            @pl.when(s > 0)
            def _():
                u_copy(s).start()
                for kind in row_kinds:
                    row_copy(s, kind).start()

        for p in peers:
            for kind in range(2):
                gc_copy(0, kind, p).wait()
        fetch_start(0)
        cott[...] = n.cot[...].T
        for s in others:
            for t in peers:
                woc_copy(s, t).wait_recv()
        for t in peers:
            woc_copy(0, t).wait_recv()
        for s in others:
            ub_copy(s).wait_recv()
            a_copy(s).wait_recv()
        vsum = jnp.zeros((1, D), f32)
        for part in range(T // TR):
            rows = slice(part * TR, (part + 1) * TR)
            branch = []
            for device in range(C):
                piece = mm(n.att[0, rows, :], n.wo[0, device], NN)
                for b in range(1, R):
                    piece += mm(n.att[b, rows, :], n.wo[b, device], NN)
                branch.append(piece)
            branch = jnp.concatenate(branch, axis=1)
            hidden = n.x[rows, :].astype(f32) + n.emb[0:1, :] + branch + vec(2)
            n.tgrad[rows, :] = hidden
            centred, inverse = normalize(hidden, D)
            n2[rows, :] = (centred * vec(3) + vec(4)).astype(bf16)
            acc[rows, :] = jnp.zeros((TR, D), f32)
            gn[rows, :] = jnp.zeros((TR, D), f32)
            vsum = vsum + jnp.sum(n.cot[rows, :].astype(f32), axis=0, keepdims=True)
        n2t[...] = n2[...].T
        n.vbuf[5:6, :] = vsum

        def second_half(s):
            z_copy(s).wait_recv()
            for p in peers:
                gc_half(s, 1, p).start()

        def arrived(s):
            for p in peers:
                for kind in range(2):
                    gc_copy(s, kind, p).wait_recv()

        def tick_step(tick, carry):
            k, t = tick // tiles, lax.rem(tick, tiles)
            b = flip(r, turn(k))
            slot, wslot = lax.rem(k, 2), lax.rem(tick, 2)
            fetch(tick).wait()

            @pl.when((t == 0) & (k >= 2))
            def _():
                for p in peers:
                    c_copy(k - 2, p).wait_send()

            @pl.when(tick == 0)
            def _():
                half_on(2)

            @pl.when(tick == tiles - 1)
            def _():
                second_half(3)
                arrived(3)

            @pl.when((t < tiles - 1) | (k == 0))
            def _():
                fetch_start(tick + 1)

            fcols = pl.ds(pl.multiple_of(t * TF, TF), TF)
            wu = wbuf[wslot, 0]
            wd = wbuf[wslot, 1]
            inner = mm(n2[...], wu, NN) + n.ub[b, 0:1, fcols]
            cdf = 0.5 * (1.0 + lax.erf(inner * 0.7071067811865476))
            slope = cdf + inner * (jnp.exp(-0.5 * inner * inner) * 0.3989422804014327)
            active = (inner * cdf).astype(bf16)
            acc[...] += mm(active, wd, NT)
            ginner = mm(n.cot[...], wd, NN) * slope
            glow = ginner.astype(bf16)
            gn[...] += mm(glow, wu, NT)
            gbuf[slot, 1, :, fcols] = mm(cott[...], active, NN).astype(bf16)
            gbuf[slot, 0, :, fcols] = mm(n2t[...], glow, NN).astype(bf16)
            n.ubg[b, :, fcols] = jnp.sum(ginner, axis=0, keepdims=True)

            @pl.when(t == tiles - 1)
            def _():
                for p in peers:
                    c_copy(k, p).start()

                for near, turn_before in ((1, 1), (2, 2)):

                    @pl.when(k == turn_before)
                    def _(near=near):
                        second_half(near)
                        arrived(near)
                        fetch_start(tick + 1)

            @pl.when((t == 0) & (k > 0))
            def _():
                join(k - 1)

            return carry

        lax.fori_loop(0, ticks, tick_step, 0)

        gain_sum = jnp.zeros((1, D), f32)
        bias_sum = jnp.zeros((1, D), f32)
        hid_sum = jnp.zeros((1, D), f32)
        for part in range(T // TR):
            rows = slice(part * TR, (part + 1) * TR)
            hidden = n.tgrad[rows, :]
            n.out[rows, :] = (hidden + acc[rows, :] + vec(5)).astype(bf16)
            centred, inverse = normalize(hidden, D)
            g = gn[rows, :]
            gh = n.cot[rows, :].astype(f32) + norm_back(g, centred, inverse, vec(3), D)
            n.tgrad[rows, :] = gh
            n2[rows, :] = gh.astype(bf16)
            gain_sum = gain_sum + jnp.sum(g * centred, axis=0, keepdims=True)
            bias_sum = bias_sum + jnp.sum(g, axis=0, keepdims=True)
            hid_sum = hid_sum + jnp.sum(gh, axis=0, keepdims=True)
        n.vbuf[2:3, :] = hid_sum
        n.vbuf[3:4, :] = gain_sum
        n.vbuf[4:5, :] = bias_sum

        def back_step(at, carry):
            s = R - 1 - at
            b = flip(r, s)
            grad = n2[...]
            back = mm(lanes(grad, 0), n.wo[b, 0], NT)
            for device in range(1, C):
                back += mm(lanes(grad, device), n.wo[b, device], NT)
            n.gsend[b] = back.astype(bf16)

            @pl.when(s > 0)
            def _():
                a2_copy(s).start()

            return carry

        lax.fori_loop(0, R, back_step, 0)
        n.gatt[r] = n.gsend[r]
        join(R - 1)

        def out_step(b, carry):
            block = mm(n.att[b], n2[...], TN).astype(bf16)
            for device in range(C):
                obuf[b, device] = lanes(block, device)
            return carry

        lax.fori_loop(0, R, out_step, 0)
        for t in peers:
            o_copy(t).start()
        for t in peers:
            o_copy(t).wait_recv()
        for b in range(R):
            total = obuf[b, c].astype(f32)
            for t in peers:
                total = total + n.orecv[t - 1, b].astype(f32)
            n.orecv[0, b] = total.astype(bf16)
        for s in others:
            wrow_copy(s).start()
        for t in peers:
            o_copy(t).wait_send()
            for s in range(R - 2, R):
                c_copy(s, t).wait_send()

    dt = bf16
    pl.run_scoped(
        middle,
        pltpu.VMEM((2, 2, D, TF), dt), pltpu.VMEM((T, D), f32), pltpu.VMEM((T, D), f32), pltpu.VMEM((T, D), dt),
        pltpu.VMEM((D, T), dt), pltpu.VMEM((D, T), dt), pltpu.VMEM((2, 2, D, F), dt), pltpu.VMEM((R, C, H, DC), dt),
    )

    sources = (n.crecv.at[0, 0, 0], n.crecv.at[0, 0, 1], n.oblk, n.qblk)
    landing = (n.zr.at[0], n.zr.at[n.zr.shape[0] - 1], n.zro, n.zrq)
    finals = (n.up_out, n.down_out, n.wo_out, n.qkv_out)

    heights = (DC, DC, H, 3 * H)
    split = [landing[kind].shape[1] != heights[kind] for kind in range(4)]
    def part_of(kind, device):
        height = landing[kind].shape[1]
        return pl.ds(pl.multiple_of(device * height, height), height) if split[kind] else slice(None)

    def zz_copy(kind, s):
        to = lax.rem(z + s, Z)
        return remote(sources[kind].at[part_of(kind, to)], landing[kind].at[s - 1], sem["z"], kind * (Z - 1) + s - 1, dp=to)

    def y_copy(kind, s):
        piece = finals[kind].at[part_of(kind, z)]
        return remote(piece, piece, sem["y"], kind * (Z - 1) + s - 1, dp=lax.rem(z + s, Z))

    def z_start(kind):
        for s in groups:
            zz_copy(kind, s).start()

    def z_end(kind):
        for s in groups:
            zz_copy(kind, s).wait_recv()
        total = sources[kind][part_of(kind, z), :].astype(f32)
        for s in groups:
            total = total + landing[kind][s - 1].astype(f32)
        finals[kind][part_of(kind, z), :] = total.astype(bf16)
        if split[kind]:
            for s in groups:
                y_copy(kind, s).start()

    def down_end():
        if not z_first:
            z_end(1)
            return
        total = n.bsum[0].astype(f32)
        for s in others:
            br_copy(s).wait_recv()
            total = total + n.brow[s - 1].astype(f32)
        finals[1][b_part(z), :] = total.astype(bf16)
        for s in groups:
            y_copy(1, s).start()

    def z_finish(kind):
        for s in groups:
            if kind != 1 or not z_first:
                zz_copy(kind, s).wait_send()
            if split[kind]:
                y_copy(kind, s).wait()

    def row_sum(kind):
        total = n.crecv[0, 0, kind].astype(f32)
        for s in others:
            row_copy(s, kind).wait_recv()
            total = total + n.grow[s - 1, kind].astype(f32)
        n.crecv[0, 0, kind] = total.astype(bf16)
        z_start(kind)

    def wrow_sum():
        for s in others:
            wrow_copy(s).wait_recv()
        total = n.orecv[0, r].astype(f32)
        for s in others:
            total = total + n.orow[s - 1].astype(f32)
        n.oblk[...] = total.astype(bf16)
        z_start(2)

    def p_copy(link, part, b):
        piece = pl.ds(part * half, half)
        return remote(n.part.at[b, piece], n.prec.at[link, piece], sem["p"], 2 * link + part, row=(nx, ny)[link])

    def pr_copy(link, b):
        return remote(n.part.at[b, pl.ds(link * half, half)], n.prel.at[link], sem["pr"], link, row=(nx, ny)[link])

    def back(d, dq, dk, dv, gp, qg):
        def spread(b):
            rows = pl.ds(b * T, T)

            @pl.when(r != b)
            def _():
                s = flip(r, b)
                remote(n.gsend.at[b], n.gatt.at[b], sem["a2"], s - 1, row=b).wait_recv()

            ga = n.gatt[b]
            both = ga.astype(f32) * n.mine[b].astype(f32)
            for h in range(heads):
                piece = slice(h * HD, (h + 1) * HD)
                delta = jnp.sum(both[:, piece], axis=1, keepdims=True)
                d[h, rows, :] = jnp.concatenate([ga[:, piece], split_parts(-delta, lane, 2)], axis=1)

        def pair(h, i, j, masked):
            qs = pl.ds(pl.multiple_of(i * T, T), T)
            ks = pl.ds(pl.multiple_of(j * T, T), T)
            qb, kb, vb, db = n.q[h, qs, :], n.k[h, ks, :], n.v[h, ks, :], d[h, qs, :]
            scores = mm(kb, qb, NT)
            if masked:
                limit = jnp.maximum(i * T + 1 + lax.broadcasted_iota(jnp.int32, (1, T), 1), prefix)
                key = j * T + lax.broadcasted_iota(jnp.int32, (T, T), 0)
                scores = jnp.where(key < limit, scores, masked_score)
            probs = jnp.exp(scores)
            gscores = (probs * mm(vb, db, NT)).astype(bf16)
            dv[h, ks, :] += mm(probs.astype(bf16), db, NN)
            dk[h, ks, :] += mm(gscores, qb, NN)
            dq[h, qs, :] += mm(gscores, kb, TN)

        def finish(b):
            rows = pl.ds(b * T, T)
            stack = jnp.concatenate(
                [dq[h, rows, :][:, :HD] * scale for h in range(heads)]
                + [dk[h, rows, :][:, :HD] for h in range(heads)]
                + [dv[h, rows, :][:, :HD] for h in range(heads)],
                axis=1,
            ).astype(bf16)
            gp[b] = stack
            n.part[b] = jnp.concatenate(
                [mm(stack, n.wq[device], NN).astype(bf16) for device in range(C)], axis=1
            )
            s = flip(r, b)

            @pl.when(s == 3)
            def _():
                pr_copy(0, b).start()
                pr_copy(1, b).start()

            for link in range(2):

                @pl.when(s == link + 1)
                def _(link=link):
                    p_copy(link, link, b).start()

        def combine(b):
            s = flip(r, b)
            for link in range(2):

                @pl.when(s == link + 1)
                def _(link=link):
                    came = 1 - link
                    pr_copy(came, b).wait_recv()
                    piece = pl.ds(came * half, half)
                    total = n.part[b, piece, :].astype(f32) + n.prel[came].astype(f32)
                    n.part[b, piece, :] = total.astype(bf16)
                    p_copy(link, came, b).start()

        dq[...] = jnp.zeros_like(dq)
        dk[...] = jnp.zeros_like(dk)
        dv[...] = jnp.zeros_like(dv)
        early = R // 2
        for i in range(R - 1, early - 1, -1):
            spread(i)

            def plain_pair(t, carry, i=i):
                pair(t // i, i, lax.rem(t, i), False)
                return carry

            def diagonal(h, carry, i=i):
                pair(h, i, i, True)
                return carry

            lax.fori_loop(0, heads * i, plain_pair, 0)
            lax.fori_loop(0, heads, diagonal, 0)
            finish(i)
            if i + 1 < R:
                combine(i + 1)
            else:
                b_sum(0)
                b_sum(3)
                b_sum(1)
        for i in range(early - 1, -1, -1):
            spread(i)
        b_sum(2)
        row_sum(0)

        def square(t, carry):
            rest = lax.rem(t, early * early)
            pair(t // (early * early), rest // early, lax.rem(rest, early), True)
            return carry

        total = heads * early * early
        lax.fori_loop(0, total // 2, square, 0)
        if not z_first:
            row_sum(1)
        wrow_sum()
        lax.fori_loop(total // 2, total, square, 0)
        down_end()
        for b in range(early - 1, -1, -1):
            finish(b)
        combine(early)

        qg[...] = jnp.zeros_like(qg)

        def qkv_step(b, carry):
            qg[...] += mm(gp[b], n.one[b], TN)
            return carry

        lax.fori_loop(0, R, qkv_step, 0)
        for device in range(C):
            n.wq[device] = lanes(qg, device).astype(bf16)

        def q_copy(t):
            to = col_at(t)
            return remote(n.wq.at[to], n.qrecv.at[t - 1], sem["q"], t - 1, col=to)

        for t in peers:
            q_copy(t).start()
        for b in range(early - 1, -1, -1):
            combine(b)
        z_end(0)
        z_end(2)
        for t in peers:
            q_copy(t).wait()
        total = n.wq[c].astype(f32)
        for t in peers:
            total = total + n.qrecv[t - 1].astype(f32)
        n.qblk[...] = total.astype(bf16)
        z_start(3)

    pl.run_scoped(
        back,
        pltpu.VMEM((heads, L, LANES), bf16), pltpu.VMEM((heads, L, LANES), f32), pltpu.VMEM((heads, L, LANES), f32),
        pltpu.VMEM((heads, L, LANES), f32), pltpu.VMEM((R, T, 3 * H), bf16), pltpu.VMEM((3 * H, D), f32),
    )

    for link in range(2):
        for part in range(2):
            p_copy(link, part, 0).wait_recv()
    gain_sum = jnp.zeros((1, D), f32)
    bias_sum = jnp.zeros((1, D), f32)
    all_sum = jnp.zeros((1, D), f32)
    for piece in range(T // TR):
        rows = slice(piece * TR, (piece + 1) * TR)
        g = n.part[r, rows, :].astype(f32) + n.prec[0, rows, :].astype(f32) + n.prec[1, rows, :].astype(f32)
        centred, inverse = normalize(n.x[rows, :].astype(f32) + n.emb[0:1, :], D)
        total = n.tgrad[rows, :] + norm_back(g, centred, inverse, vec(0), D)
        n.tgrad[rows, :] = total
        gain_sum = gain_sum + jnp.sum(g * centred, axis=0, keepdims=True)
        bias_sum = bias_sum + jnp.sum(g, axis=0, keepdims=True)
        all_sum = all_sum + jnp.sum(total, axis=0, keepdims=True)

    n.vbuf[0:1, :] = gain_sum
    n.vbuf[1:2, :] = bias_sum
    n.vbuf[6:7, :] = all_sum
    n.vbuf[7:8, :] = jnp.zeros((1, D), f32)

    def v_copy(s):
        return remote(n.vbuf, n.vrow.at[s - 1], sem["v"], s - 1, row=flip(r, s))

    def all_copy(s, t):
        piece = n.vall.at[z, c]
        return remote(piece, piece, sem["vz"], s * C + t - 1, dp=lax.rem(z + s, Z), col=col_at(t))

    rest = [(s, t) for s in range(Z) for t in range(C) if s + t > 0]
    for s in others:
        v_copy(s).start()
    up_bias = n.ubg[r]
    for s in others:
        u_copy(s).wait_recv()
        up_bias = up_bias + n.urow[s - 1]
    for s in others:
        v_copy(s).wait_recv()
    total = n.vbuf[...]
    for s in others:
        total = total + n.vrow[s - 1]
    n.vall[z, c, 0:8, :] = total
    n.vall[z, c, 7:8, :] = up_bias
    n.vall[z, c, 8:16, :] = jnp.full((8, D), n.stamp[0].astype(f32))
    for s, t in rest:
        all_copy(s, t).start()
    z_end(3)
    for s, t in rest:
        all_copy(s, t).wait_recv()
    total = jnp.zeros((8, D), f32)
    number = (lax.broadcasted_iota(jnp.int32, (NTB, D), 0) + c * NTB).astype(f32)
    table = jnp.zeros((NTB, D), f32)
    for s in range(Z):
        for t in range(C):
            total = total + n.vall[s, t, 0:8, :]
            table = table + jnp.where(number == n.vall[s, t, 8:9, :], n.vall[s, t, 6:7, :], 0.0)
    n.small[...] = total
    n.table_out[...] = table

    for t in peers:
        stamp_copy(t).wait_send()
        pick_copy(t).wait_send()
        w_copy(t).wait_send()
        for s in range(R):
            woc_copy(s, t).wait_send()
            if s > 0:
                gc_copy(s, 0, t).wait_send()
                gc_copy(s, 1, t).wait_send()
    for link in range(2):
        relay_copy(link).wait_send()
        pr_copy(link, 0).wait_send()
        for part in range(2):
            n_copy(link, part).wait_send()
            p_copy(link, part, 0).wait_send()
    for s in others:
        half_copy(s, 0).wait_send()
        for copy in (a_copy, z_copy, wo_copy, ub_copy, a2_copy, wrow_copy, u_copy, v_copy):
            copy(s).wait_send()
        for kind in row_kinds:
            row_copy(s, kind).wait_send()
        if z_first:
            br_copy(s).wait_send()
    if z_first:
        for s in range(R):
            for g in groups:
                b_copy(s, g).wait_send()
    for s, t in rest:
        all_copy(s, t).wait_send()
    for kind in range(4):
        z_finish(kind)


def run_layer(C, Z, stamp, prefix, x, cot, table, vectors, w_qkv, w_out, w_up, w_down):
    T, D = x.shape
    DC, F = w_up.shape
    H = w_out.shape[0]
    heads = H // HD
    L = R * T
    NTB = table.shape[0]
    part = lambda height: height // Z if height % (16 * Z) == 0 else height
    kinds, rows_b = (1, DC // Z) if DC % (16 * Z) == 0 else (2, 16)
    vm = pltpu.VMEM
    given = ("ln1_gain", "ln1_bias", "out_bias", "ln2_gain", "ln2_bias", "down_bias", "up_bias")
    ins = dict(stamp=SM, prefix=SM, x=VM, cot=VM, table=VM, **{name: VM for name in given}, w_qkv=VM, w_out=VM, w_up=AN, w_down=AN)
    outs = dict(
        out=((T, D), bf16), tgrad=((T, D), f32), up_out=((DC, F), bf16), down_out=((DC, F), bf16),
        wo_out=((H, DC), bf16), qkv_out=((3 * H, DC), bf16), small=((8, D), f32), table_out=((NTB, D), f32),
        wud=((2, R, D, F), bf16),
    )
    scratch = dict(
        stamp_own=vm((8, LANES), f32), stamp_got=vm((C - 1, 8, LANES), f32), picked=vm((C - 1, 8, D), f32),
        picked_got=vm((C - 1, 8, D), f32), emb=vm((8, D), f32), vectors=vm((8, D), f32), wq=vm((C, 3 * H, DC), bf16), one=vm((R, T, D), bf16),
        q=vm((heads, L, LANES), bf16), k=vm((heads, L, LANES), bf16), v=vm((heads, L, LANES), bf16),
        mine=vm((R, T, H), bf16), att=vm((R, T, H), bf16), wo=vm((R, C, H, DC), bf16),
        ub=vm((R, 8, F), f32), vbuf=vm((8, D), f32), ubg=vm((R, 1, F), f32),
        crecv=vm((R, C - 1, 2, DC, F), bf16), orecv=vm((C - 1, R, H, DC), bf16), gsend=vm((R, T, H), bf16),
        gatt=vm((R, T, H), bf16), grow=vm((R - 1, kinds, DC, F), bf16), orow=vm((R - 1, H, DC), bf16),
        urow=vm((R - 1, 1, F), f32), bz=vm((R, Z - 1, rows_b, F), bf16), bsum=vm((R, rows_b, F), bf16), brow=vm((R - 1, rows_b, F), bf16), part=vm((R, T, D), bf16), prec=vm((2, T, D), bf16), prel=vm((2, T // 2, D), bf16),
        qrecv=vm((C - 1, 3 * H, DC), bf16), oblk=vm((H, DC), bf16), qblk=vm((3 * H, DC), bf16),
        zr=vm((kinds, Z - 1, part(DC), F), bf16), zro=vm((Z - 1, part(H), DC), bf16), zrq=vm((Z - 1, part(3 * H), DC), bf16),
        vrow=vm((R - 1, 8, D), f32), vall=vm((Z, C, 16, D), f32),
    )
    sems = dict(
        stamp=C - 1, pick=C - 1, w=C - 1, n=4, relay=2, g=R - 1, gz=R - 1, b=R * (Z - 1), br=R - 1, gc=2 * R * (C - 1), wo=R - 1,
        woc=R * (C - 1), ub=R - 1, a=R - 1, a2=R - 1, row=2 * (R - 1), wrow=R - 1, u=R - 1, c=R * (C - 1), o=C - 1,
        z=4 * (Z - 1), y=4 * (Z - 1), p=4, pr=2, q=C - 1, v=R - 1, vz=Z * C - 1,
    )
    names = list(ins) + list(outs) + list(scratch) + ["sem_" + name for name in sems]
    dma = pltpu.SemaphoreType.DMA
    semaphores = []
    for count in sems.values():
        semaphores += [dma((count,)), dma((count,))]
    results = pl.pallas_call(
        functools.partial(layer_kernel, names, C, Z),
        out_shape=tuple(jax.ShapeDtypeStruct(*spec) for spec in outs.values()),
        in_specs=list(ins.values()),
        out_specs=(VM,) * (len(outs) - 1) + (AN,),
        scratch_shapes=list(scratch.values()) + semaphores + [dma((2,))],
        compiler_params=pltpu.CompilerParams(collective_id=0, has_side_effects=True, vmem_limit_bytes=67043328),
        name="layer",
    )(stamp, prefix, x, cot, table, *vectors, w_qkv, w_out, w_up, w_down)
    return dict(zip(outs, results))


def body(C, Z, *args):
    (tokens, cotangent, timesteps, prefix_len, time_table, ln1_gain, ln1_bias, w_qkv, w_out, out_bias,
     ln2_gain, ln2_bias, w_up, up_bias, w_down, down_bias) = args
    DC, _, H = w_qkv.shape
    vectors = (ln1_gain, ln1_bias, out_bias, ln2_gain, ln2_bias, down_bias, up_bias)
    o = run_layer(
        C, Z, timesteps, prefix_len, tokens[0], cotangent[0], time_table, vectors,
        w_qkv.transpose(1, 2, 0).reshape(3 * H, DC), w_out.T, w_up, w_down,
    )
    small = o["small"]
    return (
        o["out"][None], o["tgrad"][None], o["table_out"], small[0], small[1],
        o["qkv_out"].astype(f32).reshape(3, H, DC).transpose(2, 0, 1), o["wo_out"].astype(f32).T, small[2], small[3], small[4],
        o["up_out"].astype(f32), small[7], o["down_out"].astype(f32), small[5],
    )


def solution(mesh):
    C, Z = mesh.shape["col"], mesh.shape["dp"]
    batch = P(("dp", "col"), "row", None)
    block = P("col", "row")
    return jax.shard_map(
        functools.partial(body, C, Z),
        mesh=mesh,
        in_specs=(
            batch, batch, P(("dp", "col")), P(("dp", "col")), P("col", None), P(), P(), P("col", None, "row"), block,
            P(), P(), P(), block, P("row"), block, P(),
        ),
        out_specs=(
            batch, batch, P("col", None), P(), P(), P("col", None, "row"), block, P(), P(), P(), block, P("row"),
            block, P(),
        ),
        check_vma=False,
    )
```

```python
import functools
from types import SimpleNamespace

import jax
import jax.numpy as jnp
from jax import lax
from jax.experimental import pallas as pl
from jax.experimental.pallas import tpu as pltpu
from jax.sharding import PartitionSpec as P

HD = 64
LANES = 128
norm_eps = 1e-05
masked_score = -1e30
f32, bf16 = jnp.float32, jnp.bfloat16
MESH = pl.DeviceIdType.MESH
NN = (((1,), (0,)), ((), ()))
NT = (((1,), (1,)), ((), ()))
TN = (((0,), (0,)), ((), ()))
VM = pl.BlockSpec(memory_space=pltpu.VMEM)
SM = pl.BlockSpec(memory_space=pltpu.SMEM)
AN = pl.BlockSpec(memory_space=pl.ANY)
R = 4


def mm(a, b, dims):
    return lax.dot_general(a, b, dims, preferred_element_type=f32)


def remote(src, dst, sems, index, **where):
    return pltpu.make_async_remote_copy(
        src_ref=src, dst_ref=dst, send_sem=sems[0].at[index], recv_sem=sems[1].at[index],
        device_id=where, device_id_type=MESH,
    )


def flip(a, b):
    a0, b0, a1, b1 = lax.rem(a, 2), lax.rem(b, 2), a // 2, b // 2
    return a0 + b0 - 2 * a0 * b0 + 2 * (a1 + b1 - 2 * a1 * b1)


def greet(sizes):
    barrier = pltpu.get_barrier_semaphore()
    total = 0
    for name, count in sizes.items():
        for step in range(1, count):
            to = lax.rem(lax.axis_index(name) + step, count)
            pl.semaphore_signal(barrier, inc=1, device_id={name: to}, device_id_type=MESH)
            total += 1
    for s in range(1, sizes["dp"]):
        for t in range(1, sizes["col"]):
            to = {"dp": lax.rem(lax.axis_index("dp") + s, sizes["dp"]), "col": lax.rem(lax.axis_index("col") + t, sizes["col"])}
            pl.semaphore_signal(barrier, inc=1, device_id=to, device_id_type=MESH)
            total += 1
    pl.semaphore_wait(barrier, total)


def normalize(hidden, width):
    average = jnp.sum(hidden, axis=-1, keepdims=True) / width
    variance = jnp.sum(hidden * hidden, axis=-1, keepdims=True) / width - average * average
    inverse = lax.rsqrt(variance + norm_eps)
    return (hidden - average) * inverse, inverse


def norm_back(grad, centred, inverse, gain, width):
    scaled = grad * gain
    first = jnp.sum(scaled, axis=-1, keepdims=True) / width
    second = jnp.sum(scaled * centred, axis=-1, keepdims=True) / width
    return inverse * (scaled - first - centred * second)


def split_parts(value, lane, count):
    out = jnp.zeros(lane.shape, f32)
    for place in range(count):
        high = value.astype(bf16).astype(f32)
        out = jnp.where(lane == place, high, out)
        value = value - high
    return out.astype(bf16)


def layer_kernel(names, C, Z, *refs):
    n = SimpleNamespace(**dict(zip([name for name in names if not name.startswith("sem_")], refs)))
    plain = sum(1 for name in names if not name.startswith("sem_"))
    sem = {}
    place = plain
    for name in names:
        if name.startswith("sem_"):
            sem[name[4:]] = (refs[place], refs[place + 1])
            place += 2
    local = refs[place]
    r, c, z = lax.axis_index("row"), lax.axis_index("col"), lax.axis_index("dp")
    T, D = n.x.shape
    DC, F = n.w_up.shape
    H = n.w_out.shape[0]
    heads = H // HD
    L = R * T
    half = T // 2
    NTB = n.table.shape[0]
    parity = lax.rem(z, 2)
    zpair = z + 1 - 2 * parity
    nx, ny = flip(r, 1), flip(r, 2)
    cols = pl.ds(pl.multiple_of(c * DC, DC), DC)
    vec = lambda row: n.vectors[row : row + 1, :]
    given = (n.ln1_gain, n.ln1_bias, n.out_bias, n.ln2_gain, n.ln2_bias, n.down_bias, n.up_bias)
    for row, ref in enumerate(given):
        n.vectors[row : row + 1, :] = ref[...].reshape(1, D)
    others = range(1, R)
    peers = range(1, C)
    groups = range(1, Z)

    def col_at(t):
        return lax.rem(c + t, C)

    def lanes(value, device):
        return value[:, device * DC : (device + 1) * DC]

    def rows_of(device):
        return pl.ds(pl.multiple_of(device * DC, DC), DC)

    greet({"row": R, "col": C, "dp": Z})

    def wo_copy(s):
        piece = n.wo.at[r, c]
        return remote(n.w_out, piece, sem["wo"], s - 1, row=flip(r, s))

    def woc_copy(s, t):
        piece = n.wo.at[flip(r, s), c]
        source = n.w_out if s == 0 else piece
        return remote(source, piece, sem["woc"], s * (C - 1) + t - 1, col=col_at(t))

    def ub_copy(s):
        return remote(n.ub.at[r], n.ub.at[r], sem["ub"], s - 1, row=flip(r, s))

    n.ub[r] = jnp.broadcast_to(vec(6), (8, F))
    n.wo[r, c] = n.w_out[...]
    for s in others:
        wo_copy(s).start()
        ub_copy(s).start()
    for t in peers:
        woc_copy(0, t).start()

    def stamp_copy(t):
        return remote(n.stamp_own, n.stamp_got.at[t - 1], sem["stamp"], t - 1, col=col_at(t))

    def pick_copy(t):
        return remote(n.picked.at[t - 1], n.picked_got.at[t - 1], sem["pick"], t - 1, col=lax.rem(c - t + C, C))

    def w_copy(t):
        return remote(n.w_qkv, n.wq.at[c], sem["w"], t - 1, col=col_at(t))

    n.stamp_own[...] = jnp.full(n.stamp_own.shape, n.stamp[0].astype(f32))
    for t in peers:
        stamp_copy(t).start()
    for t in peers:
        w_copy(t).start()
    n.wq[c] = n.w_qkv[...]

    def row_of(stamps):
        number = (lax.broadcasted_iota(jnp.int32, (NTB, D), 0) + c * NTB).astype(f32)
        return jnp.sum(jnp.where(number == stamps, n.table[...].astype(f32), 0.0), axis=0, keepdims=True)

    for t in peers:
        stamp_copy(t).wait_recv()
        n.picked[t - 1] = jnp.broadcast_to(row_of(n.stamp_got[t - 1][0:1, 0:1]), (8, D))
        pick_copy(t).start()
    embed = row_of(n.stamp_own[0:1, 0:1])
    for t in peers:
        pick_copy(t).wait_recv()
        embed = embed + n.picked_got[t - 1][0:1]
    n.emb[...] = jnp.broadcast_to(embed, n.emb.shape)

    def n_copy(link, part):
        piece = n.one.at[r, pl.ds(part * half, half)]
        return remote(piece, piece, sem["n"], 2 * link + part, row=(nx, ny)[link])

    def relay_copy(link):
        piece = n.one.at[(ny, nx)[link], pl.ds(link * half, half)]
        return remote(piece, piece, sem["relay"], link, row=(nx, ny)[link])

    rows_ln = 128
    for part in range(2):

        def norm_step(t, carry, part=part):
            rows = pl.ds(pl.multiple_of(part * half + t * rows_ln, rows_ln), rows_ln)
            centred, inverse = normalize(n.x[rows, :].astype(f32) + n.emb[0:1, :], D)
            n.one[r, rows, :] = (centred * vec(0) + vec(1)).astype(bf16)
            return carry

        lax.fori_loop(0, half // rows_ln, norm_step, 0)
        n_copy(1 - part, part).start()
    n_copy(0, 0).start()
    n_copy(1, 1).start()

    for t in peers:
        w_copy(t).wait_recv()
    lane = lax.broadcasted_iota(jnp.int32, (T, HD), 1)
    q_tail = jnp.zeros((T, HD), bf16)
    k_tail = jnp.where(lane < 3, 1.0, 0.0).astype(bf16)
    v_tail = jnp.where(lane < 2, 1.0, 0.0).astype(bf16)
    scale = HD ** (-0.5)

    def project(s, carry):
        @pl.when(s == 1)
        def _():
            n_copy(1, 0).wait_recv()
            relay_copy(0).start()
            n_copy(0, 1).wait_recv()
            relay_copy(1).start()
            n_copy(0, 0).wait_recv()

        @pl.when(s == 2)
        def _():
            n_copy(1, 1).wait_recv()

        @pl.when(s == 3)
        def _():
            relay_copy(0).wait_recv()
            relay_copy(1).wait_recv()
            weights_start()

        block = flip(r, s)
        normed = n.one[block]
        y = mm(lanes(normed, 0), n.wq[0], NT)
        for device in range(1, C):
            y += mm(lanes(normed, device), n.wq[device], NT)
        y = y.astype(bf16)
        rows = pl.ds(pl.multiple_of(block * T, T), T)
        for h in range(heads):
            n.q[h, rows, :] = jnp.concatenate([y[:, h * HD : (h + 1) * HD] * scale, q_tail], axis=1)
            n.k[h, rows, :] = jnp.concatenate([y[:, H + h * HD : H + (h + 1) * HD], k_tail], axis=1)
            n.v[h, rows, :] = jnp.concatenate([y[:, 2 * H + h * HD : 2 * H + (h + 1) * HD], v_tail], axis=1)
        return carry

    ups = (n.w_up, n.w_down)

    def half_copy(s, kind):
        return remote(ups[kind], n.wud.at[kind, r, cols], sem["g"], s - 1, row=flip(r, s))

    def z_copy(s):
        piece = n.wud.at[parity, flip(r, s), cols]
        return remote(piece, piece, sem["gz"], s - 1, dp=zpair)

    def gc_copy(s, kind, t):
        piece = n.wud.at[kind, flip(r, s), cols]
        source = ups[kind] if s == 0 else piece
        return remote(source, piece, sem["gc"], (2 * s + kind) * (C - 1) + t - 1, col=col_at(t))

    def gc_half(s, second, t):
        piece = n.wud.at[1 - parity if second else parity, flip(r, s), cols]
        return remote(piece, piece, sem["gc"], (2 * s + second) * (C - 1) + t - 1, col=col_at(t))

    def half_start(s):
        for kind in range(2):

            @pl.when(parity == kind)
            def _(kind=kind):
                half_copy(s, kind).start()

    def half_on(s):
        half_copy(s, 0).wait_recv()
        z_copy(s).start()
        for t in peers:
            gc_half(s, 0, t).start()

    def weights_start():
        half_start(3)

    for t in peers:
        for kind in range(2):
            gc_copy(0, kind, t).start()

    lax.fori_loop(0, R, project, 0)

    prefix = n.prefix[0]
    longest = L // 2
    SB = min(256, T)
    nsub = T // SB
    lane_sb = lax.broadcasted_iota(jnp.int32, (SB, HD), 1)

    def a_copy(s):
        i = flip(r, s)
        return remote(n.mine.at[i], n.att.at[r], sem["a"], s - 1, row=i)

    def attend_block(step, carry):
        s = lax.rem(step + 1, R)
        i = flip(r, s)
        for static in range(R):
            early = (static + 1) * T <= longest
            nk = longest if early else (static + 1) * T
            nm = nk if early else T

            def attend(t, inner, nk=nk, nm=nm):
                h = t // nsub
                sub = pl.multiple_of(lax.rem(t, nsub) * SB, SB)
                row = i * T + sub
                rows = pl.ds(pl.multiple_of(row, SB), SB)
                scores = mm(n.q[h, rows, :], n.k[h, :nk, :], NT)
                limit = jnp.maximum(row + 1 + lax.broadcasted_iota(jnp.int32, (SB, 1), 0), prefix)
                key = (nk - nm) + lax.broadcasted_iota(jnp.int32, (SB, nm), 1)
                last = jnp.where(key < limit, scores[:, nk - nm :], masked_score)
                top = jnp.max(last, axis=1, keepdims=True)
                if nk > nm:
                    top = jnp.maximum(top, jnp.max(scores[:, : nk - nm], axis=1, keepdims=True))
                mixed = mm(jnp.exp(last - top).astype(bf16), n.v[h, nk - nm : nk, :], NN)
                if nk > nm:
                    mixed += mm(jnp.exp(scores[:, : nk - nm] - top).astype(bf16), n.v[h, : nk - nm, :], NN)
                weight = mixed[:, HD : HD + 1]
                n.mixed[h, pl.ds(sub, SB), :] = mixed / weight
                n.q[h, rows, HD:] = split_parts(-(top + jnp.log(weight)), lane_sb, 3)
                return inner

            @pl.when(i == static)
            def _(attend=attend):
                lax.fori_loop(0, heads * nsub, attend, 0)

        n.mine[i] = jnp.concatenate([n.mixed[h][:, :HD] for h in range(heads)], axis=1).astype(bf16)

        for at in range(R - 1):

            @pl.when(step == at)
            def _(at=at):
                a_copy(at + 1).start()
                if at == 0:
                    for s in others:
                        wo_copy(s).wait_recv()
                        for t in peers:
                            woc_copy(s, t).start()
                    half_start(1)
                if at == 1:
                    half_on(3)

        return carry

    def attend_all(mixed_ref):
        n.mixed = mixed_ref
        lax.fori_loop(0, R, attend_block, 0)

    pl.run_scoped(attend_all, pltpu.VMEM((heads, T, LANES), f32))
    half_start(2)
    n.att[r] = n.mine[r]
    half_on(1)

    TR = min(256, T)
    TF = 384 if F % 384 == 0 else F
    tiles = F // TF
    ticks = R * tiles

    def turn(k):
        return lax.rem(156 // ((1 + 3 * lax.rem(k, 2)) * (1 + 15 * (k // 2))), R)

    def a2_copy(s):
        b = flip(r, s)
        return remote(n.gsend.at[b], n.gatt.at[r], sem["a2"], s - 1, row=b)

    z_first = n.grow.shape[1] == 1
    row_kinds = (0,) if z_first else (0, 1)

    def row_copy(s, kind):
        return remote(n.crecv.at[s, 0, kind], n.grow.at[s - 1, kind], sem["row"], 2 * (s - 1) + kind, row=flip(r, s))

    def b_part(device):
        height = n.bsum.shape[1]
        return pl.ds(pl.multiple_of(device * height, height), height)

    def b_copy(s, g):
        to = lax.rem(z + g, Z)
        return remote(n.crecv.at[s, 0, 1, b_part(to)], n.bz.at[s, g - 1], sem["b"], s * (Z - 1) + g - 1, dp=to)

    def br_copy(s):
        return remote(n.bsum.at[s], n.brow.at[s - 1], sem["br"], s - 1, row=flip(r, s))

    def b_sum(s):
        if not z_first:
            return
        for g in groups:
            b_copy(s, g).wait_recv()
        total = n.crecv[s, 0, 1, b_part(z), :].astype(f32)
        for g in groups:
            total = total + n.bz[s, g - 1].astype(f32)
        n.bsum[s] = total.astype(bf16)
        if s > 0:
            br_copy(s).start()

    def wrow_copy(s):
        b = flip(r, s)
        return remote(n.orecv.at[0, b], n.orow.at[s - 1], sem["wrow"], s - 1, row=b)

    def u_copy(s):
        return remote(n.ubg.at[flip(r, s)], n.urow.at[s - 1], sem["u"], s - 1, row=flip(r, s))

    def middle(wbuf, acc, gn, n2, n2t, cott, gbuf, obuf):
        def fetch(tick):
            fcols = pl.ds(pl.multiple_of(lax.rem(tick, tiles) * TF, TF), TF)
            slot = lax.rem(tick, 2)
            return pltpu.make_async_copy(
                n.wud.at[:, flip(r, turn(tick // tiles)), :, fcols], wbuf.at[slot], local.at[slot]
            )

        def fetch_start(tick):
            own = turn(tick // tiles) == 0

            @pl.when(jnp.logical_not(own))
            def _():
                fetch(tick).start()

            @pl.when(own)
            def _():
                fcols = pl.ds(pl.multiple_of(lax.rem(tick, tiles) * TF, TF), TF)
                slot = lax.rem(tick, 2)
                for kind in range(2):
                    source = (n.w_up, n.w_down)[kind].at[:, fcols]
                    pltpu.make_async_copy(source, wbuf.at[slot, kind, cols], local.at[slot]).start()
                    for p in peers:
                        rows = rows_of(col_at(p))
                        pltpu.make_async_copy(
                            n.wud.at[kind, r, rows, fcols], wbuf.at[slot, kind, rows], local.at[slot]
                        ).start()

        def c_copy(k, t):
            to = col_at(t)
            return remote(
                gbuf.at[lax.rem(k, 2), :, rows_of(to)], n.crecv.at[turn(k), t - 1], sem["c"], k * (C - 1) + t - 1,
                col=to,
            )

        def o_copy(t):
            to = col_at(t)
            return remote(obuf.at[:, to], n.orecv.at[t - 1], sem["o"], t - 1, col=to)

        def join(k):
            s = turn(k)
            for t in peers:
                c_copy(k, t).wait_recv()
            for kind in range(2):
                total = gbuf[lax.rem(k, 2), kind, cols, :].astype(f32)
                for t in peers:
                    total = total + n.crecv[s, t - 1, kind].astype(f32)
                n.crecv[s, 0, kind] = total.astype(bf16)

            if z_first:
                for g in groups:
                    b_copy(s, g).start()

            @pl.when(s > 0)
            def _():
                u_copy(s).start()
                for kind in row_kinds:
                    row_copy(s, kind).start()

        for p in peers:
            for kind in range(2):
                gc_copy(0, kind, p).wait()
        fetch_start(0)
        cott[...] = n.cot[...].T
        for s in others:
            for t in peers:
                woc_copy(s, t).wait_recv()
        for t in peers:
            woc_copy(0, t).wait_recv()
        for s in others:
            ub_copy(s).wait_recv()
            a_copy(s).wait_recv()
        vsum = jnp.zeros((1, D), f32)
        for part in range(T // TR):
            rows = slice(part * TR, (part + 1) * TR)
            branch = []
            for device in range(C):
                piece = mm(n.att[0, rows, :], n.wo[0, device], NN)
                for b in range(1, R):
                    piece += mm(n.att[b, rows, :], n.wo[b, device], NN)
                branch.append(piece)
            branch = jnp.concatenate(branch, axis=1)
            hidden = n.x[rows, :].astype(f32) + n.emb[0:1, :] + branch + vec(2)
            n.tgrad[rows, :] = hidden
            centred, inverse = normalize(hidden, D)
            n2[rows, :] = (centred * vec(3) + vec(4)).astype(bf16)
            acc[rows, :] = jnp.zeros((TR, D), f32)
            gn[rows, :] = jnp.zeros((TR, D), f32)
            vsum = vsum + jnp.sum(n.cot[rows, :].astype(f32), axis=0, keepdims=True)
        n2t[...] = n2[...].T
        n.vbuf[5:6, :] = vsum

        def second_half(s):
            z_copy(s).wait_recv()
            for p in peers:
                gc_half(s, 1, p).start()

        def arrived(s):
            for p in peers:
                for kind in range(2):
                    gc_copy(s, kind, p).wait_recv()

        def tick_step(tick, carry):
            k, t = tick // tiles, lax.rem(tick, tiles)
            b = flip(r, turn(k))
            slot, wslot = lax.rem(k, 2), lax.rem(tick, 2)
            fetch(tick).wait()

            @pl.when((t == 0) & (k >= 2))
            def _():
                for p in peers:
                    c_copy(k - 2, p).wait_send()

            @pl.when(tick == tiles - 1)
            def _():
                half_on(2)
                second_half(3)
                arrived(3)

            @pl.when((t < tiles - 1) | (k == 0))
            def _():
                fetch_start(tick + 1)

            fcols = pl.ds(pl.multiple_of(t * TF, TF), TF)
            wu = wbuf[wslot, 0]
            wd = wbuf[wslot, 1]
            inner = mm(n2[...], wu, NN) + n.ub[b, 0:1, fcols]
            cdf = 0.5 * (1.0 + lax.erf(inner * 0.7071067811865476))
            slope = cdf + inner * (jnp.exp(-0.5 * inner * inner) * 0.3989422804014327)
            active = (inner * cdf).astype(bf16)
            acc[...] += mm(active, wd, NT)
            ginner = mm(n.cot[...], wd, NN) * slope
            glow = ginner.astype(bf16)
            gn[...] += mm(glow, wu, NT)
            gbuf[slot, 1, :, fcols] = mm(cott[...], active, NN).astype(bf16)
            gbuf[slot, 0, :, fcols] = mm(n2t[...], glow, NN).astype(bf16)
            n.ubg[b, :, fcols] = jnp.sum(ginner, axis=0, keepdims=True)

            @pl.when(t == tiles - 1)
            def _():
                for p in peers:
                    c_copy(k, p).start()

                for near, turn_before in ((1, 1), (2, 2)):

                    @pl.when(k == turn_before)
                    def _(near=near):
                        second_half(near)
                        arrived(near)
                        fetch_start(tick + 1)

            @pl.when((t == 0) & (k > 0))
            def _():
                join(k - 1)

            return carry

        lax.fori_loop(0, ticks, tick_step, 0)

        gain_sum = jnp.zeros((1, D), f32)
        bias_sum = jnp.zeros((1, D), f32)
        hid_sum = jnp.zeros((1, D), f32)
        for part in range(T // TR):
            rows = slice(part * TR, (part + 1) * TR)
            hidden = n.tgrad[rows, :]
            n.out[rows, :] = (hidden + acc[rows, :] + vec(5)).astype(bf16)
            centred, inverse = normalize(hidden, D)
            g = gn[rows, :]
            gh = n.cot[rows, :].astype(f32) + norm_back(g, centred, inverse, vec(3), D)
            n.tgrad[rows, :] = gh
            n2[rows, :] = gh.astype(bf16)
            gain_sum = gain_sum + jnp.sum(g * centred, axis=0, keepdims=True)
            bias_sum = bias_sum + jnp.sum(g, axis=0, keepdims=True)
            hid_sum = hid_sum + jnp.sum(gh, axis=0, keepdims=True)
        n.vbuf[2:3, :] = hid_sum
        n.vbuf[3:4, :] = gain_sum
        n.vbuf[4:5, :] = bias_sum

        def back_step(at, carry):
            s = R - 1 - at
            b = flip(r, s)
            grad = n2[...]
            back = mm(lanes(grad, 0), n.wo[b, 0], NT)
            for device in range(1, C):
                back += mm(lanes(grad, device), n.wo[b, device], NT)
            n.gsend[b] = back.astype(bf16)

            @pl.when(s > 0)
            def _():
                a2_copy(s).start()

            return carry

        lax.fori_loop(0, R, back_step, 0)
        n.gatt[r] = n.gsend[r]
        join(R - 1)

        def out_step(b, carry):
            block = mm(n.att[b], n2[...], TN).astype(bf16)
            for device in range(C):
                obuf[b, device] = lanes(block, device)
            return carry

        lax.fori_loop(0, R, out_step, 0)
        for t in peers:
            o_copy(t).start()
        for t in peers:
            o_copy(t).wait_recv()
        for b in range(R):
            total = obuf[b, c].astype(f32)
            for t in peers:
                total = total + n.orecv[t - 1, b].astype(f32)
            n.orecv[0, b] = total.astype(bf16)
        for s in others:
            wrow_copy(s).start()
        for t in peers:
            o_copy(t).wait_send()
            for s in range(R - 2, R):
                c_copy(s, t).wait_send()

    dt = bf16
    pl.run_scoped(
        middle,
        pltpu.VMEM((2, 2, D, TF), dt), pltpu.VMEM((T, D), f32), pltpu.VMEM((T, D), f32), pltpu.VMEM((T, D), dt),
        pltpu.VMEM((D, T), dt), pltpu.VMEM((D, T), dt), pltpu.VMEM((2, 2, D, F), dt), pltpu.VMEM((R, C, H, DC), dt),
    )

    sources = (n.crecv.at[0, 0, 0], n.crecv.at[0, 0, 1], n.oblk, n.qblk)
    landing = (n.zr.at[0], n.zr.at[n.zr.shape[0] - 1], n.zro, n.zrq)
    finals = (n.up_out, n.down_out, n.wo_out, n.qkv_out)

    heights = (DC, DC, H, 3 * H)
    split = [landing[kind].shape[1] != heights[kind] for kind in range(4)]
    def part_of(kind, device):
        height = landing[kind].shape[1]
        return pl.ds(pl.multiple_of(device * height, height), height) if split[kind] else slice(None)

    def zz_copy(kind, s):
        to = lax.rem(z + s, Z)
        return remote(sources[kind].at[part_of(kind, to)], landing[kind].at[s - 1], sem["z"], kind * (Z - 1) + s - 1, dp=to)

    def y_copy(kind, s):
        piece = finals[kind].at[part_of(kind, z)]
        return remote(piece, piece, sem["y"], kind * (Z - 1) + s - 1, dp=lax.rem(z + s, Z))

    def z_start(kind):
        for s in groups:
            zz_copy(kind, s).start()

    def z_end(kind):
        for s in groups:
            zz_copy(kind, s).wait_recv()
        total = sources[kind][part_of(kind, z), :].astype(f32)
        for s in groups:
            total = total + landing[kind][s - 1].astype(f32)
        finals[kind][part_of(kind, z), :] = total.astype(bf16)
        if split[kind]:
            for s in groups:
                y_copy(kind, s).start()

    def down_end():
        if not z_first:
            z_end(1)
            return
        total = n.bsum[0].astype(f32)
        for s in others:
            br_copy(s).wait_recv()
            total = total + n.brow[s - 1].astype(f32)
        finals[1][b_part(z), :] = total.astype(bf16)
        for s in groups:
            y_copy(1, s).start()

    def z_finish(kind):
        for s in groups:
            if kind != 1 or not z_first:
                zz_copy(kind, s).wait_send()
            if split[kind]:
                y_copy(kind, s).wait()

    def row_sum(kind):
        total = n.crecv[0, 0, kind].astype(f32)
        for s in others:
            row_copy(s, kind).wait_recv()
            total = total + n.grow[s - 1, kind].astype(f32)
        n.crecv[0, 0, kind] = total.astype(bf16)
        z_start(kind)

    def wrow_sum():
        for s in others:
            wrow_copy(s).wait_recv()
        total = n.orecv[0, r].astype(f32)
        for s in others:
            total = total + n.orow[s - 1].astype(f32)
        n.oblk[...] = total.astype(bf16)
        z_start(2)

    def p_copy(link, part, b):
        piece = pl.ds(part * half, half)
        return remote(n.part.at[b, piece], n.prec.at[link, piece], sem["p"], 2 * link + part, row=(nx, ny)[link])

    def pr_copy(link, b):
        return remote(n.part.at[b, pl.ds(link * half, half)], n.prel.at[link], sem["pr"], link, row=(nx, ny)[link])

    def back(d, dq, dk, dv, gp, qg):
        def spread(b):
            rows = pl.ds(b * T, T)

            @pl.when(r != b)
            def _():
                s = flip(r, b)
                remote(n.gsend.at[b], n.gatt.at[b], sem["a2"], s - 1, row=b).wait_recv()

            ga = n.gatt[b]
            both = ga.astype(f32) * n.mine[b].astype(f32)
            for h in range(heads):
                piece = slice(h * HD, (h + 1) * HD)
                delta = jnp.sum(both[:, piece], axis=1, keepdims=True)
                d[h, rows, :] = jnp.concatenate([ga[:, piece], split_parts(-delta, lane, 2)], axis=1)

        def pair(h, i, j, masked):
            qs = pl.ds(pl.multiple_of(i * T, T), T)
            ks = pl.ds(pl.multiple_of(j * T, T), T)
            qb, kb, vb, db = n.q[h, qs, :], n.k[h, ks, :], n.v[h, ks, :], d[h, qs, :]
            scores = mm(kb, qb, NT)
            if masked:
                limit = jnp.maximum(i * T + 1 + lax.broadcasted_iota(jnp.int32, (1, T), 1), prefix)
                key = j * T + lax.broadcasted_iota(jnp.int32, (T, T), 0)
                scores = jnp.where(key < limit, scores, masked_score)
            probs = jnp.exp(scores)
            gscores = (probs * mm(vb, db, NT)).astype(bf16)
            dv[h, ks, :] += mm(probs.astype(bf16), db, NN)
            dk[h, ks, :] += mm(gscores, qb, NN)
            dq[h, qs, :] += mm(gscores, kb, TN)

        def finish(b):
            rows = pl.ds(b * T, T)
            stack = jnp.concatenate(
                [dq[h, rows, :][:, :HD] * scale for h in range(heads)]
                + [dk[h, rows, :][:, :HD] for h in range(heads)]
                + [dv[h, rows, :][:, :HD] for h in range(heads)],
                axis=1,
            ).astype(bf16)
            gp[b] = stack
            n.part[b] = jnp.concatenate(
                [mm(stack, n.wq[device], NN).astype(bf16) for device in range(C)], axis=1
            )
            s = flip(r, b)

            @pl.when(s == 3)
            def _():
                pr_copy(0, b).start()
                pr_copy(1, b).start()

            for link in range(2):

                @pl.when(s == link + 1)
                def _(link=link):
                    p_copy(link, link, b).start()

        def combine(b):
            s = flip(r, b)
            for link in range(2):

                @pl.when(s == link + 1)
                def _(link=link):
                    came = 1 - link
                    pr_copy(came, b).wait_recv()
                    piece = pl.ds(came * half, half)
                    total = n.part[b, piece, :].astype(f32) + n.prel[came].astype(f32)
                    n.part[b, piece, :] = total.astype(bf16)
                    p_copy(link, came, b).start()

        dq[...] = jnp.zeros_like(dq)
        dk[...] = jnp.zeros_like(dk)
        dv[...] = jnp.zeros_like(dv)
        early = R // 2
        for i in range(R - 1, early - 1, -1):
            spread(i)

            def plain_pair(t, carry, i=i):
                pair(t // i, i, lax.rem(t, i), False)
                return carry

            def diagonal(h, carry, i=i):
                pair(h, i, i, True)
                return carry

            lax.fori_loop(0, heads * i, plain_pair, 0)
            lax.fori_loop(0, heads, diagonal, 0)
            finish(i)
            if i + 1 < R:
                combine(i + 1)
            else:
                b_sum(0)
                b_sum(3)
                b_sum(1)
        for i in range(early - 1, -1, -1):
            spread(i)
        b_sum(2)
        row_sum(0)

        def square(t, carry):
            rest = lax.rem(t, early * early)
            pair(t // (early * early), rest // early, lax.rem(rest, early), True)
            return carry

        def corner(t, carry):
            rest = lax.rem(t, 3)
            pair(t // 3, 1 - rest // 2, (rest + 1) // 2 - rest // 2 + rest // 2, True)
            return carry

        def origin(h, carry):
            pair(h, 0, 0, True)
            return carry

        if early == 2:
            lax.fori_loop(0, 3 * heads // 2, corner, 0)
        else:
            lax.fori_loop(0, heads * early * early, square, 0)
        if not z_first:
            row_sum(1)
        wrow_sum()
        if early == 2:
            lax.fori_loop(3 * heads // 2, 3 * heads, corner, 0)
            down_end()
            finish(1)
            combine(2)
            lax.fori_loop(0, heads, origin, 0)
            finish(0)
            z_end(0)
        else:
            for b in range(early - 1, -1, -1):
                finish(b)
            combine(early)
            down_end()
            z_end(0)

        qg[...] = jnp.zeros_like(qg)

        def qkv_step(b, carry):
            qg[...] += mm(gp[b], n.one[b], TN)
            return carry

        lax.fori_loop(0, R, qkv_step, 0)
        for device in range(C):
            n.wq[device] = lanes(qg, device).astype(bf16)

        def q_copy(t):
            to = col_at(t)
            return remote(n.wq.at[to], n.qrecv.at[t - 1], sem["q"], t - 1, col=to)

        for t in peers:
            q_copy(t).start()
        for b in range(early - 1, -1, -1):
            combine(b)
        z_end(2)
        for t in peers:
            q_copy(t).wait()
        total = n.wq[c].astype(f32)
        for t in peers:
            total = total + n.qrecv[t - 1].astype(f32)
        n.qblk[...] = total.astype(bf16)
        z_start(3)

    pl.run_scoped(
        back,
        pltpu.VMEM((heads, L, LANES), bf16), pltpu.VMEM((heads, L, LANES), f32), pltpu.VMEM((heads, L, LANES), f32),
        pltpu.VMEM((heads, L, LANES), f32), pltpu.VMEM((R, T, 3 * H), bf16), pltpu.VMEM((3 * H, D), f32),
    )

    for link in range(2):
        for part in range(2):
            p_copy(link, part, 0).wait_recv()
    gain_sum = jnp.zeros((1, D), f32)
    bias_sum = jnp.zeros((1, D), f32)
    all_sum = jnp.zeros((1, D), f32)
    for piece in range(T // TR):
        rows = slice(piece * TR, (piece + 1) * TR)
        g = n.part[r, rows, :].astype(f32) + n.prec[0, rows, :].astype(f32) + n.prec[1, rows, :].astype(f32)
        centred, inverse = normalize(n.x[rows, :].astype(f32) + n.emb[0:1, :], D)
        total = n.tgrad[rows, :] + norm_back(g, centred, inverse, vec(0), D)
        n.tgrad[rows, :] = total
        gain_sum = gain_sum + jnp.sum(g * centred, axis=0, keepdims=True)
        bias_sum = bias_sum + jnp.sum(g, axis=0, keepdims=True)
        all_sum = all_sum + jnp.sum(total, axis=0, keepdims=True)

    n.vbuf[0:1, :] = gain_sum
    n.vbuf[1:2, :] = bias_sum
    n.vbuf[6:7, :] = all_sum
    n.vbuf[7:8, :] = jnp.zeros((1, D), f32)

    def v_copy(s):
        return remote(n.vbuf, n.vrow.at[s - 1], sem["v"], s - 1, row=flip(r, s))

    def all_copy(s, t):
        piece = n.vall.at[z, c]
        return remote(piece, piece, sem["vz"], s * C + t - 1, dp=lax.rem(z + s, Z), col=col_at(t))

    rest = [(s, t) for s in range(Z) for t in range(C) if s + t > 0]
    for s in others:
        v_copy(s).start()
    up_bias = n.ubg[r]
    for s in others:
        u_copy(s).wait_recv()
        up_bias = up_bias + n.urow[s - 1]
    for s in others:
        v_copy(s).wait_recv()
    total = n.vbuf[...]
    for s in others:
        total = total + n.vrow[s - 1]
    n.vall[z, c, 0:8, :] = total
    n.vall[z, c, 7:8, :] = up_bias
    n.vall[z, c, 8:16, :] = jnp.full((8, D), n.stamp[0].astype(f32))
    for s, t in rest:
        all_copy(s, t).start()
    z_end(3)
    for s, t in rest:
        all_copy(s, t).wait_recv()
    total = jnp.zeros((8, D), f32)
    number = (lax.broadcasted_iota(jnp.int32, (NTB, D), 0) + c * NTB).astype(f32)
    table = jnp.zeros((NTB, D), f32)
    for s in range(Z):
        for t in range(C):
            total = total + n.vall[s, t, 0:8, :]
            table = table + jnp.where(number == n.vall[s, t, 8:9, :], n.vall[s, t, 6:7, :], 0.0)
    n.small[...] = total
    n.table_out[...] = table

    for t in peers:
        stamp_copy(t).wait_send()
        pick_copy(t).wait_send()
        w_copy(t).wait_send()
        for s in range(R):
            woc_copy(s, t).wait_send()
            if s > 0:
                gc_copy(s, 0, t).wait_send()
                gc_copy(s, 1, t).wait_send()
    for link in range(2):
        relay_copy(link).wait_send()
        pr_copy(link, 0).wait_send()
        for part in range(2):
            n_copy(link, part).wait_send()
            p_copy(link, part, 0).wait_send()
    for s in others:
        half_copy(s, 0).wait_send()
        for copy in (a_copy, z_copy, wo_copy, ub_copy, a2_copy, wrow_copy, u_copy, v_copy):
            copy(s).wait_send()
        for kind in row_kinds:
            row_copy(s, kind).wait_send()
        if z_first:
            br_copy(s).wait_send()
    if z_first:
        for s in range(R):
            for g in groups:
                b_copy(s, g).wait_send()
    for s, t in rest:
        all_copy(s, t).wait_send()
    for kind in range(4):
        z_finish(kind)


def run_layer(C, Z, stamp, prefix, x, cot, table, vectors, w_qkv, w_out, w_up, w_down):
    T, D = x.shape
    DC, F = w_up.shape
    H = w_out.shape[0]
    heads = H // HD
    L = R * T
    NTB = table.shape[0]
    part = lambda height: height // Z if height % (16 * Z) == 0 else height
    kinds, rows_b = (1, DC // Z) if DC % (16 * Z) == 0 else (2, 16)
    vm = pltpu.VMEM
    given = ("ln1_gain", "ln1_bias", "out_bias", "ln2_gain", "ln2_bias", "down_bias", "up_bias")
    ins = dict(stamp=SM, prefix=SM, x=VM, cot=VM, table=VM, **{name: VM for name in given}, w_qkv=VM, w_out=VM, w_up=AN, w_down=AN)
    outs = dict(
        out=((T, D), bf16), tgrad=((T, D), f32), up_out=((DC, F), bf16), down_out=((DC, F), bf16),
        wo_out=((H, DC), bf16), qkv_out=((3 * H, DC), bf16), small=((8, D), f32), table_out=((NTB, D), f32),
        wud=((2, R, D, F), bf16),
    )
    scratch = dict(
        stamp_own=vm((8, LANES), f32), stamp_got=vm((C - 1, 8, LANES), f32), picked=vm((C - 1, 8, D), f32),
        picked_got=vm((C - 1, 8, D), f32), emb=vm((8, D), f32), vectors=vm((8, D), f32), wq=vm((C, 3 * H, DC), bf16), one=vm((R, T, D), bf16),
        q=vm((heads, L, LANES), bf16), k=vm((heads, L, LANES), bf16), v=vm((heads, L, LANES), bf16),
        mine=vm((R, T, H), bf16), att=vm((R, T, H), bf16), wo=vm((R, C, H, DC), bf16),
        ub=vm((R, 8, F), f32), vbuf=vm((8, D), f32), ubg=vm((R, 1, F), f32),
        crecv=vm((R, C - 1, 2, DC, F), bf16), orecv=vm((C - 1, R, H, DC), bf16), gsend=vm((R, T, H), bf16),
        gatt=vm((R, T, H), bf16), grow=vm((R - 1, kinds, DC, F), bf16), orow=vm((R - 1, H, DC), bf16),
        urow=vm((R - 1, 1, F), f32), bz=vm((R, Z - 1, rows_b, F), bf16), bsum=vm((R, rows_b, F), bf16), brow=vm((R - 1, rows_b, F), bf16), part=vm((R, T, D), bf16), prec=vm((2, T, D), bf16), prel=vm((2, T // 2, D), bf16),
        qrecv=vm((C - 1, 3 * H, DC), bf16), oblk=vm((H, DC), bf16), qblk=vm((3 * H, DC), bf16),
        zr=vm((kinds, Z - 1, part(DC), F), bf16), zro=vm((Z - 1, part(H), DC), bf16), zrq=vm((Z - 1, part(3 * H), DC), bf16),
        vrow=vm((R - 1, 8, D), f32), vall=vm((Z, C, 16, D), f32),
    )
    sems = dict(
        stamp=C - 1, pick=C - 1, w=C - 1, n=4, relay=2, g=R - 1, gz=R - 1, b=R * (Z - 1), br=R - 1, gc=2 * R * (C - 1), wo=R - 1,
        woc=R * (C - 1), ub=R - 1, a=R - 1, a2=R - 1, row=2 * (R - 1), wrow=R - 1, u=R - 1, c=R * (C - 1), o=C - 1,
        z=4 * (Z - 1), y=4 * (Z - 1), p=4, pr=2, q=C - 1, v=R - 1, vz=Z * C - 1,
    )
    names = list(ins) + list(outs) + list(scratch) + ["sem_" + name for name in sems]
    dma = pltpu.SemaphoreType.DMA
    semaphores = []
    for count in sems.values():
        semaphores += [dma((count,)), dma((count,))]
    results = pl.pallas_call(
        functools.partial(layer_kernel, names, C, Z),
        out_shape=tuple(jax.ShapeDtypeStruct(*spec) for spec in outs.values()),
        in_specs=list(ins.values()),
        out_specs=(VM,) * (len(outs) - 1) + (AN,),
        scratch_shapes=list(scratch.values()) + semaphores + [dma((2,))],
        compiler_params=pltpu.CompilerParams(collective_id=0, has_side_effects=True, vmem_limit_bytes=67043328),
        name="layer",
    )(stamp, prefix, x, cot, table, *vectors, w_qkv, w_out, w_up, w_down)
    return dict(zip(outs, results))


def tail_kernel(out, tgrad, table, small, up, down, wo, qkv, *refs):
    refs[0][...] = out[...]
    refs[1][...] = tgrad[...]
    for source, target in zip((up, down, wo, qkv), refs[3:7]):
        target[...] = source[...].astype(f32)

    @pl.when(pl.program_id(0) == 0)
    def _():
        refs[2][...] = table[...]
        for row in range(8):
            if row != 6:
                target = refs[7 + (row if row < 6 else 6)]
                target[...] = small[row : row + 1, :].reshape(target.shape[0])


def run_tail(o):
    steps = 4
    arrays = [o[name] for name in ("out", "tgrad", "table_out", "small", "up_out", "down_out", "wo_out", "qkv_out")]

    def rows(array):
        return pl.BlockSpec((array.shape[0] // steps, array.shape[1]), lambda i: (i, 0))

    def whole(array):
        return pl.BlockSpec(array.shape, lambda i: (0, 0))

    ins = [whole(array) if i in (2, 3) else rows(array) for i, array in enumerate(arrays)]
    width = arrays[3].shape[1]
    line = pl.BlockSpec((width,), lambda i: (0,))
    chosen = (0, 1, 2, 4, 5, 6, 7)
    kinds = [arrays[i].dtype if i < 4 else f32 for i in chosen]
    return pl.pallas_call(
        tail_kernel,
        grid=(steps,),
        out_shape=[jax.ShapeDtypeStruct(arrays[i].shape, kind) for i, kind in zip(chosen, kinds)]
        + [jax.ShapeDtypeStruct((width,), f32)] * 7,
        in_specs=ins,
        out_specs=[ins[i] for i in chosen] + [line] * 7,
        name="results",
    )(*arrays)


def body(C, Z, *args):
    (tokens, cotangent, timesteps, prefix_len, time_table, ln1_gain, ln1_bias, w_qkv, w_out, out_bias,
     ln2_gain, ln2_bias, w_up, up_bias, w_down, down_bias) = args
    DC, _, H = w_qkv.shape
    vectors = (ln1_gain, ln1_bias, out_bias, ln2_gain, ln2_bias, down_bias, up_bias)
    o = run_layer(
        C, Z, timesteps, prefix_len, tokens[0], cotangent[0], time_table, vectors,
        w_qkv.transpose(1, 2, 0).reshape(3 * H, DC), w_out.T, w_up, w_down,
    )
    out, tgrad, table, up, down, wo, qkv, gain1, bias1, bias_out, gain2, bias2, bias_down, bias_up = run_tail(o)
    return (
        out[None], tgrad[None], table, gain1, bias1, qkv.reshape(3, H, DC).transpose(2, 0, 1), wo.T, bias_out, gain2,
        bias2, up, bias_up, down, bias_down,
    )


def solution(mesh):
    C, Z = mesh.shape["col"], mesh.shape["dp"]
    batch = P(("dp", "col"), "row", None)
    block = P("col", "row")
    return jax.shard_map(
        functools.partial(body, C, Z),
        mesh=mesh,
        in_specs=(
            batch, batch, P(("dp", "col")), P(("dp", "col")), P("col", None), P(), P(), P("col", None, "row"), block,
            P(), P(), P(), block, P("row"), block, P(),
        ),
        out_specs=(
            batch, batch, P("col", None), P(), P(), P("col", None, "row"), block, P(), P(), P(), block, P("row"),
            block, P(),
        ),
        check_vma=False,
    )
```

```python
import functools
from types import SimpleNamespace

import jax
import jax.numpy as jnp
from jax import lax
from jax.experimental import pallas as pl
from jax.experimental.pallas import tpu as pltpu
from jax.sharding import PartitionSpec as P

HD = 64
LANES = 128
norm_eps = 1e-05
masked_score = -1e30
f32, bf16 = jnp.float32, jnp.bfloat16
MESH = pl.DeviceIdType.MESH
NN = (((1,), (0,)), ((), ()))
NT = (((1,), (1,)), ((), ()))
TN = (((0,), (0,)), ((), ()))
VM = pl.BlockSpec(memory_space=pltpu.VMEM)
SM = pl.BlockSpec(memory_space=pltpu.SMEM)
AN = pl.BlockSpec(memory_space=pl.ANY)
R = 4


def mm(a, b, dims):
    return lax.dot_general(a, b, dims, preferred_element_type=f32)


def remote(src, dst, sems, index, **where):
    return pltpu.make_async_remote_copy(
        src_ref=src, dst_ref=dst, send_sem=sems[0].at[index], recv_sem=sems[1].at[index],
        device_id=where, device_id_type=MESH,
    )


def flip(a, b):
    a0, b0, a1, b1 = lax.rem(a, 2), lax.rem(b, 2), a // 2, b // 2
    return a0 + b0 - 2 * a0 * b0 + 2 * (a1 + b1 - 2 * a1 * b1)


def greet(sizes, local_work):
    barrier = pltpu.get_barrier_semaphore()
    total = 0
    for name, count in sizes.items():
        for step in range(1, count):
            to = lax.rem(lax.axis_index(name) + step, count)
            pl.semaphore_signal(barrier, inc=1, device_id={name: to}, device_id_type=MESH)
            total += 1
    for s in range(1, sizes["dp"]):
        for t in range(1, sizes["col"]):
            to = {"dp": lax.rem(lax.axis_index("dp") + s, sizes["dp"]), "col": lax.rem(lax.axis_index("col") + t, sizes["col"])}
            pl.semaphore_signal(barrier, inc=1, device_id=to, device_id_type=MESH)
            total += 1
    local_work()
    pl.semaphore_wait(barrier, total)


def normalize(hidden, width):
    average = jnp.sum(hidden, axis=-1, keepdims=True) / width
    variance = jnp.sum(hidden * hidden, axis=-1, keepdims=True) / width - average * average
    inverse = lax.rsqrt(variance + norm_eps)
    return (hidden - average) * inverse, inverse


def norm_back(grad, centred, inverse, gain, width):
    scaled = grad * gain
    first = jnp.sum(scaled, axis=-1, keepdims=True) / width
    second = jnp.sum(scaled * centred, axis=-1, keepdims=True) / width
    return inverse * (scaled - first - centred * second)


def split_parts(value, lane, count):
    out = jnp.zeros(lane.shape, f32)
    for place in range(count):
        high = value.astype(bf16).astype(f32)
        out = jnp.where(lane == place, high, out)
        value = value - high
    return out.astype(bf16)


def layer_kernel(names, C, Z, *refs):
    n = SimpleNamespace(**dict(zip([name for name in names if not name.startswith("sem_")], refs)))
    plain = sum(1 for name in names if not name.startswith("sem_"))
    sem = {}
    place = plain
    for name in names:
        if name.startswith("sem_"):
            sem[name[4:]] = (refs[place], refs[place + 1])
            place += 2
    local = refs[place]
    r, c, z = lax.axis_index("row"), lax.axis_index("col"), lax.axis_index("dp")
    T, D = n.x.shape
    DC, F = n.w_up.shape
    H = n.w_out.shape[0]
    heads = H // HD
    L = R * T
    half = T // 2
    NTB = n.table.shape[0]
    parity = lax.rem(z, 2)
    zpair = z + 1 - 2 * parity
    nx, ny = flip(r, 1), flip(r, 2)
    cols = pl.ds(pl.multiple_of(c * DC, DC), DC)
    vec = lambda row: n.vectors[row : row + 1, :]
    given = (n.ln1_gain, n.ln1_bias, n.out_bias, n.ln2_gain, n.ln2_bias, n.down_bias, n.up_bias)
    others = range(1, R)
    peers = range(1, C)
    groups = range(1, Z)

    def col_at(t):
        return lax.rem(c + t, C)

    def lanes(value, device):
        return value[:, device * DC : (device + 1) * DC]

    def rows_of(device):
        return pl.ds(pl.multiple_of(device * DC, DC), DC)

    def row_of(stamps):
        number = (lax.broadcasted_iota(jnp.int32, (NTB, D), 0) + c * NTB).astype(f32)
        return jnp.sum(jnp.where(number == stamps, n.table[...].astype(f32), 0.0), axis=0, keepdims=True)

    def prepare():
        for row, ref in enumerate(given):
            n.vectors[row : row + 1, :] = ref[...].reshape(1, D)
        n.stamp_own[...] = jnp.full(n.stamp_own.shape, n.stamp[0].astype(f32))
        n.ub[r] = jnp.broadcast_to(vec(6), (8, F))
        n.wo[r, c] = n.w_out[...]
        n.wq[c] = n.w_qkv[...]
        n.emb[...] = jnp.broadcast_to(row_of(n.stamp_own[0:1, 0:1]), n.emb.shape)

    greet({"row": R, "col": C, "dp": Z}, prepare)

    def wo_copy(s):
        piece = n.wo.at[r, c]
        return remote(n.w_out, piece, sem["wo"], s - 1, row=flip(r, s))

    def woc_copy(s, t):
        piece = n.wo.at[flip(r, s), c]
        source = n.w_out if s == 0 else piece
        return remote(source, piece, sem["woc"], s * (C - 1) + t - 1, col=col_at(t))

    def ub_copy(s):
        return remote(n.ub.at[r], n.ub.at[r], sem["ub"], s - 1, row=flip(r, s))

    for s in others:
        wo_copy(s).start()
        ub_copy(s).start()
    for t in peers:
        woc_copy(0, t).start()

    def stamp_copy(t):
        return remote(n.stamp_own, n.stamp_got.at[t - 1], sem["stamp"], t - 1, col=col_at(t))

    def pick_copy(t):
        return remote(n.picked.at[t - 1], n.picked_got.at[t - 1], sem["pick"], t - 1, col=lax.rem(c - t + C, C))

    def w_copy(t):
        return remote(n.w_qkv, n.wq.at[c], sem["w"], t - 1, col=col_at(t))

    for t in peers:
        stamp_copy(t).start()
    for t in peers:
        w_copy(t).start()

    for t in peers:
        stamp_copy(t).wait_recv()
        n.picked[t - 1] = jnp.broadcast_to(row_of(n.stamp_got[t - 1][0:1, 0:1]), (8, D))
        pick_copy(t).start()
    embed = n.emb[0:1, :]
    for t in peers:
        pick_copy(t).wait_recv()
        embed = embed + n.picked_got[t - 1][0:1]
    n.emb[...] = jnp.broadcast_to(embed, n.emb.shape)

    def n_copy(link, part):
        piece = n.one.at[r, pl.ds(part * half, half)]
        return remote(piece, piece, sem["n"], 2 * link + part, row=(nx, ny)[link])

    def relay_copy(link):
        piece = n.one.at[(ny, nx)[link], pl.ds(link * half, half)]
        return remote(piece, piece, sem["relay"], link, row=(nx, ny)[link])

    rows_ln = 128
    for part in range(2):

        def norm_step(t, carry, part=part):
            rows = pl.ds(pl.multiple_of(part * half + t * rows_ln, rows_ln), rows_ln)
            centred, inverse = normalize(n.x[rows, :].astype(f32) + n.emb[0:1, :], D)
            n.one[r, rows, :] = (centred * vec(0) + vec(1)).astype(bf16)
            return carry

        lax.fori_loop(0, half // rows_ln, norm_step, 0)
        n_copy(1 - part, part).start()
    n_copy(0, 0).start()
    n_copy(1, 1).start()

    for t in peers:
        w_copy(t).wait_recv()
    lane = lax.broadcasted_iota(jnp.int32, (T, HD), 1)
    q_tail = jnp.zeros((T, HD), bf16)
    k_tail = jnp.where(lane < 3, 1.0, 0.0).astype(bf16)
    v_tail = jnp.where(lane < 2, 1.0, 0.0).astype(bf16)
    scale = HD ** (-0.5)

    def project(s, carry):
        @pl.when(s == 1)
        def _():
            n_copy(1, 0).wait_recv()
            relay_copy(0).start()
            n_copy(0, 1).wait_recv()
            relay_copy(1).start()
            n_copy(0, 0).wait_recv()

        @pl.when(s == 2)
        def _():
            n_copy(1, 1).wait_recv()

        @pl.when(s == 3)
        def _():
            relay_copy(0).wait_recv()
            relay_copy(1).wait_recv()
            weights_start()

        block = flip(r, s)
        normed = n.one[block]
        y = mm(lanes(normed, 0), n.wq[0], NT)
        for device in range(1, C):
            y += mm(lanes(normed, device), n.wq[device], NT)
        y = y.astype(bf16)
        rows = pl.ds(pl.multiple_of(block * T, T), T)
        for h in range(heads):
            n.q[h, rows, :] = jnp.concatenate([y[:, h * HD : (h + 1) * HD] * scale, q_tail], axis=1)
            n.k[h, rows, :] = jnp.concatenate([y[:, H + h * HD : H + (h + 1) * HD], k_tail], axis=1)
            n.v[h, rows, :] = jnp.concatenate([y[:, 2 * H + h * HD : 2 * H + (h + 1) * HD], v_tail], axis=1)
        return carry

    ups = (n.w_up, n.w_down)

    def half_copy(s, kind):
        return remote(ups[kind], n.wud.at[kind, r, cols], sem["g"], s - 1, row=flip(r, s))

    def z_copy(s):
        piece = n.wud.at[parity, flip(r, s), cols]
        return remote(piece, piece, sem["gz"], s - 1, dp=zpair)

    def gc_copy(s, kind, t):
        piece = n.wud.at[kind, flip(r, s), cols]
        source = ups[kind] if s == 0 else piece
        return remote(source, piece, sem["gc"], (2 * s + kind) * (C - 1) + t - 1, col=col_at(t))

    def gc_half(s, second, t):
        piece = n.wud.at[1 - parity if second else parity, flip(r, s), cols]
        return remote(piece, piece, sem["gc"], (2 * s + second) * (C - 1) + t - 1, col=col_at(t))

    def half_start(s):
        for kind in range(2):

            @pl.when(parity == kind)
            def _(kind=kind):
                half_copy(s, kind).start()

    def half_on(s):
        half_copy(s, 0).wait_recv()
        z_copy(s).start()
        for t in peers:
            gc_half(s, 0, t).start()

    def weights_start():
        half_start(3)

    for t in peers:
        for kind in range(2):
            gc_copy(0, kind, t).start()

    lax.fori_loop(0, R, project, 0)

    prefix = n.prefix[0]
    longest = L // 2
    SB = min(256, T)
    nsub = T // SB
    lane_sb = lax.broadcasted_iota(jnp.int32, (SB, HD), 1)

    def a_copy(s):
        i = flip(r, s)
        return remote(n.mine.at[i], n.att.at[r], sem["a"], s - 1, row=i)

    def attend_block(step, carry):
        s = lax.rem(step + 1, R)
        i = flip(r, s)
        for static in range(R):
            early = (static + 1) * T <= longest
            nk = longest if early else (static + 1) * T
            nm = nk if early else T

            def attend(t, inner, nk=nk, nm=nm):
                h = t // nsub
                sub = pl.multiple_of(lax.rem(t, nsub) * SB, SB)
                row = i * T + sub
                rows = pl.ds(pl.multiple_of(row, SB), SB)
                scores = mm(n.q[h, rows, :], n.k[h, :nk, :], NT)
                limit = jnp.maximum(row + 1 + lax.broadcasted_iota(jnp.int32, (SB, 1), 0), prefix)
                key = (nk - nm) + lax.broadcasted_iota(jnp.int32, (SB, nm), 1)
                last = jnp.where(key < limit, scores[:, nk - nm :], masked_score)
                top = jnp.max(last, axis=1, keepdims=True)
                if nk > nm:
                    top = jnp.maximum(top, jnp.max(scores[:, : nk - nm], axis=1, keepdims=True))
                mixed = mm(jnp.exp(last - top).astype(bf16), n.v[h, nk - nm : nk, :], NN)
                if nk > nm:
                    mixed += mm(jnp.exp(scores[:, : nk - nm] - top).astype(bf16), n.v[h, : nk - nm, :], NN)
                weight = mixed[:, HD : HD + 1]
                n.mixed[h, pl.ds(sub, SB), :] = mixed / weight
                n.q[h, rows, HD:] = split_parts(-(top + jnp.log(weight)), lane_sb, 3)
                return inner

            @pl.when(i == static)
            def _(attend=attend):
                lax.fori_loop(0, heads * nsub, attend, 0)

        n.mine[i] = jnp.concatenate([n.mixed[h][:, :HD] for h in range(heads)], axis=1).astype(bf16)

        for at in range(R - 1):

            @pl.when(step == at)
            def _(at=at):
                a_copy(at + 1).start()
                if at == 0:
                    for s in others:
                        wo_copy(s).wait_recv()
                        for t in peers:
                            woc_copy(s, t).start()
                    half_start(1)
                if at == 1:
                    half_on(3)

        return carry

    def attend_all(mixed_ref):
        n.mixed = mixed_ref
        lax.fori_loop(0, R, attend_block, 0)

    pl.run_scoped(attend_all, pltpu.VMEM((heads, T, LANES), f32))
    half_start(2)
    n.att[r] = n.mine[r]
    half_on(1)

    TR = min(256, T)
    TF = 384 if F % 384 == 0 else F
    tiles = F // TF
    ticks = R * tiles

    def turn(k):
        return lax.rem(156 // ((1 + 3 * lax.rem(k, 2)) * (1 + 15 * (k // 2))), R)

    def a2_copy(s):
        b = flip(r, s)
        return remote(n.gsend.at[b], n.gatt.at[r], sem["a2"], s - 1, row=b)

    z_first = n.grow.shape[1] == 1
    row_kinds = (0,) if z_first else (0, 1)

    def row_copy(s, kind):
        return remote(n.crecv.at[s, 0, kind], n.grow.at[s - 1, kind], sem["row"], 2 * (s - 1) + kind, row=flip(r, s))

    def b_part(device):
        height = n.bsum.shape[1]
        return pl.ds(pl.multiple_of(device * height, height), height)

    def b_copy(s, g):
        to = lax.rem(z + g, Z)
        return remote(n.crecv.at[s, 0, 1, b_part(to)], n.bz.at[s, g - 1], sem["b"], s * (Z - 1) + g - 1, dp=to)

    def br_copy(s):
        return remote(n.bsum.at[s], n.brow.at[s - 1], sem["br"], s - 1, row=flip(r, s))

    def b_sum(s):
        if not z_first:
            return
        for g in groups:
            b_copy(s, g).wait_recv()
        total = n.crecv[s, 0, 1, b_part(z), :].astype(f32)
        for g in groups:
            total = total + n.bz[s, g - 1].astype(f32)
        n.bsum[s] = total.astype(bf16)
        if s > 0:
            br_copy(s).start()

    def wrow_copy(s):
        b = flip(r, s)
        return remote(n.orecv.at[0, b], n.orow.at[s - 1], sem["wrow"], s - 1, row=b)

    def u_copy(s):
        return remote(n.ubg.at[flip(r, s)], n.urow.at[s - 1], sem["u"], s - 1, row=flip(r, s))

    def middle(wbuf, acc, gn, n2, n2t, cott, gbuf, obuf):
        def fetch(tick):
            fcols = pl.ds(pl.multiple_of(lax.rem(tick, tiles) * TF, TF), TF)
            slot = lax.rem(tick, 2)
            return pltpu.make_async_copy(
                n.wud.at[:, flip(r, turn(tick // tiles)), :, fcols], wbuf.at[slot], local.at[slot]
            )

        def fetch_start(tick):
            own = turn(tick // tiles) == 0

            @pl.when(jnp.logical_not(own))
            def _():
                fetch(tick).start()

            @pl.when(own)
            def _():
                fcols = pl.ds(pl.multiple_of(lax.rem(tick, tiles) * TF, TF), TF)
                slot = lax.rem(tick, 2)
                for kind in range(2):
                    source = (n.w_up, n.w_down)[kind].at[:, fcols]
                    pltpu.make_async_copy(source, wbuf.at[slot, kind, cols], local.at[slot]).start()
                    for p in peers:
                        rows = rows_of(col_at(p))
                        pltpu.make_async_copy(
                            n.wud.at[kind, r, rows, fcols], wbuf.at[slot, kind, rows], local.at[slot]
                        ).start()

        def c_copy(k, t):
            to = col_at(t)
            return remote(
                gbuf.at[lax.rem(k, 2), :, rows_of(to)], n.crecv.at[turn(k), t - 1], sem["c"], k * (C - 1) + t - 1,
                col=to,
            )

        def o_copy(t):
            to = col_at(t)
            return remote(obuf.at[:, to], n.orecv.at[t - 1], sem["o"], t - 1, col=to)

        def join(k):
            s = turn(k)
            for t in peers:
                c_copy(k, t).wait_recv()
            for kind in range(2):
                total = gbuf[lax.rem(k, 2), kind, cols, :].astype(f32)
                for t in peers:
                    total = total + n.crecv[s, t - 1, kind].astype(f32)
                n.crecv[s, 0, kind] = total.astype(bf16)

            if z_first:
                for g in groups:
                    b_copy(s, g).start()

            @pl.when(s > 0)
            def _():
                u_copy(s).start()
                for kind in row_kinds:
                    row_copy(s, kind).start()

        for p in peers:
            for kind in range(2):
                gc_copy(0, kind, p).wait()
        fetch_start(0)
        cott[...] = n.cot[...].T
        for s in others:
            for t in peers:
                woc_copy(s, t).wait_recv()
        for t in peers:
            woc_copy(0, t).wait_recv()
        for s in others:
            ub_copy(s).wait_recv()
            a_copy(s).wait_recv()
        vsum = jnp.zeros((1, D), f32)
        for part in range(T // TR):
            rows = slice(part * TR, (part + 1) * TR)
            branch = []
            for device in range(C):
                piece = mm(n.att[0, rows, :], n.wo[0, device], NN)
                for b in range(1, R):
                    piece += mm(n.att[b, rows, :], n.wo[b, device], NN)
                branch.append(piece)
            branch = jnp.concatenate(branch, axis=1)
            hidden = n.x[rows, :].astype(f32) + n.emb[0:1, :] + branch + vec(2)
            n.tgrad[rows, :] = hidden
            centred, inverse = normalize(hidden, D)
            n2[rows, :] = (centred * vec(3) + vec(4)).astype(bf16)
            acc[rows, :] = jnp.zeros((TR, D), f32)
            gn[rows, :] = jnp.zeros((TR, D), f32)
            vsum = vsum + jnp.sum(n.cot[rows, :].astype(f32), axis=0, keepdims=True)
        n2t[...] = n2[...].T
        n.vbuf[5:6, :] = vsum

        def second_half(s):
            z_copy(s).wait_recv()
            for p in peers:
                gc_half(s, 1, p).start()

        def arrived(s):
            for p in peers:
                for kind in range(2):
                    gc_copy(s, kind, p).wait_recv()

        def tick_step(tick, carry):
            k, t = tick // tiles, lax.rem(tick, tiles)
            b = flip(r, turn(k))
            slot, wslot = lax.rem(k, 2), lax.rem(tick, 2)
            fetch(tick).wait()

            @pl.when((t == 0) & (k >= 2))
            def _():
                for p in peers:
                    c_copy(k - 2, p).wait_send()

            @pl.when(tick == tiles - 1)
            def _():
                half_on(2)
                second_half(3)
                arrived(3)

            @pl.when((t < tiles - 1) | (k == 0))
            def _():
                fetch_start(tick + 1)

            fcols = pl.ds(pl.multiple_of(t * TF, TF), TF)
            wu = wbuf[wslot, 0]
            wd = wbuf[wslot, 1]
            inner = mm(n2[...], wu, NN) + n.ub[b, 0:1, fcols]
            cdf = 0.5 * (1.0 + lax.erf(inner * 0.7071067811865476))
            slope = cdf + inner * (jnp.exp(-0.5 * inner * inner) * 0.3989422804014327)
            active = (inner * cdf).astype(bf16)
            acc[...] += mm(active, wd, NT)
            ginner = mm(n.cot[...], wd, NN) * slope
            glow = ginner.astype(bf16)
            gn[...] += mm(glow, wu, NT)
            gbuf[slot, 1, :, fcols] = mm(cott[...], active, NN).astype(bf16)
            gbuf[slot, 0, :, fcols] = mm(n2t[...], glow, NN).astype(bf16)
            n.ubg[b, :, fcols] = jnp.sum(ginner, axis=0, keepdims=True)

            @pl.when(t == tiles - 1)
            def _():
                for p in peers:
                    c_copy(k, p).start()

                for near, turn_before in ((1, 1), (2, 2)):

                    @pl.when(k == turn_before)
                    def _(near=near):
                        second_half(near)
                        arrived(near)
                        fetch_start(tick + 1)

            @pl.when((t == 0) & (k > 0))
            def _():
                join(k - 1)

            return carry

        lax.fori_loop(0, ticks, tick_step, 0)

        gain_sum = jnp.zeros((1, D), f32)
        bias_sum = jnp.zeros((1, D), f32)
        hid_sum = jnp.zeros((1, D), f32)
        for part in range(T // TR):
            rows = slice(part * TR, (part + 1) * TR)
            hidden = n.tgrad[rows, :]
            n.out[rows, :] = (hidden + acc[rows, :] + vec(5)).astype(bf16)
            centred, inverse = normalize(hidden, D)
            g = gn[rows, :]
            gh = n.cot[rows, :].astype(f32) + norm_back(g, centred, inverse, vec(3), D)
            n.tgrad[rows, :] = gh
            n2[rows, :] = gh.astype(bf16)
            gain_sum = gain_sum + jnp.sum(g * centred, axis=0, keepdims=True)
            bias_sum = bias_sum + jnp.sum(g, axis=0, keepdims=True)
            hid_sum = hid_sum + jnp.sum(gh, axis=0, keepdims=True)
        n.vbuf[2:3, :] = hid_sum
        n.vbuf[3:4, :] = gain_sum
        n.vbuf[4:5, :] = bias_sum

        def back_step(at, carry):
            s = R - 1 - at
            b = flip(r, s)
            grad = n2[...]
            back = mm(lanes(grad, 0), n.wo[b, 0], NT)
            for device in range(1, C):
                back += mm(lanes(grad, device), n.wo[b, device], NT)
            n.gsend[b] = back.astype(bf16)

            @pl.when(s > 0)
            def _():
                a2_copy(s).start()

            return carry

        lax.fori_loop(0, R, back_step, 0)
        n.gatt[r] = n.gsend[r]
        join(R - 1)

        def out_step(b, carry):
            block = mm(n.att[b], n2[...], TN).astype(bf16)
            for device in range(C):
                obuf[b, device] = lanes(block, device)
            return carry

        lax.fori_loop(0, R, out_step, 0)
        for t in peers:
            o_copy(t).start()
        for t in peers:
            o_copy(t).wait_recv()
        for b in range(R):
            total = obuf[b, c].astype(f32)
            for t in peers:
                total = total + n.orecv[t - 1, b].astype(f32)
            n.orecv[0, b] = total.astype(bf16)
        for s in others:
            wrow_copy(s).start()
        for t in peers:
            o_copy(t).wait_send()
            for s in range(R - 2, R):
                c_copy(s, t).wait_send()

    dt = bf16
    pl.run_scoped(
        middle,
        pltpu.VMEM((2, 2, D, TF), dt), pltpu.VMEM((T, D), f32), pltpu.VMEM((T, D), f32), pltpu.VMEM((T, D), dt),
        pltpu.VMEM((D, T), dt), pltpu.VMEM((D, T), dt), pltpu.VMEM((2, 2, D, F), dt), pltpu.VMEM((R, C, H, DC), dt),
    )

    sources = (n.crecv.at[0, 0, 0], n.crecv.at[0, 0, 1], n.oblk, n.qblk)
    landing = (n.zr.at[0], n.zr.at[n.zr.shape[0] - 1], n.zro, n.zrq)
    finals = (n.up_out, n.down_out, n.wo_out, n.qkv_out)

    heights = (DC, DC, H, 3 * H)
    split = [landing[kind].shape[1] != heights[kind] for kind in range(4)]
    def part_of(kind, device):
        height = landing[kind].shape[1]
        return pl.ds(pl.multiple_of(device * height, height), height) if split[kind] else slice(None)

    def zz_copy(kind, s):
        to = lax.rem(z + s, Z)
        return remote(sources[kind].at[part_of(kind, to)], landing[kind].at[s - 1], sem["z"], kind * (Z - 1) + s - 1, dp=to)

    def y_copy(kind, s):
        piece = finals[kind].at[part_of(kind, z)]
        return remote(piece, piece, sem["y"], kind * (Z - 1) + s - 1, dp=lax.rem(z + s, Z))

    def z_start(kind):
        for s in groups:
            zz_copy(kind, s).start()

    def z_end(kind):
        for s in groups:
            zz_copy(kind, s).wait_recv()
        total = sources[kind][part_of(kind, z), :].astype(f32)
        for s in groups:
            total = total + landing[kind][s - 1].astype(f32)
        finals[kind][part_of(kind, z), :] = total.astype(bf16)
        if split[kind]:
            for s in groups:
                y_copy(kind, s).start()

    def down_end():
        if not z_first:
            z_end(1)
            return
        total = n.bsum[0].astype(f32)
        for s in others:
            br_copy(s).wait_recv()
            total = total + n.brow[s - 1].astype(f32)
        finals[1][b_part(z), :] = total.astype(bf16)
        for s in groups:
            y_copy(1, s).start()

    def z_finish(kind):
        for s in groups:
            if kind != 1 or not z_first:
                zz_copy(kind, s).wait_send()
            if split[kind]:
                y_copy(kind, s).wait()

    def row_sum(kind):
        total = n.crecv[0, 0, kind].astype(f32)
        for s in others:
            row_copy(s, kind).wait_recv()
            total = total + n.grow[s - 1, kind].astype(f32)
        n.crecv[0, 0, kind] = total.astype(bf16)
        z_start(kind)

    def wrow_sum():
        for s in others:
            wrow_copy(s).wait_recv()
        total = n.orecv[0, r].astype(f32)
        for s in others:
            total = total + n.orow[s - 1].astype(f32)
        n.oblk[...] = total.astype(bf16)
        z_start(2)

    def p_copy(link, part, b):
        piece = pl.ds(part * half, half)
        return remote(n.part.at[b, piece], n.prec.at[link, piece], sem["p"], 2 * link + part, row=(nx, ny)[link])

    def pr_copy(link, b):
        return remote(n.part.at[b, pl.ds(link * half, half)], n.prel.at[link], sem["pr"], link, row=(nx, ny)[link])

    def back(d, dq, dk, dv, gp, qg):
        def spread(b):
            rows = pl.ds(b * T, T)

            @pl.when(r != b)
            def _():
                s = flip(r, b)
                remote(n.gsend.at[b], n.gatt.at[b], sem["a2"], s - 1, row=b).wait_recv()

            ga = n.gatt[b]
            both = ga.astype(f32) * n.mine[b].astype(f32)
            for h in range(heads):
                piece = slice(h * HD, (h + 1) * HD)
                delta = jnp.sum(both[:, piece], axis=1, keepdims=True)
                d[h, rows, :] = jnp.concatenate([ga[:, piece], split_parts(-delta, lane, 2)], axis=1)

        def pair(h, i, j, masked):
            qs = pl.ds(pl.multiple_of(i * T, T), T)
            ks = pl.ds(pl.multiple_of(j * T, T), T)
            qb, kb, vb, db = n.q[h, qs, :], n.k[h, ks, :], n.v[h, ks, :], d[h, qs, :]
            scores = mm(kb, qb, NT)
            if masked:
                limit = jnp.maximum(i * T + 1 + lax.broadcasted_iota(jnp.int32, (1, T), 1), prefix)
                key = j * T + lax.broadcasted_iota(jnp.int32, (T, T), 0)
                scores = jnp.where(key < limit, scores, masked_score)
            probs = jnp.exp(scores)
            gscores = (probs * mm(vb, db, NT)).astype(bf16)
            dv[h, ks, :] += mm(probs.astype(bf16), db, NN)
            dk[h, ks, :] += mm(gscores, qb, NN)
            dq[h, qs, :] += mm(gscores, kb, TN)

        def finish(b):
            rows = pl.ds(b * T, T)
            stack = jnp.concatenate(
                [dq[h, rows, :][:, :HD] * scale for h in range(heads)]
                + [dk[h, rows, :][:, :HD] for h in range(heads)]
                + [dv[h, rows, :][:, :HD] for h in range(heads)],
                axis=1,
            ).astype(bf16)
            gp[b] = stack
            n.part[b] = jnp.concatenate(
                [mm(stack, n.wq[device], NN).astype(bf16) for device in range(C)], axis=1
            )
            s = flip(r, b)

            @pl.when(s == 3)
            def _():
                pr_copy(0, b).start()
                pr_copy(1, b).start()

            for link in range(2):

                @pl.when(s == link + 1)
                def _(link=link):
                    p_copy(link, link, b).start()

        def combine(b):
            s = flip(r, b)
            for link in range(2):

                @pl.when(s == link + 1)
                def _(link=link):
                    came = 1 - link
                    pr_copy(came, b).wait_recv()
                    piece = pl.ds(came * half, half)
                    total = n.part[b, piece, :].astype(f32) + n.prel[came].astype(f32)
                    n.part[b, piece, :] = total.astype(bf16)
                    p_copy(link, came, b).start()

        dq[...] = jnp.zeros_like(dq)
        dk[...] = jnp.zeros_like(dk)
        dv[...] = jnp.zeros_like(dv)
        early = R // 2
        for i in range(R - 1, early - 1, -1):
            spread(i)

            def plain_pair(t, carry, i=i):
                pair(t // i, i, lax.rem(t, i), False)
                return carry

            def diagonal(h, carry, i=i):
                pair(h, i, i, True)
                return carry

            lax.fori_loop(0, heads * i, plain_pair, 0)
            lax.fori_loop(0, heads, diagonal, 0)
            finish(i)
            if i + 1 < R:
                combine(i + 1)
            else:
                b_sum(0)
                b_sum(3)
                b_sum(1)
        for i in range(early - 1, -1, -1):
            spread(i)
        b_sum(2)
        row_sum(0)

        def square(t, carry):
            rest = lax.rem(t, early * early)
            pair(t // (early * early), rest // early, lax.rem(rest, early), True)
            return carry

        def corner(t, carry):
            rest = lax.rem(t, 3)
            pair(t // 3, 1 - rest // 2, (rest + 1) // 2 - rest // 2 + rest // 2, True)
            return carry

        def origin(h, carry):
            pair(h, 0, 0, True)
            return carry

        if early == 2:
            lax.fori_loop(0, 3 * heads // 2, corner, 0)
        else:
            lax.fori_loop(0, heads * early * early, square, 0)
        if not z_first:
            row_sum(1)
        wrow_sum()
        if early == 2:
            lax.fori_loop(3 * heads // 2, 3 * heads, corner, 0)
            down_end()
            finish(1)
            combine(2)
            lax.fori_loop(0, heads, origin, 0)
            finish(0)
            z_end(0)
        else:
            for b in range(early - 1, -1, -1):
                finish(b)
            combine(early)
            down_end()
            z_end(0)

        qg[...] = jnp.zeros_like(qg)

        def qkv_step(b, carry):
            qg[...] += mm(gp[b], n.one[b], TN)
            return carry

        lax.fori_loop(0, R, qkv_step, 0)
        for device in range(C):
            n.wq[device] = lanes(qg, device).astype(bf16)

        def q_copy(t):
            to = col_at(t)
            return remote(n.wq.at[to], n.qrecv.at[t - 1], sem["q"], t - 1, col=to)

        for t in peers:
            q_copy(t).start()
        for b in range(early - 1, -1, -1):
            combine(b)
        z_end(2)
        for t in peers:
            q_copy(t).wait()
        total = n.wq[c].astype(f32)
        for t in peers:
            total = total + n.qrecv[t - 1].astype(f32)
        n.qblk[...] = total.astype(bf16)
        z_start(3)

    pl.run_scoped(
        back,
        pltpu.VMEM((heads, L, LANES), bf16), pltpu.VMEM((heads, L, LANES), f32), pltpu.VMEM((heads, L, LANES), f32),
        pltpu.VMEM((heads, L, LANES), f32), pltpu.VMEM((R, T, 3 * H), bf16), pltpu.VMEM((3 * H, D), f32),
    )

    for link in range(2):
        for part in range(2):
            p_copy(link, part, 0).wait_recv()
    gain_sum = jnp.zeros((1, D), f32)
    bias_sum = jnp.zeros((1, D), f32)
    all_sum = jnp.zeros((1, D), f32)
    for piece in range(T // TR):
        rows = slice(piece * TR, (piece + 1) * TR)
        g = n.part[r, rows, :].astype(f32) + n.prec[0, rows, :].astype(f32) + n.prec[1, rows, :].astype(f32)
        centred, inverse = normalize(n.x[rows, :].astype(f32) + n.emb[0:1, :], D)
        total = n.tgrad[rows, :] + norm_back(g, centred, inverse, vec(0), D)
        n.tgrad[rows, :] = total
        gain_sum = gain_sum + jnp.sum(g * centred, axis=0, keepdims=True)
        bias_sum = bias_sum + jnp.sum(g, axis=0, keepdims=True)
        all_sum = all_sum + jnp.sum(total, axis=0, keepdims=True)

    n.vbuf[0:1, :] = gain_sum
    n.vbuf[1:2, :] = bias_sum
    n.vbuf[6:7, :] = all_sum
    n.vbuf[7:8, :] = jnp.zeros((1, D), f32)

    def v_copy(s):
        return remote(n.vbuf, n.vrow.at[s - 1], sem["v"], s - 1, row=flip(r, s))

    def all_copy(s, t):
        piece = n.vall.at[z, c]
        return remote(piece, piece, sem["vz"], s * C + t - 1, dp=lax.rem(z + s, Z), col=col_at(t))

    rest = [(s, t) for s in range(Z) for t in range(C) if s + t > 0]
    for s in others:
        v_copy(s).start()
    up_bias = n.ubg[r]
    for s in others:
        u_copy(s).wait_recv()
        up_bias = up_bias + n.urow[s - 1]
    for s in others:
        v_copy(s).wait_recv()
    total = n.vbuf[...]
    for s in others:
        total = total + n.vrow[s - 1]
    n.vall[z, c, 0:8, :] = total
    n.vall[z, c, 7:8, :] = up_bias
    n.vall[z, c, 8:16, :] = jnp.full((8, D), n.stamp[0].astype(f32))
    for s, t in rest:
        all_copy(s, t).start()
    z_end(3)
    for s, t in rest:
        all_copy(s, t).wait_recv()
    total = jnp.zeros((8, D), f32)
    number = (lax.broadcasted_iota(jnp.int32, (NTB, D), 0) + c * NTB).astype(f32)
    table = jnp.zeros((NTB, D), f32)
    for s in range(Z):
        for t in range(C):
            total = total + n.vall[s, t, 0:8, :]
            table = table + jnp.where(number == n.vall[s, t, 8:9, :], n.vall[s, t, 6:7, :], 0.0)
    n.small[...] = total
    n.table_out[...] = table

    for t in peers:
        stamp_copy(t).wait_send()
        pick_copy(t).wait_send()
        w_copy(t).wait_send()
        for s in range(R):
            woc_copy(s, t).wait_send()
            if s > 0:
                gc_copy(s, 0, t).wait_send()
                gc_copy(s, 1, t).wait_send()
    for link in range(2):
        relay_copy(link).wait_send()
        pr_copy(link, 0).wait_send()
        for part in range(2):
            n_copy(link, part).wait_send()
            p_copy(link, part, 0).wait_send()
    for s in others:
        half_copy(s, 0).wait_send()
        for copy in (a_copy, z_copy, wo_copy, ub_copy, a2_copy, wrow_copy, u_copy, v_copy):
            copy(s).wait_send()
        for kind in row_kinds:
            row_copy(s, kind).wait_send()
        if z_first:
            br_copy(s).wait_send()
    if z_first:
        for s in range(R):
            for g in groups:
                b_copy(s, g).wait_send()
    for s, t in rest:
        all_copy(s, t).wait_send()
    for kind in range(4):
        z_finish(kind)


def run_layer(C, Z, stamp, prefix, x, cot, table, vectors, w_qkv, w_out, w_up, w_down):
    T, D = x.shape
    DC, F = w_up.shape
    H = w_out.shape[0]
    heads = H // HD
    L = R * T
    NTB = table.shape[0]
    part = lambda height: height // Z if height % (16 * Z) == 0 else height
    kinds, rows_b = (1, DC // Z) if DC % (16 * Z) == 0 else (2, 16)
    vm = pltpu.VMEM
    given = ("ln1_gain", "ln1_bias", "out_bias", "ln2_gain", "ln2_bias", "down_bias", "up_bias")
    ins = dict(stamp=SM, prefix=SM, x=VM, cot=VM, table=VM, **{name: VM for name in given}, w_qkv=VM, w_out=VM, w_up=AN, w_down=AN)
    outs = dict(
        out=((T, D), bf16), tgrad=((T, D), f32), up_out=((DC, F), bf16), down_out=((DC, F), bf16),
        wo_out=((H, DC), bf16), qkv_out=((3 * H, DC), bf16), small=((8, D), f32), table_out=((NTB, D), f32),
        wud=((2, R, D, F), bf16),
    )
    scratch = dict(
        stamp_own=vm((8, LANES), f32), stamp_got=vm((C - 1, 8, LANES), f32), picked=vm((C - 1, 8, D), f32),
        picked_got=vm((C - 1, 8, D), f32), emb=vm((8, D), f32), vectors=vm((8, D), f32), wq=vm((C, 3 * H, DC), bf16), one=vm((R, T, D), bf16),
        q=vm((heads, L, LANES), bf16), k=vm((heads, L, LANES), bf16), v=vm((heads, L, LANES), bf16),
        mine=vm((R, T, H), bf16), att=vm((R, T, H), bf16), wo=vm((R, C, H, DC), bf16),
        ub=vm((R, 8, F), f32), vbuf=vm((8, D), f32), ubg=vm((R, 1, F), f32),
        crecv=vm((R, C - 1, 2, DC, F), bf16), orecv=vm((C - 1, R, H, DC), bf16), gsend=vm((R, T, H), bf16),
        gatt=vm((R, T, H), bf16), grow=vm((R - 1, kinds, DC, F), bf16), orow=vm((R - 1, H, DC), bf16),
        urow=vm((R - 1, 1, F), f32), bz=vm((R, Z - 1, rows_b, F), bf16), bsum=vm((R, rows_b, F), bf16), brow=vm((R - 1, rows_b, F), bf16), part=vm((R, T, D), bf16), prec=vm((2, T, D), bf16), prel=vm((2, T // 2, D), bf16),
        qrecv=vm((C - 1, 3 * H, DC), bf16), oblk=vm((H, DC), bf16), qblk=vm((3 * H, DC), bf16),
        zr=vm((kinds, Z - 1, part(DC), F), bf16), zro=vm((Z - 1, part(H), DC), bf16), zrq=vm((Z - 1, part(3 * H), DC), bf16),
        vrow=vm((R - 1, 8, D), f32), vall=vm((Z, C, 16, D), f32),
    )
    sems = dict(
        stamp=C - 1, pick=C - 1, w=C - 1, n=4, relay=2, g=R - 1, gz=R - 1, b=R * (Z - 1), br=R - 1, gc=2 * R * (C - 1), wo=R - 1,
        woc=R * (C - 1), ub=R - 1, a=R - 1, a2=R - 1, row=2 * (R - 1), wrow=R - 1, u=R - 1, c=R * (C - 1), o=C - 1,
        z=4 * (Z - 1), y=4 * (Z - 1), p=4, pr=2, q=C - 1, v=R - 1, vz=Z * C - 1,
    )
    names = list(ins) + list(outs) + list(scratch) + ["sem_" + name for name in sems]
    dma = pltpu.SemaphoreType.DMA
    semaphores = []
    for count in sems.values():
        semaphores += [dma((count,)), dma((count,))]
    results = pl.pallas_call(
        functools.partial(layer_kernel, names, C, Z),
        out_shape=tuple(jax.ShapeDtypeStruct(*spec) for spec in outs.values()),
        in_specs=list(ins.values()),
        out_specs=(VM,) * (len(outs) - 1) + (AN,),
        scratch_shapes=list(scratch.values()) + semaphores + [dma((2,))],
        compiler_params=pltpu.CompilerParams(collective_id=0, has_side_effects=True, vmem_limit_bytes=67043328),
        name="layer",
    )(stamp, prefix, x, cot, table, *vectors, w_qkv, w_out, w_up, w_down)
    return dict(zip(outs, results))


def tail_kernel(out, tgrad, table, small, up, down, wo, qkv, *refs):
    refs[0][...] = out[...]
    refs[1][...] = tgrad[...]
    for source, target in zip((up, down, wo, qkv), refs[3:7]):
        target[...] = source[...].astype(f32)

    @pl.when(pl.program_id(0) == 0)
    def _():
        refs[2][...] = table[...]
        for row in range(8):
            if row != 6:
                target = refs[7 + (row if row < 6 else 6)]
                target[...] = small[row : row + 1, :].reshape(target.shape[0])


def run_tail(o):
    steps = 4
    arrays = [o[name] for name in ("out", "tgrad", "table_out", "small", "up_out", "down_out", "wo_out", "qkv_out")]

    def rows(array):
        return pl.BlockSpec((array.shape[0] // steps, array.shape[1]), lambda i: (i, 0))

    def whole(array):
        return pl.BlockSpec(array.shape, lambda i: (0, 0))

    ins = [whole(array) if i in (2, 3) else rows(array) for i, array in enumerate(arrays)]
    width = arrays[3].shape[1]
    line = pl.BlockSpec((width,), lambda i: (0,))
    chosen = (0, 1, 2, 4, 5, 6, 7)
    kinds = [arrays[i].dtype if i < 4 else f32 for i in chosen]
    return pl.pallas_call(
        tail_kernel,
        grid=(steps,),
        out_shape=[jax.ShapeDtypeStruct(arrays[i].shape, kind) for i, kind in zip(chosen, kinds)]
        + [jax.ShapeDtypeStruct((width,), f32)] * 7,
        in_specs=ins,
        out_specs=[ins[i] for i in chosen] + [line] * 7,
        name="results",
    )(*arrays)


def body(C, Z, *args):
    (tokens, cotangent, timesteps, prefix_len, time_table, ln1_gain, ln1_bias, w_qkv, w_out, out_bias,
     ln2_gain, ln2_bias, w_up, up_bias, w_down, down_bias) = args
    DC, _, H = w_qkv.shape
    vectors = (ln1_gain, ln1_bias, out_bias, ln2_gain, ln2_bias, down_bias, up_bias)
    o = run_layer(
        C, Z, timesteps, prefix_len, tokens[0], cotangent[0], time_table, vectors,
        w_qkv.transpose(1, 2, 0).reshape(3 * H, DC), w_out.T, w_up, w_down,
    )
    out, tgrad, table, up, down, wo, qkv, gain1, bias1, bias_out, gain2, bias2, bias_down, bias_up = run_tail(o)
    return (
        out[None], tgrad[None], table, gain1, bias1, qkv.reshape(3, H, DC).transpose(2, 0, 1), wo.T, bias_out, gain2,
        bias2, up, bias_up, down, bias_down,
    )


def solution(mesh):
    C, Z = mesh.shape["col"], mesh.shape["dp"]
    batch = P(("dp", "col"), "row", None)
    block = P("col", "row")
    return jax.shard_map(
        functools.partial(body, C, Z),
        mesh=mesh,
        in_specs=(
            batch, batch, P(("dp", "col")), P(("dp", "col")), P("col", None), P(), P(), P("col", None, "row"), block,
            P(), P(), P(), block, P("row"), block, P(),
        ),
        out_specs=(
            batch, batch, P("col", None), P(), P(), P("col", None, "row"), block, P(), P(), P(), block, P("row"),
            block, P(),
        ),
        check_vma=False,
    )
```
